256 devices in a mesh: tm: 8 (over z_hi, y), aux: 32 (over z_lo, x, core).
Axes of the slice: x: 4, y: 4, z: 8 (z_hi: 2, z_lo: 4; z = z_hi * 4 + z_lo), core: 2. Of those that a mesh axis runs over, the one named last changes fastest.
Arguments:
- green: bfloat16 [16, 1024, 1024], P('tm'), may hold values from -4 to 4
- factors: bfloat16 [4096, 1024], P('aux'), may hold values from -0.1875 to 0.1875
- pattern: int32 [32, 8], P('aux'), may hold values 0 or 1
- coulomb: float32 [4096], P('aux'), may hold values from 0.5 to 2
Outputs:
- sigma: float32 [1024, 16, 1024], P('aux', 'tm')
The draws below stay inside these ranges and needn't reach their ends.
All inputs are finite; a program needn't handle non-finite values. No bound on the sum of `pattern` on one device may be relied on, other than what follows from the above.
Results may differ from the reference program's by a relative error of at most 0.006.
Values may be sent and summed in bfloat16 or wider, within the bound.
No kernel may reach another device: no remote copies, remote signals or barrier semaphores. Data moves between devices by JAX's collectives and lax.ppermute only.
A program may use at most 64 MiB of HBM per device.

```python
import math
import jax
import jax.numpy as jnp
from jax import lax

ORB = 1024
AUX = 4096
BLOCK = 128
TIMES = 16


def plant(result, own_key, smallest, top_value):
    dims = result.shape
    index_at = [jax.random.randint(jax.random.fold_in(own_key, axis), (), 0, dims[axis]) for axis in range(len(dims))]
    result = result.at[tuple(index_at)].set(smallest)
    longest = dims.index(max(dims))
    index_at[longest] = (index_at[longest] + 1) % dims[longest]
    return result.at[tuple(index_at)].set(top_value)


def block_levels(key, shape, shards, smallest, top_value):
    loudness, own = 1.0, jax.random.fold_in(key, 6)
    for axis_at, blocks in shards:
        heights = jnp.exp(jax.random.uniform(jax.random.fold_in(own, axis_at), (blocks,), jnp.float32, smallest / len(shards), top_value / len(shards)))
        loudness = loudness * jnp.repeat(heights, shape[axis_at] // blocks).reshape([-1 if axis == axis_at else 1 for axis in range(len(shape))])
    return loudness


def normal_values(rng, dims, spread, reach, pieces=(), kind=jnp.bfloat16):
    entries = jax.random.normal(rng, dims, jnp.float32) * spread
    if len(pieces) > 0:
        entries = block_levels(rng, dims, pieces, -0.22, 0.18) * entries
    return jnp.clip(entries, min=-reach, max=reach).astype(kind)


def setup_inputs(seed: int = 0) -> dict:
    splits = jax.random.split(jax.random.key(seed), 5)
    return {
        "green": normal_values(splits[0], (TIMES, ORB, ORB), 0.45, 4.0, ((0, 8),)),
        "factors": normal_values(splits[1], (AUX, ORB), ORB ** -0.5, 0.1875, ((0, 32),)),
        "pattern": plant((jax.random.randint(splits[2], (AUX // BLOCK, ORB // BLOCK), 0, 4) < 3).astype(jnp.int32), jax.random.fold_in(splits[2], 1), 0, 1),
        "coulomb": jnp.clip(jnp.exp(math.log(2.0) - 1.3862944 * jax.random.uniform(splits[3], (AUX,), jnp.float32) ** block_levels(splits[3], (AUX,), ((0, 32),), -0.2, 0.2)), 0.5, 2.0),
    }


def reference(green, factors, pattern, coulomb):
    mask = jnp.repeat(jnp.repeat(pattern, BLOCK, axis=0), BLOCK, axis=1)
    masked = factors * mask.astype(factors.dtype)

    def project(gmat):
        left = jnp.dot(masked, gmat, preferred_element_type=jnp.float32).astype(jnp.bfloat16)
        right = jnp.dot(masked, gmat.T, preferred_element_type=jnp.float32).astype(jnp.bfloat16)
        return left, right

    lefts, rights = lax.map(project, green)
    mirrored = jnp.roll(rights, TIMES // 2, axis=0)

    def self_energy(pair):
        left, right = pair
        aux_green = jnp.dot(left, masked.T, preferred_element_type=jnp.float32)
        mirror = jnp.dot(right, masked.T, preferred_element_type=jnp.float32)
        chi = -aux_green * mirror
        kernel = (aux_green * coulomb[:, None] * chi * coulomb[None, :]).astype(jnp.bfloat16)
        carried = jnp.dot(kernel, masked, preferred_element_type=jnp.float32).astype(jnp.bfloat16)
        return -jnp.dot(masked.T, carried, preferred_element_type=jnp.float32)

    sigma = lax.map(self_energy, (lefts, mirrored))
    return jnp.transpose(sigma, (1, 0, 2))
```

```python
import jax
import jax.numpy as jnp
from jax import lax
from jax.sharding import PartitionSpec as P

BLOCK = 128


def local(green, factors, pattern, coulomb):
    f32, bf16 = jnp.float32, jnp.bfloat16
    devices = lax.axis_size("aux")
    own = factors.shape[0]
    mask = jnp.repeat(jnp.repeat(pattern, BLOCK, axis=0), BLOCK, axis=1)
    masked = factors * mask.astype(factors.dtype)
    rows = lax.all_gather(masked, "aux", axis=0, tiled=True)
    left = jnp.einsum("qo,tok->tqk", masked, green, preferred_element_type=f32).astype(bf16)
    half = lax.axis_size("tm") // 2
    left = lax.ppermute(left, "tm", [(i, (i + half) % (2 * half)) for i in range(2 * half)])
    right = jnp.einsum("qo,tko->tqk", masked, green, preferred_element_type=f32).astype(bf16)
    weights = lax.all_gather(coulomb, "aux", axis=0, tiled=True)
    aux_green = jnp.einsum("tqo,po->tqp", right, rows, preferred_element_type=f32)
    mirror = jnp.einsum("tqo,po->tqp", left, rows, preferred_element_type=f32)
    kernel = aux_green * weights[None, None, :] * (aux_green * mirror) * coulomb[None, :, None]
    kernel = kernel.astype(bf16)
    part = jnp.einsum("tqp,pi->tqi", kernel, rows, preferred_element_type=f32).astype(bf16)
    times, orb = green.shape[0], green.shape[1]
    part = part.reshape(times, own, devices, orb // devices).transpose(2, 0, 1, 3)
    part = lax.all_to_all(part, "aux", split_axis=0, concat_axis=0, tiled=True)
    rows = rows.reshape(devices, own, orb)
    return jnp.einsum("dtqi,dqj->itj", part, rows, preferred_element_type=f32)


def solution(mesh):
    in_specs = (P("tm", None, None), P("aux", None), P("aux", None), P("aux"))
    out_specs = P("aux", "tm", None)
    return jax.shard_map(local, mesh=mesh, in_specs=in_specs, out_specs=out_specs, check_vma=False)
```

```python
import functools

import jax
import jax.numpy as jnp
from jax import lax
from jax.experimental import pallas as pl
from jax.experimental.pallas import tpu as pltpu
from jax.sharding import PartitionSpec as P

BLOCK = 128
ORB = 1024
F32, BF16 = jnp.float32, jnp.bfloat16
BOTH = ("tm", "aux")
NT = (((1,), (1,)), ((), ()))
NN = (((1,), (0,)), ((), ()))


def device_at(x, y, z, core):
    return (z // 4 * 4 + y % 4) * 32 + (z % 4 * 4 + x % 4) * 2 + core


def hop(value, dx=0, dz=0, flip=0):
    pairs = []
    for x in range(4):
        for y in range(4):
            for z in range(8):
                for core in range(2):
                    to = device_at((x + dx) % 4, y, (z + dz) % 8, core ^ flip)
                    pairs.append((device_at(x, y, z, core), to))
    return lax.ppermute(value, BOTH, sorted(pairs))


def params(mib):
    return pltpu.CompilerParams(vmem_limit_bytes=mib << 20)


def weights_of(ref, row, block):
    parts = [ref[pl.ds(row + block, 1), pl.ds(k * BLOCK, BLOCK)].astype(F32) for k in range(3)]
    return parts[0] + (parts[1] + parts[2])


def chunk_kernel(spans, first, *refs):
    count = len({span[0] for span in spans})
    right_own, right_other, left_own, left_other = refs[:4]
    rows = refs[4 : 4 + count]
    rest = refs[4 + count :]
    if not first:
        acc_own, acc_other = rest[:2]
        rest = rest[2:]
    out_own, out_other = rest
    for t in range(out_own.shape[0]):
        right = jnp.concatenate([right_own[t], right_other[t]], axis=0)
        left = jnp.concatenate([left_own[t], left_other[t]], axis=0)
        total = None
        for at, start, size, weight_at, weight_row, block in spans:
            part = rows[at][pl.ds(start, size), :]
            weight = jnp.concatenate(
                [weights_of(rows[weight_at], weight_row, block + k) for k in range(size // BLOCK)],
                axis=1,
            )
            a = lax.dot_general(right, part, NT, preferred_element_type=F32)
            m = lax.dot_general(left, part, NT, preferred_element_type=F32)
            k = (a * weight * (a * m)).astype(BF16)
            d = lax.dot_general(k, part, NN, preferred_element_type=F32)
            total = d if total is None else total + d
        own = out_own.shape[1]
        if first:
            out_own[t] = total[:own]
            out_other[t] = total[own:]
        else:
            out_own[t] = acc_own[t] + total[:own]
            out_other[t] = acc_other[t] + total[own:]


def chunk(sides, rows, spans, acc=None):
    times, own, orb = sides[0].shape
    shape = jax.ShapeDtypeStruct((times, own, orb), F32)
    n = sum(span[2] for span in spans)
    extra = () if acc is None else tuple(acc)
    aliases = {} if acc is None else {4 + len(rows): 0, 5 + len(rows): 1}
    return pl.pallas_call(
        functools.partial(chunk_kernel, tuple(spans), acc is None),
        out_shape=(shape, shape),
        input_output_aliases=aliases,
        compiler_params=params(40),
        cost_estimate=pl.CostEstimate(
            flops=times * 3 * 2 * (2 * own) * n * orb, bytes_accessed=2 << 20, transcendentals=0
        ),
    )(*sides, *rows, *extra)


def finish_kernel(own_ref, got_ref, coulomb_ref, out_ref):
    chips, times, rows, _ = out_ref.shape
    for t in range(times):
        d = jnp.transpose(own_ref[t] + got_ref[t]) * coulomb_ref[...]
        d = d.astype(BF16)
        for chip in range(chips):
            out_ref[chip, t] = d[chip * rows : (chip + 1) * rows]


def sigma_kernel(spans, where_ref, part_ref, *refs):
    rows = refs[:-4]
    keep_ref, send_ref, lhs, total_ref = refs[-4:]
    chips, times, i_rows, width = part_ref.shape
    for b in range(chips):
        for t in range(times):
            lhs[pl.ds(t * i_rows, i_rows), pl.ds(b * width, width)] = part_ref[where_ref[b], t]
    total = None
    offset = 0
    for at, start, size in spans:
        d = lax.dot_general(
            lhs[:, pl.ds(offset, size)],
            rows[at][pl.ds(start, size), :],
            NN,
            preferred_element_type=F32,
        )
        total = d if total is None else total + d
        offset += size
    total_ref[...] = total
    half = i_rows // 2
    core = where_ref[chips]
    for t in range(times):
        keep = pl.multiple_of(t * i_rows + core * half, half)
        send = pl.multiple_of(t * i_rows + (1 - core) * half, half)
        keep_ref[t] = total_ref[pl.ds(keep, half), :]
        send_ref[t] = total_ref[pl.ds(send, half), :]


def add_kernel(keep_ref, got_ref, out_ref):
    for t in range(keep_ref.shape[0]):
        out_ref[:, t, :] = keep_ref[t] + got_ref[t]


def local(green, factors, pattern, coulomb):
    times, orb, _ = green.shape
    own = factors.shape[0]
    barrier = lax.optimization_barrier
    mask = jnp.repeat(jnp.repeat(pattern, BLOCK, axis=0), BLOCK, axis=1)
    masked = factors * mask.astype(factors.dtype)
    high = lax.reduce_precision(coulomb, 8, 7)
    middle = lax.reduce_precision(coulomb - high, 8, 7)
    low = coulomb - high - middle
    packed = jnp.concatenate([high, middle, low]).astype(BF16)
    packed = jnp.pad(packed[None, :], ((0, 7), (0, orb - 3 * own)))
    payload = jnp.concatenate([masked, packed], axis=0)

    half = own // 2
    below = hop(payload, dz=1)
    above = hop(payload, dz=-1)
    far_a = hop(payload[:half], dz=2)
    far_b = hop(payload[half:], dz=-2)

    left = jnp.einsum("qo,tok->tqk", masked, green, preferred_element_type=F32).astype(BF16)
    right = jnp.einsum("qo,tko->tqk", masked, green, preferred_element_type=F32).astype(BF16)
    right_other = hop(right, flip=1)

    weights = [payload[own : own + 1], below[own : own + 1], above[own : own + 1], far_b[half : half + 1]]
    weights = jnp.concatenate(weights + [jnp.zeros((4, orb), BF16)], axis=0)
    here = jnp.concatenate([masked, below[:own], above[:own], far_a, far_b[:half], weights], axis=0)
    here, left = barrier((here, left))

    west = hop(here, dx=1)
    east = hop(here, dx=-1)
    left = hop(left, dz=4)
    left_other = hop(left, flip=1)

    sides = (right, right_other, left, left_other)
    n = 4 * own
    full = [(0, 2 * own, 0, n, 0), (2 * own, 2 * own, 0, n, 2)]

    def whole(at):
        return [(at, 0, 2 * own, at, n, 0), (at, 2 * own, 2 * own, at, n, 2)]

    acc = chunk(sides, (here,), whole(0))
    west, east = barrier((west, east))
    over_a = hop(west[: 2 * own], dx=1)
    over_b = hop(east[2 * own :], dx=-1)
    acc = chunk(sides, (west, east), whole(0) + whole(1), acc)
    spans = [(0, 0, 2 * own, 1, 2 * own, 0), (1, 0, 2 * own, 1, 2 * own, 2)]
    keep, send = chunk(sides, (over_a, over_b), spans, acc)

    got = hop(send, flip=1)
    chips, i_rows = 16, orb // 16
    part = pl.pallas_call(
        finish_kernel,
        out_shape=jax.ShapeDtypeStruct((chips, times, i_rows, own), BF16),
        compiler_params=params(24),
    )(keep, got, coulomb[None, :])
    groups = [[2 * chip + core for chip in range(chips)] for core in range(2)]
    part = lax.all_to_all(part, "aux", 0, 0, axis_index_groups=groups, tiled=True)

    me = lax.axis_index("aux")
    core, x, z = me % 2, me // 2 % 4, me // 8
    where = [(z + dz) % 4 * 4 + (x + dx) % 4 for dx in (0, -1, 1, 2) for dz in (0, -1, 1, 2)]
    where = jnp.stack(where + [core]).astype(jnp.int32)
    spans = [(0, 0, n), (1, 0, n), (2, 0, n), (3, 0, n // 2), (4, 0, n // 2)]
    shape = jax.ShapeDtypeStruct((times, i_rows // 2, orb), F32)
    vmem = pl.BlockSpec(memory_space=pltpu.VMEM)
    keep, send = pl.pallas_call(
        functools.partial(sigma_kernel, tuple(spans)),
        out_shape=(shape, shape),
        in_specs=[pl.BlockSpec(memory_space=pltpu.SMEM)] + [vmem] * 6,
        out_specs=(vmem, vmem),
        scratch_shapes=[
            pltpu.VMEM((times * i_rows, chips * own), BF16),
            pltpu.VMEM((times * i_rows, orb), F32),
        ],
        compiler_params=params(32),
    )(where, part, here, west, east, over_a, over_b)
    got = hop(send, flip=1)
    return pl.pallas_call(
        add_kernel,
        out_shape=jax.ShapeDtypeStruct((i_rows // 2, times, orb), F32),
        compiler_params=params(16),
    )(keep, got)


def solution(mesh):
    in_specs = (P("tm", None, None), P("aux", None), P("aux", None), P("aux"))
    out_specs = P("aux", "tm", None)
    return jax.shard_map(local, mesh=mesh, in_specs=in_specs, out_specs=out_specs, check_vma=False)
```

```python
import functools

import jax
import jax.numpy as jnp
from jax import lax
from jax.experimental import pallas as pl
from jax.experimental.pallas import tpu as pltpu
from jax.sharding import PartitionSpec as P

BLOCK = 128
HALF = 64
F32, BF16 = jnp.float32, jnp.bfloat16
BOTH = ("tm", "aux")
NT = (((1,), (1,)), ((), ()))
NN = (((1,), (0,)), ((), ()))
VMEM = pl.BlockSpec(memory_space=pltpu.VMEM)


def device_at(x, y, z, core):
    return (z // 4 * 4 + y) * 32 + (z % 4 * 4 + x) * 2 + core


def hop(value, dx=0, dy=0, dz=0, flip=0):
    pairs = []
    for x in range(4):
        for y in range(4):
            for z in range(8):
                for core in range(2):
                    to = device_at((x + dx) % 4, (y + dy) % 4, (z + dz) % 8, core ^ flip)
                    pairs.append((device_at(x, y, z, core), to))
    return lax.ppermute(value, BOTH, sorted(pairs))


def params(mib):
    return pltpu.CompilerParams(vmem_limit_bytes=mib << 20)


def prologue_kernel(factors, pattern, coulomb, masked_ref, whole_ref, first_ref, second_ref, own_ref):
    parity = lax.axis_index("tm") & 1
    orb = factors.shape[1]
    for block in range(orb // BLOCK):
        lanes = pl.ds(block * BLOCK, BLOCK)
        keep = pattern[:, block : block + 1].astype(F32)
        for half in range(2):
            at = parity if half == 0 else 1 - parity
            part = factors[pl.ds(pl.multiple_of(at * HALF, HALF), HALF), lanes]
            part = (part.astype(F32) * keep).astype(BF16)
            masked_ref[pl.ds(half * HALF, HALF), lanes] = part
            if half == 0:
                whole_ref[pl.ds(0, HALF), lanes] = part
                first_ref[:, lanes] = part[: HALF // 2]
                second_ref[pl.ds(0, HALF // 2), lanes] = part[HALF // 2 :]
    c = coulomb[...]
    turned = pltpu.roll(c, HALF, 1)
    own = jnp.where(parity == 0, c, turned)
    own_ref[...] = own
    lane = lax.broadcasted_iota(jnp.int32, own.shape, 1)
    twice = jnp.where(lane < HALF, own, pltpu.roll(own, HALF, 1))
    high = twice.astype(BF16)
    rest = twice - high.astype(F32)
    middle = rest.astype(BF16)
    low = (rest - middle.astype(F32)).astype(BF16)
    zero = jnp.zeros((1, orb - 3 * BLOCK), BF16)
    row = jnp.concatenate([high, middle, low, zero], axis=1)
    rows = jnp.broadcast_to(row.astype(F32), (8, orb)).astype(BF16)
    whole_ref[pl.ds(HALF, 8), :] = rows
    second_ref[pl.ds(HALF // 2, 8), :] = rows


def prologue(factors, pattern, coulomb):
    own, orb = factors.shape
    shapes = [(own, orb), (HALF + 8, orb), (HALF // 2, orb), (HALF // 2 + 8, orb)]
    return pl.pallas_call(
        prologue_kernel,
        out_shape=[jax.ShapeDtypeStruct(s, BF16) for s in shapes]
        + [jax.ShapeDtypeStruct((1, own), F32)],
        in_specs=[VMEM] * 3,
        out_specs=[VMEM] * 5,
        compiler_params=params(8),
    )(factors, pattern, coulomb[None, :])


def weight_of(ref, row):
    parts = [ref[pl.ds(row, 1), pl.ds(k * BLOCK, BLOCK)].astype(F32) for k in range(3)]
    return parts[0] + (parts[1] + parts[2])


def weights_of(ref, row, blocks):
    lane = lax.broadcasted_iota(jnp.int32, (1, BLOCK), 1)
    pairs = []
    for k in range(0, blocks, 2):
        pairs.append(jnp.where(lane < HALF, weight_of(ref, row + k), weight_of(ref, row + k + 1)))
    return jnp.concatenate(pairs, axis=1) if len(pairs) > 1 else pairs[0]


def chunk_kernel(pieces, count, first, *refs):
    right_own, right_other, left_own, left_other = refs[:4]
    rows = refs[4 : 4 + count]
    rest = refs[4 + count :]
    if not first:
        acc_own, acc_other = rest[:2]
        rest = rest[2:]
    out_own, out_other = rest
    own = out_own.shape[1]
    for t in range(out_own.shape[0]):
        right = jnp.concatenate([right_own[t], right_other[t]], axis=0)
        left = jnp.concatenate([left_own[t], left_other[t]], axis=0)
        total = None
        for piece in pieces:
            part = jnp.concatenate([rows[at][pl.ds(0, n), :] for at, n in piece[0]], axis=0)
            weight = weights_of(rows[piece[1]], piece[2], part.shape[0] // HALF)
            a = lax.dot_general(right, part, NT, preferred_element_type=F32)
            m = lax.dot_general(left, part, NT, preferred_element_type=F32)
            k = (a * weight * (a * m)).astype(BF16)
            d = lax.dot_general(k, part, NN, preferred_element_type=F32)
            total = d if total is None else total + d
        if first:
            out_own[t] = total[:own]
            out_other[t] = total[own:]
        else:
            out_own[t] = acc_own[t] + total[:own]
            out_other[t] = acc_other[t] + total[own:]


def chunk(sides, rows, pieces, acc=None):
    times, own, orb = sides[0].shape
    shape = jax.ShapeDtypeStruct((times, own, orb), F32)
    extra = () if acc is None else tuple(acc)
    aliases = {} if acc is None else {4 + len(rows): 0, 5 + len(rows): 1}
    flops = len(pieces) * 4 * HALF * times * 3 * 2 * (2 * own) * orb
    return pl.pallas_call(
        functools.partial(chunk_kernel, tuple(pieces), len(rows), acc is None),
        out_shape=(shape, shape),
        in_specs=[VMEM] * (4 + len(rows) + len(extra)),
        out_specs=(VMEM, VMEM),
        input_output_aliases=aliases,
        compiler_params=params(16),
        cost_estimate=pl.CostEstimate(flops=flops, bytes_accessed=2 << 20, transcendentals=0),
    )(*sides, *rows, *extra)


def finish_kernel(own_ref, got_ref, coulomb_ref, out_ref):
    chips, times, rows, _ = out_ref.shape
    for t in range(times):
        d = jnp.transpose(own_ref[t] + got_ref[t]) * coulomb_ref[...]
        d = d.astype(BF16)
        for chip in range(chips):
            out_ref[chip, t] = d[chip * rows : (chip + 1) * rows]


def sigma_kernel(part_ref, *refs):
    here, west, east = refs[0:2], refs[2:4], refs[4:6]
    far = (refs[6:8], refs[8:10])
    keep_ref, send_ref, lhs, total_ref = refs[10:]
    chips, times, i_rows, width = part_ref.shape
    me = lax.axis_index("aux")
    core, x, z = me & 1, (me >> 1) & 3, me >> 3
    total = None
    for column, dx in enumerate((0, 3, 1, 2)):
        parts = []
        for k, dz in enumerate((0, 3, 1, 2)):
            source = ((z + dz) & 3) * 4 + ((x + dx) & 3)
            for t in range(times):
                at = pl.ds((column * 4 + k) * width, width)
                lhs[pl.ds(t * i_rows, i_rows), at] = part_ref[source, t]
            for parity in range(2):
                if column < 3:
                    ref, row = (here, west, east)[column][parity], k * HALF
                else:
                    ref, row = far[parity][k // 2], k % 2 * HALF
                parts.append(ref[pl.ds(row, HALF), :])
        d = lax.dot_general(
            lhs[:, pl.ds(column * 4 * width, 4 * width)],
            jnp.concatenate(parts, axis=0),
            NN,
            preferred_element_type=F32,
        )
        total = d if total is None else total + d
    total_ref[...] = total
    half = i_rows // 2
    for t in range(times):
        keep = pl.multiple_of(t * i_rows + core * half, half)
        send = pl.multiple_of(t * i_rows + (1 - core) * half, half)
        keep_ref[t] = total_ref[pl.ds(keep, half), :]
        send_ref[t] = total_ref[pl.ds(send, half), :]


def add_kernel(keep_ref, got_ref, out_ref):
    for t in range(keep_ref.shape[0]):
        out_ref[:, t, :] = keep_ref[t] + got_ref[t]


def local(green, factors, pattern, coulomb):
    times, orb, _ = green.shape
    own = factors.shape[0]
    barrier = lax.optimization_barrier
    masked, whole, first, second, coulomb = prologue(factors, pattern, coulomb)

    below = hop(whole, dz=1)
    above = hop(whole, dz=-1)
    far_a = hop(first, dz=2)
    far_b = hop(second, dz=-2)
    left = jnp.einsum("qo,tok->tqk", masked, green, preferred_element_type=F32).astype(BF16)
    right = jnp.einsum("qo,tko->tqk", masked, green, preferred_element_type=F32).astype(BF16)
    right_other = hop(right, flip=1)

    quarter = HALF // 2
    weights = [whole[HALF : HALF + 1], below[HALF : HALF + 1], above[HALF : HALF + 1]]
    weights += [far_b[quarter : quarter + 1], jnp.zeros((4, orb), BF16)]
    here = [masked[:HALF], below[:HALF], above[:HALF], far_a, far_b[:quarter]] + weights
    here, left = barrier((jnp.concatenate(here, axis=0), left))

    n = 4 * HALF
    west = hop(here, dx=1)
    east = hop(here, dx=-1)
    left = hop(left, dz=4)
    cut = HALF + 3 * quarter
    rest_a = hop(here[HALF:cut], dy=-1)
    rest_b = hop(here[cut:], dy=1)
    left_other = hop(left, flip=1)
    here_q = jnp.concatenate([masked[HALF:], rest_a, rest_b], axis=0)

    west, east = barrier((west, east))
    over_a = hop(west[: n // 2], dx=1)
    over_b = hop(east[n // 2 :], dx=-1)
    west_q = hop(west, dy=-1)
    east_q = hop(east, dy=1)
    over_a, over_b = barrier((over_a, over_b))
    over_aq = hop(over_a, dy=-1)
    over_bq = hop(over_b, dy=1)

    sides = (right, right_other, left, left_other)
    acc = chunk(sides, (here, here_q), [(((0, n),), 0, n), (((1, n),), 1, n)])
    acc = chunk(sides, (west, east), [(((0, n),), 0, n), (((1, n),), 1, n)], acc)
    acc = chunk(sides, (west_q, east_q), [(((0, n),), 0, n), (((1, n),), 1, n)], acc)
    pieces = [(((0, n // 2), (1, n // 2)), 1, n // 2), (((2, n // 2), (3, n // 2)), 3, n // 2)]
    keep, send = chunk(sides, (over_a, over_b, over_aq, over_bq), pieces, acc)

    got = hop(send, flip=1)
    chips, i_rows = 16, orb // 16
    part = pl.pallas_call(
        finish_kernel,
        out_shape=jax.ShapeDtypeStruct((chips, times, i_rows, own), BF16),
        in_specs=[VMEM] * 3,
        out_specs=VMEM,
        compiler_params=params(12),
    )(keep, got, coulomb)
    groups = [[2 * chip + core for chip in range(chips)] for core in range(2)]
    part = lax.all_to_all(part, "aux", 0, 0, axis_index_groups=groups, tiled=True)

    shape = jax.ShapeDtypeStruct((times, i_rows // 2, orb), F32)
    keep, send = pl.pallas_call(
        sigma_kernel,
        out_shape=(shape, shape),
        in_specs=[VMEM] * 11,
        out_specs=(VMEM, VMEM),
        scratch_shapes=[
            pltpu.VMEM((times * i_rows, chips * own), BF16),
            pltpu.VMEM((times * i_rows, orb), F32),
        ],
        compiler_params=params(12),
    )(part, here, here_q, west, west_q, east, east_q, over_a, over_b, over_aq, over_bq)
    got = hop(send, flip=1)
    return pl.pallas_call(
        add_kernel,
        out_shape=jax.ShapeDtypeStruct((i_rows // 2, times, orb), F32),
        in_specs=[VMEM] * 2,
        out_specs=VMEM,
        compiler_params=params(8),
    )(keep, got)


def solution(mesh):
    in_specs = (P("tm", None, None), P("aux", None), P("aux", None), P("aux"))
    out_specs = P("aux", "tm", None)
    return jax.shard_map(local, mesh=mesh, in_specs=in_specs, out_specs=out_specs, check_vma=False)
```

```python
import functools

import jax
import jax.numpy as jnp
from jax import lax
from jax.experimental import pallas as pl
from jax.experimental.pallas import tpu as pltpu
from jax.sharding import PartitionSpec as P

BLOCK = 128
HALF = 64
F32, BF16 = jnp.float32, jnp.bfloat16
BOTH = ("tm", "aux")
NT = (((1,), (1,)), ((), ()))
NN = (((1,), (0,)), ((), ()))
VMEM = pl.BlockSpec(memory_space=pltpu.VMEM)


def device_at(x, y, z, core):
    return (z // 4 * 4 + y) * 32 + (z % 4 * 4 + x) * 2 + core


def send(value, to):
    pairs = []
    for x in range(4):
        for y in range(4):
            for z in range(8):
                for core in range(2):
                    tx, ty, tz, tcore = to(x, y, z, core)
                    pairs.append((device_at(x, y, z, core), device_at(tx % 4, ty % 4, tz % 8, tcore)))
    return lax.ppermute(value, BOTH, sorted(pairs))


def along_x(value, step):
    return send(value, lambda x, y, z, core: (x + step, y, z, core))


def along_z(value, step):
    return send(value, lambda x, y, z, core: (x, y, z + step, core))


def other_core(value):
    return send(value, lambda x, y, z, core: (x, y, z, 1 - core))


def two_along_z(value):
    return send(value, lambda x, y, z, core: (x, y, z + (2 if core == 0 else -2), core))


def split_x(value):
    return send(value, lambda x, y, z, core: (x + (1 if core == 0 else -1), y, z, core))


def other_parity(value):
    return send(value, lambda x, y, z, core: (x, y + (1 if y % 2 == core else -1), z, core))


def params(mib):
    return pltpu.CompilerParams(vmem_limit_bytes=mib << 20)


def prologue_kernel(factors_in, pattern_in, coulomb_in, masked_ref, whole_ref, own_ref, factors, pattern, coulomb, sems):
    copies = [
        pltpu.make_async_copy(factors_in, factors, sems.at[0]),
        pltpu.make_async_copy(pattern_in, pattern, sems.at[1]),
        pltpu.make_async_copy(coulomb_in, coulomb, sems.at[2]),
    ]
    for copy in copies:
        copy.start()
    for copy in copies:
        copy.wait()
    parity = lax.axis_index("tm") & 1
    orb = factors.shape[1]
    for block in range(orb // BLOCK):
        lanes = pl.ds(block * BLOCK, BLOCK)
        keep = pattern[:, block : block + 1].astype(F32)
        for half in range(2):
            at = parity if half == 0 else 1 - parity
            part = factors[pl.ds(pl.multiple_of(at * HALF, HALF), HALF), lanes]
            part = (part.astype(F32) * keep).astype(BF16)
            masked_ref[pl.ds(half * HALF, HALF), lanes] = part
            if half == 0:
                whole_ref[pl.ds(0, HALF), lanes] = part
    c = coulomb[...]
    turned = pltpu.roll(c, HALF, 1)
    own = jnp.where(parity == 0, c, turned)
    own_ref[...] = own
    lane = lax.broadcasted_iota(jnp.int32, own.shape, 1)
    twice = jnp.where(lane < HALF, own, pltpu.roll(own, HALF, 1))
    high = twice.astype(BF16)
    rest = twice - high.astype(F32)
    middle = rest.astype(BF16)
    low = (rest - middle.astype(F32)).astype(BF16)
    zero = jnp.zeros((1, orb - 3 * BLOCK), BF16)
    row = jnp.concatenate([high, middle, low, zero], axis=1)
    rows = jnp.broadcast_to(row.astype(F32), (8, orb)).astype(BF16)
    whole_ref[pl.ds(HALF, 8), :] = rows


def prologue(factors, pattern, coulomb):
    own, orb = factors.shape
    return pl.pallas_call(
        prologue_kernel,
        out_shape=[
            jax.ShapeDtypeStruct((own, orb), BF16),
            jax.ShapeDtypeStruct((HALF + 8, orb), BF16),
            jax.ShapeDtypeStruct((1, own), F32),
        ],
        in_specs=[pl.BlockSpec(memory_space=pltpu.HBM)] * 3,
        out_specs=[VMEM] * 3,
        scratch_shapes=[
            pltpu.VMEM((own, orb), BF16),
            pltpu.VMEM(pattern.shape, jnp.int32),
            pltpu.VMEM((1, own), F32),
            pltpu.SemaphoreType.DMA((3,)),
        ],
        compiler_params=params(58),
    )(factors, pattern, coulomb[None, :])


def mix_kernel(west_ref, east_ref, onward_ref, both_ref):
    core = lax.axis_index("aux") & 1
    n = west_ref.shape[0]
    west, east = west_ref[...], east_ref[...]
    onward_ref[...] = jnp.where(core == 0, west, east)
    both_ref[pl.ds(0, n), :] = west
    both_ref[pl.ds(n, n), :] = east


def mix(west, east):
    n, orb = west.shape
    return pl.pallas_call(
        mix_kernel,
        out_shape=(jax.ShapeDtypeStruct((n, orb), BF16), jax.ShapeDtypeStruct((2 * n, orb), BF16)),
        in_specs=[VMEM] * 2,
        out_specs=[VMEM] * 2,
        compiler_params=params(8),
    )(west, east)


def weight_of(ref, row):
    parts = [ref[pl.ds(row, 1), pl.ds(k * BLOCK, BLOCK)].astype(F32) for k in range(3)]
    return parts[0] + (parts[1] + parts[2])


def weights_of(ref, row, blocks):
    lane = lax.broadcasted_iota(jnp.int32, (1, BLOCK), 1)
    pairs = []
    for k in range(0, blocks, 2):
        pairs.append(jnp.where(lane < HALF, weight_of(ref, row + k), weight_of(ref, row + k + 1)))
    return jnp.concatenate(pairs, axis=1) if len(pairs) > 1 else pairs[0]


def chunk_kernel(pieces, count, first, *refs):
    right_own, right_other, left_own, left_other = refs[:4]
    rows = refs[4 : 4 + count]
    rest = refs[4 + count :]
    if not first:
        acc_own, acc_other = rest[:2]
        rest = rest[2:]
    out_own, out_other = rest
    own = out_own.shape[1]
    for t in range(out_own.shape[0]):
        right = jnp.concatenate([right_own[t], right_other[t]], axis=0)
        left = jnp.concatenate([left_own[t], left_other[t]], axis=0)
        total = None
        for piece in pieces:
            part = jnp.concatenate([rows[at][pl.ds(start, n), :] for at, start, n in piece[0]], axis=0)
            weight = weights_of(rows[piece[1]], piece[2], part.shape[0] // HALF)
            a = lax.dot_general(right, part, NT, preferred_element_type=F32)
            m = lax.dot_general(left, part, NT, preferred_element_type=F32)
            k = (a * weight * (a * m)).astype(BF16)
            d = lax.dot_general(k, part, NN, preferred_element_type=F32)
            total = d if total is None else total + d
        mine, theirs = total[:own], total[own:]
        if not first:
            mine, theirs = acc_own[t] + mine, acc_other[t] + theirs
        out_own[t] = mine
        out_other[t] = theirs.astype(out_other.dtype)


def chunk(sides, rows, pieces, acc=None, last=False):
    times, own, orb = sides[0].shape
    shape = jax.ShapeDtypeStruct((times, own, orb), F32)
    extra = () if acc is None else tuple(acc)
    theirs = jax.ShapeDtypeStruct((times, own, orb), BF16 if last else F32)
    aliases = {}
    if acc is not None:
        aliases[4 + len(rows)] = 0
        if not last:
            aliases[5 + len(rows)] = 1
    flops = len(pieces) * 4 * HALF * times * 3 * 2 * (2 * own) * orb
    return pl.pallas_call(
        functools.partial(chunk_kernel, tuple(pieces), len(rows), acc is None),
        out_shape=(shape, theirs),
        in_specs=[VMEM] * (4 + len(rows) + len(extra)),
        out_specs=(VMEM, VMEM),
        input_output_aliases=aliases,
        compiler_params=params(16),
        cost_estimate=pl.CostEstimate(flops=flops, bytes_accessed=2 << 20, transcendentals=0),
    )(*sides, *rows, *extra)


def finish_kernel(own_ref, got_ref, coulomb_ref, out_ref):
    chips, times, rows, _ = out_ref.shape
    for t in range(times):
        d = jnp.transpose(own_ref[t] + got_ref[t].astype(F32)) * coulomb_ref[...]
        d = d.astype(BF16)
        for chip in range(chips):
            out_ref[chip, t] = d[chip * rows : (chip + 1) * rows]


def sigma_kernel(part_ref, *refs):
    here, here_q, west, east, sides_q, far, far_q = refs[:7]
    keep_ref, send_ref, lhs, total_ref = refs[7:]
    skip = west.shape[0]
    columns = [((here, 0), (here_q, 0)), ((west, 0), (sides_q, 0)), ((east, 0), (sides_q, skip)), ((far, 0), (far_q, 0))]
    chips, times, i_rows, width = part_ref.shape
    me = lax.axis_index("aux")
    core, x, z = me & 1, (me >> 1) & 3, me >> 3
    total = None
    for column, dx in enumerate((0, 3, 1, 2)):
        parts = []
        for k, dz in enumerate((0, 3, 1, 2)):
            source = ((z + dz) & 3) * 4 + ((x + dx) & 3)
            for t in range(times):
                at = pl.ds((column * 4 + k) * width, width)
                lhs[pl.ds(t * i_rows, i_rows), at] = part_ref[source, t]
            for ref, start in columns[column]:
                parts.append(ref[pl.ds(start + k * HALF, HALF), :])
        d = lax.dot_general(
            lhs[:, pl.ds(column * 4 * width, 4 * width)],
            jnp.concatenate(parts, axis=0),
            NN,
            preferred_element_type=F32,
        )
        total = d if total is None else total + d
    total_ref[...] = total
    half = i_rows // 2
    for t in range(times):
        keep = pl.multiple_of(t * i_rows + core * half, half)
        send = pl.multiple_of(t * i_rows + (1 - core) * half, half)
        keep_ref[t] = total_ref[pl.ds(keep, half), :]
        send_ref[t] = total_ref[pl.ds(send, half), :]


def add_kernel(keep_ref, got_ref, out_ref):
    for t in range(keep_ref.shape[0]):
        out_ref[:, t, :] = keep_ref[t] + got_ref[t]


def local(green, factors, pattern, coulomb):
    times, orb, _ = green.shape
    own = factors.shape[0]
    barrier = lax.optimization_barrier
    masked, whole, coulomb = prologue(factors, pattern, coulomb)

    below = along_z(whole, 1)
    above = along_z(whole, -1)
    beyond = two_along_z(whole)
    left = jnp.einsum("qo,tok->tqk", masked, green, preferred_element_type=F32).astype(BF16)
    right = jnp.einsum("qo,tko->tqk", masked, green, preferred_element_type=F32).astype(BF16)
    right_other = other_core(right)

    blocks = [whole, below, above, beyond]
    weights = [block[HALF : HALF + 1] for block in blocks] + [jnp.zeros((4, orb), BF16)]
    here = jnp.concatenate([block[:HALF] for block in blocks] + weights, axis=0)
    here, left = barrier((here, left))

    n = 4 * HALF
    west = along_x(here, 1)
    east = along_x(here, -1)
    rest = other_parity(here[HALF:])
    left = two_along_z(left)
    here_q = jnp.concatenate([masked[HALF:], rest], axis=0)

    west, east, here_q, left = barrier((west, east, here_q, left))
    onward, both = mix(west, east)
    far = split_x(onward)
    sides_q = other_parity(both)
    left = two_along_z(left)
    left, _ = barrier((left, far[:8, :BLOCK]))
    far_q = other_parity(far)
    left_other = other_core(left)

    def piece(at, start=0):
        return (((at, start, n),), at, start + n)

    sides = (right, right_other, left, left_other)
    acc = chunk(sides, (here, here_q), [piece(0), piece(1)])
    acc = chunk(sides, (west, east), [piece(0), piece(1)], acc)
    acc = chunk(sides, (sides_q,), [piece(0), piece(0, n + 8)], acc)
    keep, theirs = chunk(sides, (far, far_q), [piece(0), piece(1)], acc, last=True)

    got = other_core(theirs)
    chips, i_rows = 16, orb // 16
    part = pl.pallas_call(
        finish_kernel,
        out_shape=jax.ShapeDtypeStruct((chips, times, i_rows, own), BF16),
        in_specs=[VMEM] * 3,
        out_specs=VMEM,
        compiler_params=params(12),
    )(keep, got, coulomb)
    groups = [[2 * chip + core for chip in range(chips)] for core in range(2)]
    part = lax.all_to_all(part, "aux", 0, 0, axis_index_groups=groups, tiled=True)

    shape = jax.ShapeDtypeStruct((times, i_rows // 2, orb), F32)
    keep, theirs = pl.pallas_call(
        sigma_kernel,
        out_shape=(shape, shape),
        in_specs=[VMEM] * 8,
        out_specs=(VMEM, VMEM),
        scratch_shapes=[
            pltpu.VMEM((times * i_rows, chips * own), BF16),
            pltpu.VMEM((times * i_rows, orb), F32),
        ],
        compiler_params=params(12),
    )(part, here, here_q, west, east, sides_q, far, far_q)
    got = other_core(theirs)
    return pl.pallas_call(
        add_kernel,
        out_shape=jax.ShapeDtypeStruct((i_rows // 2, times, orb), F32),
        in_specs=[VMEM] * 2,
        out_specs=VMEM,
        compiler_params=params(8),
    )(keep, got)


def solution(mesh):
    in_specs = (P("tm", None, None), P("aux", None), P("aux", None), P("aux"))
    out_specs = P("aux", "tm", None)
    return jax.shard_map(local, mesh=mesh, in_specs=in_specs, out_specs=out_specs, check_vma=False)
```

```python
import functools

import jax
import jax.numpy as jnp
from jax import lax
from jax.experimental import pallas as pl
from jax.experimental.pallas import tpu as pltpu
from jax.sharding import PartitionSpec as P

BLOCK = 128
HALF = 64
F32, BF16 = jnp.float32, jnp.bfloat16
BOTH = ("tm", "aux")
NT = (((1,), (1,)), ((), ()))
NN = (((1,), (0,)), ((), ()))
VMEM = pl.BlockSpec(memory_space=pltpu.VMEM)


def device_at(x, y, z, core):
    return (z // 4 * 4 + y) * 32 + (z % 4 * 4 + x) * 2 + core


def send(value, to):
    pairs = []
    for x in range(4):
        for y in range(4):
            for z in range(8):
                for core in range(2):
                    tx, ty, tz, tcore = to(x, y, z, core)
                    pairs.append((device_at(x, y, z, core), device_at(tx % 4, ty % 4, tz % 8, tcore)))
    return lax.ppermute(value, BOTH, sorted(pairs))


def along_x(value, step):
    return send(value, lambda x, y, z, core: (x + step, y, z, core))


def along_z(value, step):
    return send(value, lambda x, y, z, core: (x, y, z + step, core))


def other_core(value):
    return send(value, lambda x, y, z, core: (x, y, z, 1 - core))


def two_along_z(value):
    return send(value, lambda x, y, z, core: (x, y, z + (2 if core == 0 else -2), core))


def split_x(value):
    return send(value, lambda x, y, z, core: (x + (1 if core == 0 else -1), y, z, core))


def other_parity(value):
    return send(value, lambda x, y, z, core: (x, y + (1 if y % 2 == core else -1), z, core))


def params(mib):
    return pltpu.CompilerParams(vmem_limit_bytes=mib << 20)


def prologue_kernel(factors_in, pattern_in, coulomb_in, masked_ref, whole_ref, own_ref, factors, pattern, coulomb, sems):
    copies = [
        pltpu.make_async_copy(factors_in, factors, sems.at[0]),
        pltpu.make_async_copy(pattern_in, pattern, sems.at[1]),
        pltpu.make_async_copy(coulomb_in, coulomb, sems.at[2]),
    ]
    for copy in copies:
        copy.start()
    for copy in copies:
        copy.wait()
    parity = lax.axis_index("tm") & 1
    orb = factors.shape[1]
    for block in range(orb // BLOCK):
        lanes = pl.ds(block * BLOCK, BLOCK)
        keep = pattern[:, block : block + 1].astype(F32)
        for half in range(2):
            at = parity if half == 0 else 1 - parity
            part = factors[pl.ds(pl.multiple_of(at * HALF, HALF), HALF), lanes]
            part = (part.astype(F32) * keep).astype(BF16)
            masked_ref[pl.ds(half * HALF, HALF), lanes] = part
            if half == 0:
                whole_ref[pl.ds(0, HALF), lanes] = part
    c = coulomb[...]
    turned = pltpu.roll(c, HALF, 1)
    own = jnp.where(parity == 0, c, turned)
    own_ref[...] = own
    lane = lax.broadcasted_iota(jnp.int32, own.shape, 1)
    twice = jnp.where(lane < HALF, own, pltpu.roll(own, HALF, 1))
    high = twice.astype(BF16)
    rest = twice - high.astype(F32)
    middle = rest.astype(BF16)
    low = (rest - middle.astype(F32)).astype(BF16)
    zero = jnp.zeros((1, orb - 3 * BLOCK), BF16)
    row = jnp.concatenate([high, middle, low, zero], axis=1)
    rows = jnp.broadcast_to(row.astype(F32), (8, orb)).astype(BF16)
    whole_ref[pl.ds(HALF, 8), :] = rows


def prologue(factors, pattern, coulomb):
    own, orb = factors.shape
    return pl.pallas_call(
        prologue_kernel,
        out_shape=[
            jax.ShapeDtypeStruct((own, orb), BF16),
            jax.ShapeDtypeStruct((HALF + 8, orb), BF16),
            jax.ShapeDtypeStruct((1, own), F32),
        ],
        in_specs=[pl.BlockSpec(memory_space=pltpu.HBM)] * 3,
        out_specs=[VMEM] * 3,
        scratch_shapes=[
            pltpu.VMEM((own, orb), BF16),
            pltpu.VMEM(pattern.shape, jnp.int32),
            pltpu.VMEM((1, own), F32),
            pltpu.SemaphoreType.DMA((3,)),
        ],
        compiler_params=params(58),
    )(factors, pattern, coulomb[None, :])


def mix_kernel(west_ref, east_ref, onward_ref, both_ref):
    core = lax.axis_index("aux") & 1
    n = west_ref.shape[0]
    west, east = west_ref[...], east_ref[...]
    onward_ref[...] = jnp.where(core == 0, west, east)
    both_ref[pl.ds(0, n), :] = west
    both_ref[pl.ds(n, n), :] = east


def mix(west, east):
    n, orb = west.shape
    return pl.pallas_call(
        mix_kernel,
        out_shape=(jax.ShapeDtypeStruct((n, orb), BF16), jax.ShapeDtypeStruct((2 * n, orb), BF16)),
        in_specs=[VMEM] * 2,
        out_specs=[VMEM] * 2,
        compiler_params=params(8),
    )(west, east)


def weight_of(ref, row):
    parts = [ref[pl.ds(row, 1), pl.ds(k * BLOCK, BLOCK)].astype(F32) for k in range(3)]
    return parts[0] + (parts[1] + parts[2])


def weights_of(ref, row, blocks):
    lane = lax.broadcasted_iota(jnp.int32, (1, BLOCK), 1)
    pairs = []
    for k in range(0, blocks, 2):
        pairs.append(jnp.where(lane < HALF, weight_of(ref, row + k), weight_of(ref, row + k + 1)))
    return jnp.concatenate(pairs, axis=1) if len(pairs) > 1 else pairs[0]


def chunk_kernel(pieces, count, first, *refs):
    right_own, right_other, left_own, left_other = refs[:4]
    rows = refs[4 : 4 + count]
    rest = refs[4 + count :]
    if not first:
        acc_own, acc_other = rest[:2]
        rest = rest[2:]
    out_own, out_other = rest
    own = out_own.shape[1]
    for t in range(out_own.shape[0]):
        right = jnp.concatenate([right_own[t], right_other[t]], axis=0)
        left = jnp.concatenate([left_own[t], left_other[t]], axis=0)
        total = None
        for piece in pieces:
            part = jnp.concatenate([rows[at][pl.ds(start, n), :] for at, start, n in piece[0]], axis=0)
            weight = weights_of(rows[piece[1]], piece[2], part.shape[0] // HALF)
            a = lax.dot_general(right, part, NT, preferred_element_type=F32)
            m = lax.dot_general(left, part, NT, preferred_element_type=F32)
            k = (a * weight * (a * m)).astype(BF16)
            d = lax.dot_general(k, part, NN, preferred_element_type=F32)
            total = d if total is None else total + d
        mine, theirs = total[:own], total[own:]
        if not first:
            mine, theirs = acc_own[t] + mine, acc_other[t] + theirs
        out_own[t] = mine
        out_other[t] = theirs.astype(out_other.dtype)


def chunk(sides, rows, pieces, acc=None, last=False):
    times, own, orb = sides[0].shape
    shape = jax.ShapeDtypeStruct((times, own, orb), F32)
    extra = () if acc is None else tuple(acc)
    theirs = jax.ShapeDtypeStruct((times, own, orb), BF16 if last else F32)
    aliases = {}
    if acc is not None:
        aliases[4 + len(rows)] = 0
        if not last:
            aliases[5 + len(rows)] = 1
    flops = len(pieces) * 4 * HALF * times * 3 * 2 * (2 * own) * orb
    return pl.pallas_call(
        functools.partial(chunk_kernel, tuple(pieces), len(rows), acc is None),
        out_shape=(shape, theirs),
        in_specs=[VMEM] * (4 + len(rows) + len(extra)),
        out_specs=(VMEM, VMEM),
        input_output_aliases=aliases,
        compiler_params=params(16),
        cost_estimate=pl.CostEstimate(flops=flops, bytes_accessed=2 << 20, transcendentals=0),
    )(*sides, *rows, *extra)


def finish_kernel(own_ref, got_ref, coulomb_ref, out_ref):
    chips, times, rows, _ = out_ref.shape
    for t in range(times):
        d = jnp.transpose(own_ref[t] + got_ref[t].astype(F32)) * coulomb_ref[...]
        d = d.astype(BF16)
        for chip in range(chips):
            out_ref[chip, t] = d[chip * rows : (chip + 1) * rows]


def sigma_kernel(part_ref, *refs):
    here, here_q, west, east, sides_q, far, far_q = refs[:7]
    keep_ref, send_ref, lhs, total_ref = refs[7:]
    skip = west.shape[0]
    columns = [((here, 0), (here_q, 0)), ((west, 0), (sides_q, 0)), ((east, 0), (sides_q, skip)), ((far, 0), (far_q, 0))]
    chips, times, i_rows, width = part_ref.shape
    me = lax.axis_index("aux")
    core, x, z = me & 1, (me >> 1) & 3, me >> 3
    total = None
    for column, dx in enumerate((0, 3, 1, 2)):
        parts = []
        for k, dz in enumerate((0, 3, 1, 2)):
            source = ((z + dz) & 3) * 4 + ((x + dx) & 3)
            for t in range(times):
                at = pl.ds((column * 4 + k) * width, width)
                lhs[pl.ds(t * i_rows, i_rows), at] = part_ref[source, t]
            for ref, start in columns[column]:
                parts.append(ref[pl.ds(start + k * HALF, HALF), :])
        d = lax.dot_general(
            lhs[:, pl.ds(column * 4 * width, 4 * width)],
            jnp.concatenate(parts, axis=0),
            NN,
            preferred_element_type=F32,
        )
        total = d if total is None else total + d
    total_ref[...] = total
    half = i_rows // 2
    for t in range(times):
        keep = pl.multiple_of(t * i_rows + core * half, half)
        send = pl.multiple_of(t * i_rows + (1 - core) * half, half)
        keep_ref[t] = total_ref[pl.ds(keep, half), :]
        send_ref[t] = total_ref[pl.ds(send, half), :]


def add_kernel(keep_ref, got_ref, out_ref):
    for t in range(keep_ref.shape[0]):
        out_ref[:, t, :] = keep_ref[t] + got_ref[t]


def local(green, factors, pattern, coulomb):
    times, orb, _ = green.shape
    own = factors.shape[0]
    barrier = lax.optimization_barrier
    masked, whole, coulomb = prologue(factors, pattern, coulomb)

    beyond = two_along_z(whole)
    below = along_z(whole, 1)
    above = along_z(whole, -1)
    left = jnp.einsum("qo,tok->tqk", masked, green, preferred_element_type=F32).astype(BF16)
    right = jnp.einsum("qo,tko->tqk", masked, green, preferred_element_type=F32).astype(BF16)
    right_other = other_core(right)

    blocks = [whole, below, above, beyond]
    weights = [block[HALF : HALF + 1] for block in blocks] + [jnp.zeros((4, orb), BF16)]
    here = jnp.concatenate([block[:HALF] for block in blocks] + weights, axis=0)
    here, left = barrier((here, left))

    n = 4 * HALF
    left = two_along_z(left)
    west = along_x(here, 1)
    east = along_x(here, -1)
    rest = other_parity(here[HALF:])
    here_q = jnp.concatenate([masked[HALF:], rest], axis=0)

    west, east, here_q = barrier((west, east, here_q))
    onward, both = mix(west, east)
    far = split_x(onward)
    sides_q = other_parity(both)
    left = two_along_z(left)
    left, _ = barrier((left, far[:8, :BLOCK]))
    far_q = other_parity(far)
    left_other = other_core(left)

    def piece(at, start=0):
        return (((at, start, n),), at, start + n)

    sides = (right, right_other, left, left_other)
    acc = chunk(sides, (here, here_q), [piece(0), piece(1)])
    acc = chunk(sides, (west, east), [piece(0), piece(1)], acc)
    acc = chunk(sides, (sides_q, far), [piece(0), piece(0, n + 8), piece(1)], acc)
    keep, theirs = chunk(sides, (far_q,), [piece(0)], acc, last=True)

    got = other_core(theirs)
    chips, i_rows = 16, orb // 16
    part = pl.pallas_call(
        finish_kernel,
        out_shape=jax.ShapeDtypeStruct((chips, times, i_rows, own), BF16),
        in_specs=[VMEM] * 3,
        out_specs=VMEM,
        compiler_params=params(12),
    )(keep, got, coulomb)
    groups = [[2 * chip + core for chip in range(chips)] for core in range(2)]
    part = lax.all_to_all(part, "aux", 0, 0, axis_index_groups=groups, tiled=True)

    shape = jax.ShapeDtypeStruct((times, i_rows // 2, orb), F32)
    keep, theirs = pl.pallas_call(
        sigma_kernel,
        out_shape=(shape, shape),
        in_specs=[VMEM] * 8,
        out_specs=(VMEM, VMEM),
        scratch_shapes=[
            pltpu.VMEM((times * i_rows, chips * own), BF16),
            pltpu.VMEM((times * i_rows, orb), F32),
        ],
        compiler_params=params(12),
    )(part, here, here_q, west, east, sides_q, far, far_q)
    got = other_core(theirs)
    return pl.pallas_call(
        add_kernel,
        out_shape=jax.ShapeDtypeStruct((i_rows // 2, times, orb), F32),
        in_specs=[VMEM] * 2,
        out_specs=VMEM,
        compiler_params=params(8),
    )(keep, got)


def solution(mesh):
    in_specs = (P("tm", None, None), P("aux", None), P("aux", None), P("aux"))
    out_specs = P("aux", "tm", None)
    return jax.shard_map(local, mesh=mesh, in_specs=in_specs, out_specs=out_specs, check_vma=False)
```

```python
import functools

import jax
import jax.numpy as jnp
from jax import lax
from jax.experimental import pallas as pl
from jax.experimental.pallas import tpu as pltpu
from jax.sharding import PartitionSpec as P

BLOCK = 128
HALF = 64
COLUMN = 512
F32, BF16 = jnp.float32, jnp.bfloat16
BOTH = ("tm", "aux")
NT = (((1,), (1,)), ((), ()))
NN = (((1,), (0,)), ((), ()))
VMEM = pl.BlockSpec(memory_space=pltpu.VMEM)


def device_at(x, y, z, core):
    return (z // 4 * 4 + y) * 32 + (z % 4 * 4 + x) * 2 + core


def send(value, to):
    pairs = []
    for x in range(4):
        for y in range(4):
            for z in range(8):
                for core in range(2):
                    tx, ty, tz, tcore = to(x, y, z, core)
                    pairs.append((device_at(x, y, z, core), device_at(tx % 4, ty % 4, tz % 8, tcore)))
    return lax.ppermute(value, BOTH, sorted(pairs))


def along_x(value, step):
    return send(value, lambda x, y, z, core: (x + step, y, z, core))


def along_z(value, step):
    return send(value, lambda x, y, z, core: (x, y, z + step, core))


def other_core(value):
    return send(value, lambda x, y, z, core: (x, y, z, 1 - core))


def two_along_z(value):
    return send(value, lambda x, y, z, core: (x, y, z + (2 if core == 0 else -2), core))


def split_x(value):
    return send(value, lambda x, y, z, core: (x + (1 if core == 0 else -1), y, z, core))


def other_parity(value):
    return send(value, lambda x, y, z, core: (x, y + (1 if y % 2 == core else -1), z, core))


def params(mib):
    return pltpu.CompilerParams(vmem_limit_bytes=mib << 20)


def prologue_kernel(factors_in, pattern_in, coulomb_in, block_ref, whole_ref, own_ref, factors, pattern, coulomb, sems):
    copies = [
        pltpu.make_async_copy(factors_in, factors, sems.at[0]),
        pltpu.make_async_copy(pattern_in, pattern, sems.at[1]),
        pltpu.make_async_copy(coulomb_in, coulomb, sems.at[2]),
    ]
    for copy in copies:
        copy.start()
    for copy in copies:
        copy.wait()
    parity = lax.axis_index("tm") & 1
    rows, orb = factors.shape
    for block in range(orb // BLOCK):
        lanes = pl.ds(block * BLOCK, BLOCK)
        keep = pattern[:, block : block + 1].astype(F32)
        for half in range(2):
            at = parity if half == 0 else 1 - parity
            part = factors[pl.ds(pl.multiple_of(at * HALF, HALF), HALF), lanes]
            part = (part.astype(F32) * keep).astype(BF16)
            block_ref[pl.ds(half * HALF, HALF), lanes] = part
            if half == 0:
                whole_ref[pl.ds(0, HALF), lanes] = part
    c = coulomb[...]
    own = jnp.where(parity == 0, c, pltpu.roll(c, HALF, 1))
    own_ref[...] = own
    lane = lax.broadcasted_iota(jnp.int32, own.shape, 1)
    twice = jnp.where(lane < HALF, own, pltpu.roll(own, HALF, 1))
    for ref, row, value in ((block_ref, rows, own), (whole_ref, HALF, twice)):
        high = value.astype(BF16)
        rest = value - high.astype(F32)
        middle = rest.astype(BF16)
        low = (rest - middle.astype(F32)).astype(BF16)
        zero = jnp.zeros((1, orb - 3 * BLOCK), BF16)
        line = jnp.concatenate([high, middle, low, zero], axis=1)
        ref[pl.ds(row, 8), :] = jnp.broadcast_to(line.astype(F32), (8, orb)).astype(BF16)


def prologue(factors, pattern, coulomb):
    own, orb = factors.shape
    return pl.pallas_call(
        prologue_kernel,
        out_shape=[
            jax.ShapeDtypeStruct((own + 8, orb), BF16),
            jax.ShapeDtypeStruct((HALF + 8, orb), BF16),
            jax.ShapeDtypeStruct((1, own), F32),
        ],
        in_specs=[pl.BlockSpec(memory_space=pltpu.HBM)] * 3,
        out_specs=[VMEM] * 3,
        scratch_shapes=[
            pltpu.VMEM((own, orb), BF16),
            pltpu.VMEM(pattern.shape, jnp.int32),
            pltpu.VMEM((1, own), F32),
            pltpu.SemaphoreType.DMA((3,)),
        ],
        compiler_params=params(58),
    )(factors, pattern, coulomb[None, :])


def pick_kernel(west_ref, east_ref, onward_ref):
    core = lax.axis_index("aux") & 1
    onward_ref[...] = jnp.where(core == 0, west_ref[...], east_ref[...])


def pick(west, east):
    return pl.pallas_call(
        pick_kernel,
        out_shape=jax.ShapeDtypeStruct(west.shape, BF16),
        in_specs=[VMEM] * 2,
        out_specs=VMEM,
        compiler_params=params(8),
    )(west, east)


def mix_kernel(west_ref, east_ref, onward_ref, both_ref):
    core = lax.axis_index("aux") & 1
    n = west_ref.shape[0]
    west, east = west_ref[...], east_ref[...]
    onward_ref[...] = jnp.where(core == 0, west, east)
    both_ref[pl.ds(0, n), :] = west
    both_ref[pl.ds(n, n), :] = east


def mix(west, east):
    n, orb = west.shape
    return pl.pallas_call(
        mix_kernel,
        out_shape=(jax.ShapeDtypeStruct((n, orb), BF16), jax.ShapeDtypeStruct((2 * n, orb), BF16)),
        in_specs=[VMEM] * 2,
        out_specs=[VMEM] * 2,
        compiler_params=params(8),
    )(west, east)


def weight_of(ref, row):
    parts = [ref[pl.ds(row, 1), pl.ds(k * BLOCK, BLOCK)].astype(F32) for k in range(3)]
    return parts[0] + (parts[1] + parts[2])


def column_of(refs, column):
    o, p, p_start, q, q_start = column
    third = 3 * HALF
    lane = lax.broadcasted_iota(jnp.int32, (1, BLOCK), 1)
    rows = [refs[o][pl.ds(0, BLOCK), :], refs[p][pl.ds(p_start, third), :], refs[q][pl.ds(q_start, third), :]]
    p_lines = [weight_of(refs[p], p_start + third + k) for k in range(3)]
    q_lines = [weight_of(refs[q], q_start + third + k) for k in range(3)]
    lines = p_lines + q_lines
    pairs = [jnp.where(lane < HALF, lines[k], lines[k + 1]) for k in range(0, 6, 2)]
    return jnp.concatenate(rows, axis=0), jnp.concatenate([weight_of(refs[o], BLOCK)] + pairs, axis=1)


def square_kernel(columns, *refs):
    right_own, right_other = refs[:2]
    rows = refs[2 : len(refs) - len(columns)]
    outs = refs[len(refs) - len(columns) :]
    for column, out in zip(columns, outs):
        for t in range(right_own.shape[0]):
            right = jnp.concatenate([right_own[t], right_other[t]], axis=0)
            part, weight = column_of(rows, column)
            a = lax.dot_general(right, part, NT, preferred_element_type=F32)
            out[t] = a * a * weight


def squares(right, right_other, rows, columns):
    times, own, orb = right.shape
    shape = jax.ShapeDtypeStruct((times, 2 * own, COLUMN), F32)
    flops = len(columns) * times * 2 * (2 * own) * COLUMN * orb
    return pl.pallas_call(
        functools.partial(square_kernel, tuple(columns)),
        out_shape=[shape] * len(columns),
        in_specs=[VMEM] * (2 + len(rows)),
        out_specs=[VMEM] * len(columns),
        compiler_params=params(12),
        cost_estimate=pl.CostEstimate(flops=flops, bytes_accessed=2 << 20, transcendentals=0),
    )(right, right_other, *rows)


def chunk_kernel(columns, sides, count, first, *refs):
    left_own, left_other = refs[sides - 2 : sides]
    rows = refs[sides : sides + count]
    rest = refs[sides + count :]
    given = () if sides == 4 else rest[: len(columns)]
    rest = rest[len(given) :]
    if not first:
        acc_own, acc_other = rest[:2]
        rest = rest[2:]
    out_own, out_other = rest
    own = out_own.shape[1]
    for t in range(out_own.shape[0]):
        left = jnp.concatenate([left_own[t], left_other[t]], axis=0)
        total = None
        for at, column in enumerate(columns):
            part, weight = column_of(rows, column)
            if given:
                square = given[at][t]
            else:
                right = jnp.concatenate([refs[0][t], refs[1][t]], axis=0)
                a = lax.dot_general(right, part, NT, preferred_element_type=F32)
                square = a * a * weight
            m = lax.dot_general(left, part, NT, preferred_element_type=F32)
            k = (square * m).astype(BF16)
            d = lax.dot_general(k, part, NN, preferred_element_type=F32)
            total = d if total is None else total + d
        mine, theirs = total[:own], total[own:]
        if not first:
            mine, theirs = acc_own[t] + mine, acc_other[t] + theirs
        out_own[t] = mine
        out_other[t] = theirs.astype(out_other.dtype)


def chunk(sides, rows, columns, given=(), acc=(), last=False):
    times, own, orb = sides[0].shape
    shape = jax.ShapeDtypeStruct((times, own, orb), F32)
    theirs = jax.ShapeDtypeStruct((times, own, orb), BF16 if last else F32)
    at = len(sides) + len(rows) + len(given)
    aliases = {}
    if acc:
        aliases[at] = 0
        if not last:
            aliases[at + 1] = 1
    flops = len(columns) * times * 2 * 2 * (2 * own) * COLUMN * orb
    return pl.pallas_call(
        functools.partial(chunk_kernel, tuple(columns), len(sides), len(rows), not acc),
        out_shape=(shape, theirs),
        in_specs=[VMEM] * (at + len(acc)),
        out_specs=(VMEM, VMEM),
        input_output_aliases=aliases,
        compiler_params=params(16),
        cost_estimate=pl.CostEstimate(flops=flops, bytes_accessed=2 << 20, transcendentals=0),
    )(*sides, *rows, *given, *acc)


def finish_kernel(own_ref, got_ref, coulomb_ref, out_ref):
    chips, times, rows, _ = out_ref.shape
    for t in range(times):
        d = jnp.transpose(own_ref[t] + got_ref[t].astype(F32)) * coulomb_ref[...]
        d = d.astype(BF16)
        for chip in range(chips):
            out_ref[chip, t] = d[chip * rows : (chip + 1) * rows]


def sigma_kernel(part_ref, *refs):
    blocks, p_parts, q_parts = refs[:4], refs[4:8], (refs[8], refs[9], refs[9], refs[10])
    keep_ref, send_ref, lhs, total_ref = refs[11:]
    chips, times, i_rows, width = part_ref.shape
    me = lax.axis_index("aux")
    core, x, z = me & 1, (me >> 1) & 3, me >> 3
    total = None
    for column, dx in enumerate((0, 3, 1, 2)):
        q_start = p_parts[2].shape[0] if column == 2 else 0
        parts = [blocks[column][pl.ds(0, BLOCK), :]]
        for k, dz in enumerate((0, 3, 1, 2)):
            source = ((z + dz) & 3) * 4 + ((x + dx) & 3)
            for t in range(times):
                at = pl.ds((column * 4 + k) * width, width)
                lhs[pl.ds(t * i_rows, i_rows), at] = part_ref[source, t]
            if k > 0:
                parts.append(p_parts[column][pl.ds((k - 1) * HALF, HALF), :])
                parts.append(q_parts[column][pl.ds(q_start + (k - 1) * HALF, HALF), :])
        d = lax.dot_general(
            lhs[:, pl.ds(column * 4 * width, 4 * width)],
            jnp.concatenate(parts, axis=0),
            NN,
            preferred_element_type=F32,
        )
        total = d if total is None else total + d
    total_ref[...] = total
    half = i_rows // 2
    for t in range(times):
        keep = pl.multiple_of(t * i_rows + core * half, half)
        send = pl.multiple_of(t * i_rows + (1 - core) * half, half)
        keep_ref[t] = total_ref[pl.ds(keep, half), :]
        send_ref[t] = total_ref[pl.ds(send, half), :]


def add_kernel(keep_ref, got_ref, out_ref):
    for t in range(keep_ref.shape[0]):
        out_ref[:, t, :] = keep_ref[t] + got_ref[t]


def local(green, factors, pattern, coulomb):
    times, orb, _ = green.shape
    own = factors.shape[0]
    barrier = lax.optimization_barrier
    block, whole, coulomb = prologue(factors, pattern, coulomb)
    masked = block[:own]

    beyond = two_along_z(whole)
    below = along_z(whole, 1)
    above = along_z(whole, -1)
    left = jnp.einsum("qo,tok->tqk", masked, green, preferred_element_type=F32).astype(BF16)
    left = two_along_z(left)
    west_o = along_x(block, 1)
    east_o = along_x(block, -1)

    near = [below, above, beyond]
    lines = [part[HALF : HALF + 1] for part in near] + [jnp.zeros((5, orb), BF16)]
    here_p = jnp.concatenate([part[:HALF] for part in near] + lines, axis=0)
    here_p, west_o, east_o = barrier((here_p, west_o, east_o))
    west_p = along_x(here_p, 1)
    east_p = along_x(here_p, -1)
    here_q = other_parity(here_p)
    far_o = split_x(pick(west_o, east_o))
    left = two_along_z(left)
    right = jnp.einsum("qo,tko->tqk", masked, green, preferred_element_type=F32).astype(BF16)
    right_other = other_core(right)

    west_p, east_p, here_q, far_o, right_other = barrier((west_p, east_p, here_q, far_o, right_other))
    onward, both = mix(west_p, east_p)
    far_p = split_x(onward)
    sides_q = other_parity(both)
    (here_z,) = squares(right, right_other, (block, here_p, here_q), [(0, 1, 0, 2, 0)])
    far_q = other_parity(far_p)
    left_other = other_core(left)

    skip = west_p.shape[0]
    pair = (west_o, west_p, east_o, east_p, sides_q)
    columns = [(0, 1, 0, 4, 0), (2, 3, 0, 4, skip)]
    pair_z = squares(right, right_other, pair, columns)
    lefts = (left, left_other)
    acc = chunk(lefts, pair, columns, given=pair_z)
    acc = chunk(lefts, (block, here_p, here_q), [(0, 1, 0, 2, 0)], given=(here_z,), acc=acc)
    sides = (right, right_other, left, left_other)
    keep, theirs = chunk(sides, (far_o, far_p, far_q), [(0, 1, 0, 2, 0)], acc=acc, last=True)

    got = other_core(theirs)
    chips, i_rows = 16, orb // 16
    part = pl.pallas_call(
        finish_kernel,
        out_shape=jax.ShapeDtypeStruct((chips, times, i_rows, own), BF16),
        in_specs=[VMEM] * 3,
        out_specs=VMEM,
        compiler_params=params(12),
    )(keep, got, coulomb)
    groups = [[2 * chip + core for chip in range(chips)] for core in range(2)]
    part = lax.all_to_all(part, "aux", 0, 0, axis_index_groups=groups, tiled=True)

    shape = jax.ShapeDtypeStruct((times, i_rows // 2, orb), F32)
    keep, theirs = pl.pallas_call(
        sigma_kernel,
        out_shape=(shape, shape),
        in_specs=[VMEM] * 12,
        out_specs=(VMEM, VMEM),
        scratch_shapes=[
            pltpu.VMEM((times * i_rows, chips * own), BF16),
            pltpu.VMEM((times * i_rows, orb), F32),
        ],
        compiler_params=params(12),
    )(part, block, west_o, east_o, far_o, here_p, west_p, east_p, far_p, here_q, sides_q, far_q)
    got = other_core(theirs)
    return pl.pallas_call(
        add_kernel,
        out_shape=jax.ShapeDtypeStruct((i_rows // 2, times, orb), F32),
        in_specs=[VMEM] * 2,
        out_specs=VMEM,
        compiler_params=params(8),
    )(keep, got)


def solution(mesh):
    in_specs = (P("tm", None, None), P("aux", None), P("aux", None), P("aux"))
    out_specs = P("aux", "tm", None)
    return jax.shard_map(local, mesh=mesh, in_specs=in_specs, out_specs=out_specs, check_vma=False)
```

```python
import functools

import jax
import jax.numpy as jnp
from jax import lax
from jax.experimental import pallas as pl
from jax.experimental.pallas import tpu as pltpu
from jax.sharding import PartitionSpec as P

BLOCK = 128
HALF = 64
COLUMN = 512
F32, BF16 = jnp.float32, jnp.bfloat16
BOTH = ("tm", "aux")
NT = (((1,), (1,)), ((), ()))
NN = (((1,), (0,)), ((), ()))
VMEM = pl.BlockSpec(memory_space=pltpu.VMEM)


def device_at(x, y, z, core):
    return (z // 4 * 4 + y) * 32 + (z % 4 * 4 + x) * 2 + core


def send(value, to):
    pairs = []
    for x in range(4):
        for y in range(4):
            for z in range(8):
                for core in range(2):
                    tx, ty, tz, tcore = to(x, y, z, core)
                    pairs.append((device_at(x, y, z, core), device_at(tx % 4, ty % 4, tz % 8, tcore)))
    return lax.ppermute(value, BOTH, sorted(pairs))


def along_x(value, step):
    return send(value, lambda x, y, z, core: (x + step, y, z, core))


def along_z(value, step):
    return send(value, lambda x, y, z, core: (x, y, z + step, core))


def other_core(value):
    return send(value, lambda x, y, z, core: (x, y, z, 1 - core))


def two_along_z(value):
    return send(value, lambda x, y, z, core: (x, y, z + (2 if core == 0 else -2), core))


def split_x(value):
    return send(value, lambda x, y, z, core: (x + (1 if core == 0 else -1), y, z, core))


def other_parity(value):
    return send(value, lambda x, y, z, core: (x, y + (1 if y % 2 == core else -1), z, core))


def params(mib):
    return pltpu.CompilerParams(vmem_limit_bytes=mib << 20)


def prologue_kernel(factors_in, pattern_in, coulomb_in, block_ref, whole_ref, own_ref, factors, pattern, coulomb, sems):
    copies = [
        pltpu.make_async_copy(factors_in, factors, sems.at[0]),
        pltpu.make_async_copy(pattern_in, pattern, sems.at[1]),
        pltpu.make_async_copy(coulomb_in, coulomb, sems.at[2]),
    ]
    for copy in copies:
        copy.start()
    for copy in copies:
        copy.wait()
    parity = lax.axis_index("tm") & 1
    rows, orb = factors.shape
    for block in range(orb // BLOCK):
        lanes = pl.ds(block * BLOCK, BLOCK)
        keep = pattern[:, block : block + 1].astype(F32)
        for half in range(2):
            at = parity if half == 0 else 1 - parity
            part = factors[pl.ds(pl.multiple_of(at * HALF, HALF), HALF), lanes]
            part = (part.astype(F32) * keep).astype(BF16)
            block_ref[pl.ds(half * HALF, HALF), lanes] = part
            if half == 0:
                whole_ref[pl.ds(0, HALF), lanes] = part
    c = coulomb[...]
    own = jnp.where(parity == 0, c, pltpu.roll(c, HALF, 1))
    own_ref[...] = own
    lane = lax.broadcasted_iota(jnp.int32, own.shape, 1)
    twice = jnp.where(lane < HALF, own, pltpu.roll(own, HALF, 1))
    for ref, row, value in ((block_ref, rows, own), (whole_ref, HALF, twice)):
        high = value.astype(BF16)
        rest = value - high.astype(F32)
        middle = rest.astype(BF16)
        low = (rest - middle.astype(F32)).astype(BF16)
        zero = jnp.zeros((1, orb - 3 * BLOCK), BF16)
        line = jnp.concatenate([high, middle, low, zero], axis=1)
        ref[pl.ds(row, 8), :] = jnp.broadcast_to(line.astype(F32), (8, orb)).astype(BF16)


def prologue(factors, pattern, coulomb):
    own, orb = factors.shape
    return pl.pallas_call(
        prologue_kernel,
        out_shape=[
            jax.ShapeDtypeStruct((own + 8, orb), BF16),
            jax.ShapeDtypeStruct((HALF + 8, orb), BF16),
            jax.ShapeDtypeStruct((1, own), F32),
        ],
        in_specs=[pl.BlockSpec(memory_space=pltpu.HBM)] * 3,
        out_specs=[VMEM] * 3,
        scratch_shapes=[
            pltpu.VMEM((own, orb), BF16),
            pltpu.VMEM(pattern.shape, jnp.int32),
            pltpu.VMEM((1, own), F32),
            pltpu.SemaphoreType.DMA((3,)),
        ],
        compiler_params=params(58),
    )(factors, pattern, coulomb[None, :])


def mix_kernel(west_o, east_o, west_p, east_p, onward_ref, both_ref):
    core = lax.axis_index("aux") & 1
    n, m = west_o.shape[0], west_p.shape[0]
    west, east = west_p[...], east_p[...]
    onward_ref[pl.ds(0, n), :] = jnp.where(core == 0, west_o[...], east_o[...])
    onward_ref[pl.ds(n, m), :] = jnp.where(core == 0, west, east)
    both_ref[pl.ds(0, m), :] = west
    both_ref[pl.ds(m, m), :] = east


def mix(west_o, east_o, west_p, east_p):
    n, orb = west_p.shape
    sizes = (west_o.shape[0] + n, 2 * n)
    return pl.pallas_call(
        mix_kernel,
        out_shape=[jax.ShapeDtypeStruct((size, orb), BF16) for size in sizes],
        in_specs=[VMEM] * 4,
        out_specs=[VMEM] * 2,
        compiler_params=params(8),
    )(west_o, east_o, west_p, east_p)


def weight_of(ref, row):
    parts = [ref[pl.ds(row, 1), pl.ds(k * BLOCK, BLOCK)].astype(F32) for k in range(3)]
    return parts[0] + (parts[1] + parts[2])


def column_of(refs, column):
    o, p, p_start, q, q_start = column
    third = 3 * HALF
    lane = lax.broadcasted_iota(jnp.int32, (1, BLOCK), 1)
    rows = [refs[o][pl.ds(0, BLOCK), :], refs[p][pl.ds(p_start, third), :], refs[q][pl.ds(q_start, third), :]]
    p_lines = [weight_of(refs[p], p_start + third + k) for k in range(3)]
    q_lines = [weight_of(refs[q], q_start + third + k) for k in range(3)]
    lines = p_lines + q_lines
    pairs = [jnp.where(lane < HALF, lines[k], lines[k + 1]) for k in range(0, 6, 2)]
    return jnp.concatenate(rows, axis=0), jnp.concatenate([weight_of(refs[o], BLOCK)] + pairs, axis=1)


def square_kernel(columns, *refs):
    right_own, right_other = refs[:2]
    rows = refs[2 : len(refs) - len(columns)]
    outs = refs[len(refs) - len(columns) :]
    for column, out in zip(columns, outs):
        for t in range(right_own.shape[0]):
            right = jnp.concatenate([right_own[t], right_other[t]], axis=0)
            part, weight = column_of(rows, column)
            a = lax.dot_general(right, part, NT, preferred_element_type=F32)
            out[t] = a * a * weight


def squares(right, right_other, rows, columns):
    times, own, orb = right.shape
    shape = jax.ShapeDtypeStruct((times, 2 * own, COLUMN), F32)
    flops = len(columns) * times * 2 * (2 * own) * COLUMN * orb
    return pl.pallas_call(
        functools.partial(square_kernel, tuple(columns)),
        out_shape=[shape] * len(columns),
        in_specs=[VMEM] * (2 + len(rows)),
        out_specs=[VMEM] * len(columns),
        compiler_params=params(12),
        cost_estimate=pl.CostEstimate(flops=flops, bytes_accessed=2 << 20, transcendentals=0),
    )(right, right_other, *rows)


def chunk_kernel(columns, sides, count, first, *refs):
    left_own, left_other = refs[sides - 2 : sides]
    rows = refs[sides : sides + count]
    rest = refs[sides + count :]
    given = () if sides == 4 else rest[: len(columns)]
    rest = rest[len(given) :]
    if not first:
        acc_own, acc_other = rest[:2]
        rest = rest[2:]
    out_own, out_other = rest
    own = out_own.shape[1]
    for t in range(out_own.shape[0]):
        left = jnp.concatenate([left_own[t], left_other[t]], axis=0)
        total = None
        for at, column in enumerate(columns):
            part, weight = column_of(rows, column)
            if given:
                square = given[at][t]
            else:
                right = jnp.concatenate([refs[0][t], refs[1][t]], axis=0)
                a = lax.dot_general(right, part, NT, preferred_element_type=F32)
                square = a * a * weight
            m = lax.dot_general(left, part, NT, preferred_element_type=F32)
            k = (square * m).astype(BF16)
            d = lax.dot_general(k, part, NN, preferred_element_type=F32)
            total = d if total is None else total + d
        mine, theirs = total[:own], total[own:]
        if not first:
            mine, theirs = acc_own[t] + mine, acc_other[t] + theirs
        out_own[t] = mine
        out_other[t] = theirs.astype(out_other.dtype)


def chunk(sides, rows, columns, given=(), acc=(), last=False):
    times, own, orb = sides[0].shape
    shape = jax.ShapeDtypeStruct((times, own, orb), F32)
    theirs = jax.ShapeDtypeStruct((times, own, orb), BF16 if last else F32)
    at = len(sides) + len(rows) + len(given)
    aliases = {}
    if acc:
        aliases[at] = 0
        if not last:
            aliases[at + 1] = 1
    flops = len(columns) * times * 2 * 2 * (2 * own) * COLUMN * orb
    return pl.pallas_call(
        functools.partial(chunk_kernel, tuple(columns), len(sides), len(rows), not acc),
        out_shape=(shape, theirs),
        in_specs=[VMEM] * (at + len(acc)),
        out_specs=(VMEM, VMEM),
        input_output_aliases=aliases,
        compiler_params=params(16),
        cost_estimate=pl.CostEstimate(flops=flops, bytes_accessed=2 << 20, transcendentals=0),
    )(*sides, *rows, *given, *acc)


def finish_kernel(own_ref, got_ref, coulomb_ref, out_ref):
    chips, times, rows, _ = out_ref.shape
    for t in range(times):
        d = jnp.transpose(own_ref[t] + got_ref[t].astype(F32)) * coulomb_ref[...]
        d = d.astype(BF16)
        for chip in range(chips):
            out_ref[chip, t] = d[chip * rows : (chip + 1) * rows]


def sigma_kernel(part_ref, *refs):
    blocks, q_parts = refs[:4], (refs[7], refs[8], refs[8], refs[9])
    p_parts = refs[4:7] + (refs[3],)
    keep_ref, send_ref, lhs, total_ref = refs[10:]
    chips, times, i_rows, width = part_ref.shape
    me = lax.axis_index("aux")
    core, x, z = me & 1, (me >> 1) & 3, me >> 3
    total = None
    for column, dx in enumerate((0, 3, 1, 2)):
        q_start = p_parts[2].shape[0] if column == 2 else 0
        p_start = BLOCK + 8 if column == 3 else 0
        parts = [blocks[column][pl.ds(0, BLOCK), :]]
        for k, dz in enumerate((0, 3, 1, 2)):
            source = ((z + dz) & 3) * 4 + ((x + dx) & 3)
            for t in range(times):
                at = pl.ds((column * 4 + k) * width, width)
                lhs[pl.ds(t * i_rows, i_rows), at] = part_ref[source, t]
            if k > 0:
                parts.append(p_parts[column][pl.ds(p_start + (k - 1) * HALF, HALF), :])
                parts.append(q_parts[column][pl.ds(q_start + (k - 1) * HALF, HALF), :])
        d = lax.dot_general(
            lhs[:, pl.ds(column * 4 * width, 4 * width)],
            jnp.concatenate(parts, axis=0),
            NN,
            preferred_element_type=F32,
        )
        total = d if total is None else total + d
    total_ref[...] = total
    half = i_rows // 2
    for t in range(times):
        keep = pl.multiple_of(t * i_rows + core * half, half)
        send = pl.multiple_of(t * i_rows + (1 - core) * half, half)
        keep_ref[t] = total_ref[pl.ds(keep, half), :]
        send_ref[t] = total_ref[pl.ds(send, half), :]


def add_kernel(keep_ref, got_ref, out_ref):
    for t in range(keep_ref.shape[0]):
        out_ref[:, t, :] = keep_ref[t] + got_ref[t]


def local(green, factors, pattern, coulomb):
    times, orb, _ = green.shape
    own = factors.shape[0]
    barrier = lax.optimization_barrier
    block, whole, coulomb = prologue(factors, pattern, coulomb)
    masked = block[:own]

    beyond = two_along_z(whole)
    below = along_z(whole, 1)
    above = along_z(whole, -1)
    left = jnp.einsum("qo,tok->tqk", masked, green, preferred_element_type=F32).astype(BF16)
    below, left = barrier((below, left))
    left = two_along_z(left)
    west_o = along_x(block, 1)
    east_o = along_x(block, -1)

    near = [below, above, beyond]
    lines = [part[HALF : HALF + 1] for part in near] + [jnp.zeros((5, orb), BF16)]
    here_p = jnp.concatenate([part[:HALF] for part in near] + lines, axis=0)
    here_p, west_o, east_o = barrier((here_p, west_o, east_o))
    west_p = along_x(here_p, 1)
    east_p = along_x(here_p, -1)
    here_q = other_parity(here_p)
    left = two_along_z(left)
    here_q, masked = barrier((here_q, masked))
    right = jnp.einsum("qo,tko->tqk", masked, green, preferred_element_type=F32).astype(BF16)
    right_other = other_core(right)

    west_p, east_p, here_q = barrier((west_p, east_p, here_q))
    onward, both = mix(west_o, east_o, west_p, east_p)
    far = split_x(onward)
    sides_q = other_parity(both)
    (here_z,) = squares(right, right_other, (block, here_p, here_q), [(0, 1, 0, 2, 0)])
    far_q = other_parity(far[own + 8 :])
    left_other = other_core(left)

    skip = west_p.shape[0]
    pair = (west_o, west_p, east_o, east_p, sides_q)
    columns = [(0, 1, 0, 4, 0), (2, 3, 0, 4, skip)]
    pair_z = squares(right, right_other, pair, columns)
    lefts = (left, left_other)
    acc = chunk(lefts, pair, columns, given=pair_z)
    acc = chunk(lefts, (block, here_p, here_q), [(0, 1, 0, 2, 0)], given=(here_z,), acc=acc)
    sides = (right, right_other, left, left_other)
    keep, theirs = chunk(sides, (far, far_q), [(0, 0, own + 8, 1, 0)], acc=acc, last=True)

    got = other_core(theirs)
    chips, i_rows = 16, orb // 16
    part = pl.pallas_call(
        finish_kernel,
        out_shape=jax.ShapeDtypeStruct((chips, times, i_rows, own), BF16),
        in_specs=[VMEM] * 3,
        out_specs=VMEM,
        compiler_params=params(12),
    )(keep, got, coulomb)
    groups = [[2 * chip + core for chip in range(chips)] for core in range(2)]
    part = lax.all_to_all(part, "aux", 0, 0, axis_index_groups=groups, tiled=True)

    shape = jax.ShapeDtypeStruct((times, i_rows // 2, orb), F32)
    keep, theirs = pl.pallas_call(
        sigma_kernel,
        out_shape=(shape, shape),
        in_specs=[VMEM] * 11,
        out_specs=(VMEM, VMEM),
        scratch_shapes=[
            pltpu.VMEM((times * i_rows, chips * own), BF16),
            pltpu.VMEM((times * i_rows, orb), F32),
        ],
        compiler_params=params(12),
    )(part, block, west_o, east_o, far, here_p, west_p, east_p, here_q, sides_q, far_q)
    got = other_core(theirs)
    return pl.pallas_call(
        add_kernel,
        out_shape=jax.ShapeDtypeStruct((i_rows // 2, times, orb), F32),
        in_specs=[VMEM] * 2,
        out_specs=VMEM,
        compiler_params=params(8),
    )(keep, got)


def solution(mesh):
    in_specs = (P("tm", None, None), P("aux", None), P("aux", None), P("aux"))
    out_specs = P("aux", "tm", None)
    return jax.shard_map(local, mesh=mesh, in_specs=in_specs, out_specs=out_specs, check_vma=False)
```

```python
import functools

import jax
import jax.numpy as jnp
from jax import lax
from jax.experimental import pallas as pl
from jax.experimental.pallas import tpu as pltpu
from jax.sharding import PartitionSpec as P

BLOCK = 128
HALF = 64
F32, BF16 = jnp.float32, jnp.bfloat16
BOTH = ("tm", "aux")
NT = (((1,), (1,)), ((), ()))
NN = (((1,), (0,)), ((), ()))
VMEM = pl.BlockSpec(memory_space=pltpu.VMEM)


def device_at(x, y, z, core):
    return (z // 4 * 4 + y) * 32 + (z % 4 * 4 + x) * 2 + core


def send(value, to):
    pairs = []
    for x in range(4):
        for y in range(4):
            for z in range(8):
                for core in range(2):
                    tx, ty, tz, tcore = to(x, y, z, core)
                    pairs.append((device_at(x, y, z, core), device_at(tx % 4, ty % 4, tz % 8, tcore)))
    return lax.ppermute(value, BOTH, sorted(pairs))


def along_x(value, step):
    return send(value, lambda x, y, z, core: (x + step, y, z, core))


def along_z(value, step):
    return send(value, lambda x, y, z, core: (x, y, z + step, core))


def other_core(value):
    return send(value, lambda x, y, z, core: (x, y, z, 1 - core))


def two_along_z(value):
    return send(value, lambda x, y, z, core: (x, y, z + (2 if core == 0 else -2), core))


def split_x(value):
    return send(value, lambda x, y, z, core: (x + (1 if core == 0 else -1), y, z, core))


def other_parity(value):
    return send(value, lambda x, y, z, core: (x, y + (1 if y % 2 == core else -1), z, core))


def params(mib):
    return pltpu.CompilerParams(vmem_limit_bytes=mib << 20)


def prologue_kernel(factors_in, pattern_in, coulomb_in, masked_ref, whole_ref, own_ref, factors, pattern, coulomb, sems):
    copies = [
        pltpu.make_async_copy(factors_in, factors, sems.at[0]),
        pltpu.make_async_copy(pattern_in, pattern, sems.at[1]),
        pltpu.make_async_copy(coulomb_in, coulomb, sems.at[2]),
    ]
    for copy in copies:
        copy.start()
    for copy in copies:
        copy.wait()
    parity = lax.axis_index("tm") & 1
    orb = factors.shape[1]
    for block in range(orb // BLOCK):
        lanes = pl.ds(block * BLOCK, BLOCK)
        keep = pattern[:, block : block + 1].astype(F32)
        for half in range(2):
            at = parity if half == 0 else 1 - parity
            part = factors[pl.ds(pl.multiple_of(at * HALF, HALF), HALF), lanes]
            part = (part.astype(F32) * keep).astype(BF16)
            masked_ref[pl.ds(half * HALF, HALF), lanes] = part
            if half == 0:
                whole_ref[pl.ds(0, HALF), lanes] = part
    c = coulomb[...]
    turned = pltpu.roll(c, HALF, 1)
    own = jnp.where(parity == 0, c, turned)
    own_ref[...] = own
    lane = lax.broadcasted_iota(jnp.int32, own.shape, 1)
    twice = jnp.where(lane < HALF, own, pltpu.roll(own, HALF, 1))
    high = twice.astype(BF16)
    rest = twice - high.astype(F32)
    middle = rest.astype(BF16)
    low = (rest - middle.astype(F32)).astype(BF16)
    zero = jnp.zeros((1, orb - 3 * BLOCK), BF16)
    row = jnp.concatenate([high, middle, low, zero], axis=1)
    rows = jnp.broadcast_to(row.astype(F32), (8, orb)).astype(BF16)
    whole_ref[pl.ds(HALF, 8), :] = rows


def prologue(factors, pattern, coulomb):
    own, orb = factors.shape
    return pl.pallas_call(
        prologue_kernel,
        out_shape=[
            jax.ShapeDtypeStruct((own, orb), BF16),
            jax.ShapeDtypeStruct((HALF + 8, orb), BF16),
            jax.ShapeDtypeStruct((1, own), F32),
        ],
        in_specs=[pl.BlockSpec(memory_space=pltpu.HBM)] * 3,
        out_specs=[VMEM] * 3,
        scratch_shapes=[
            pltpu.VMEM((own, orb), BF16),
            pltpu.VMEM(pattern.shape, jnp.int32),
            pltpu.VMEM((1, own), F32),
            pltpu.SemaphoreType.DMA((3,)),
        ],
        compiler_params=params(58),
    )(factors, pattern, coulomb[None, :])


def mix_kernel(west_ref, east_ref, onward_ref, both_ref):
    core = lax.axis_index("aux") & 1
    n = west_ref.shape[0]
    west, east = west_ref[...], east_ref[...]
    onward_ref[...] = jnp.where(core == 0, west, east)
    both_ref[pl.ds(0, n), :] = west
    both_ref[pl.ds(n, n), :] = east


def mix(west, east):
    n, orb = west.shape
    return pl.pallas_call(
        mix_kernel,
        out_shape=(jax.ShapeDtypeStruct((n, orb), BF16), jax.ShapeDtypeStruct((2 * n, orb), BF16)),
        in_specs=[VMEM] * 2,
        out_specs=[VMEM] * 2,
        compiler_params=params(8),
    )(west, east)


def after_kernel(value_ref, first_ref, out_ref):
    del first_ref
    pltpu.touch(value_ref)
    pltpu.touch(out_ref)


def after(value, first):
    return pl.pallas_call(
        after_kernel,
        out_shape=jax.ShapeDtypeStruct(value.shape, value.dtype),
        in_specs=[VMEM] * 2,
        out_specs=VMEM,
        input_output_aliases={0: 0},
        compiler_params=params(8),
    )(value, first)


def weight_of(ref, row):
    parts = [ref[pl.ds(row, 1), pl.ds(k * BLOCK, BLOCK)].astype(F32) for k in range(3)]
    return parts[0] + (parts[1] + parts[2])


def weights_of(ref, row, blocks):
    lane = lax.broadcasted_iota(jnp.int32, (1, BLOCK), 1)
    pairs = []
    for k in range(0, blocks, 2):
        pairs.append(jnp.where(lane < HALF, weight_of(ref, row + k), weight_of(ref, row + k + 1)))
    return jnp.concatenate(pairs, axis=1) if len(pairs) > 1 else pairs[0]


def rows_of(refs, piece):
    at, start, size = piece
    return refs[at][pl.ds(start, size), :], weights_of(refs[at], start + size, size // HALF)


def square_kernel(pieces, right_own, right_other, *refs):
    rows, out = refs[:-1], refs[-1]
    for t in range(right_own.shape[0]):
        right = jnp.concatenate([right_own[t], right_other[t]], axis=0)
        offset = 0
        for piece in pieces:
            part, weight = rows_of(rows, piece)
            a = lax.dot_general(right, part, NT, preferred_element_type=F32)
            out[t, :, pl.ds(offset, piece[2])] = a * a * weight
            offset += piece[2]


def squares(right, right_other, rows, pieces):
    times, own, orb = right.shape
    n = sum(piece[2] for piece in pieces)
    return pl.pallas_call(
        functools.partial(square_kernel, tuple(pieces)),
        out_shape=jax.ShapeDtypeStruct((times, 2 * own, n), F32),
        in_specs=[VMEM] * (2 + len(rows)),
        out_specs=VMEM,
        compiler_params=params(12),
        cost_estimate=pl.CostEstimate(
            flops=times * 2 * (2 * own) * n * orb, bytes_accessed=2 << 20, transcendentals=0
        ),
    )(right, right_other, *rows)


def chunk_kernel(pieces, sides, count, given, first, *refs):
    left_own, left_other = refs[sides - 2 : sides]
    rows = refs[sides : sides + count]
    rest = refs[sides + count :]
    if given:
        squared = rest[0]
        rest = rest[1:]
    if not first:
        acc_own, acc_other = rest[:2]
        rest = rest[2:]
    out_own, out_other = rest
    own = out_own.shape[1]
    for t in range(out_own.shape[0]):
        left = jnp.concatenate([left_own[t], left_other[t]], axis=0)
        total = None
        offset = 0
        for piece in pieces:
            part, weight = rows_of(rows, piece)
            if given:
                square = squared[t, :, pl.ds(offset, piece[2])]
            else:
                right = jnp.concatenate([refs[0][t], refs[1][t]], axis=0)
                a = lax.dot_general(right, part, NT, preferred_element_type=F32)
                square = a * a * weight
            offset += piece[2]
            m = lax.dot_general(left, part, NT, preferred_element_type=F32)
            k = (square * m).astype(BF16)
            d = lax.dot_general(k, part, NN, preferred_element_type=F32)
            total = d if total is None else total + d
        mine, theirs = total[:own], total[own:]
        if not first:
            mine, theirs = acc_own[t] + mine, acc_other[t] + theirs
        out_own[t] = mine
        out_other[t] = theirs.astype(out_other.dtype)


def chunk(sides, rows, pieces, given=(), acc=(), last=False):
    times, own, orb = sides[0].shape
    shape = jax.ShapeDtypeStruct((times, own, orb), F32)
    theirs = jax.ShapeDtypeStruct((times, own, orb), BF16 if last else F32)
    at = len(sides) + len(rows) + len(given)
    aliases = {}
    if acc:
        aliases[at] = 0
        if not last:
            aliases[at + 1] = 1
    n = sum(piece[2] for piece in pieces)
    flops = times * 2 * 2 * (2 * own) * n * orb
    return pl.pallas_call(
        functools.partial(
            chunk_kernel, tuple(pieces), len(sides), len(rows), bool(given), not acc
        ),
        out_shape=(shape, theirs),
        in_specs=[VMEM] * (at + len(acc)),
        out_specs=(VMEM, VMEM),
        input_output_aliases=aliases,
        compiler_params=params(16),
        cost_estimate=pl.CostEstimate(flops=flops, bytes_accessed=2 << 20, transcendentals=0),
    )(*sides, *rows, *given, *acc)


def finish_kernel(own_ref, got_ref, coulomb_ref, out_ref):
    chips, times, rows, _ = out_ref.shape
    for t in range(times):
        d = jnp.transpose(own_ref[t] + got_ref[t].astype(F32)) * coulomb_ref[...]
        d = d.astype(BF16)
        for chip in range(chips):
            out_ref[chip, t] = d[chip * rows : (chip + 1) * rows]


def sigma_kernel(part_ref, *refs):
    here, here_q, west, east, sides_q, far, far_q = refs[:7]
    keep_ref, send_ref, lhs, total_ref = refs[7:]
    skip = west.shape[0]
    columns = [((here, 0), (here_q, 0)), ((west, 0), (sides_q, 0)), ((east, 0), (sides_q, skip)), ((far, 0), (far_q, 0))]
    chips, times, i_rows, width = part_ref.shape
    me = lax.axis_index("aux")
    core, x, z = me & 1, (me >> 1) & 3, me >> 3
    total = None
    for column, dx in enumerate((0, 3, 1, 2)):
        parts = []
        for k, dz in enumerate((0, 3, 1, 2)):
            source = ((z + dz) & 3) * 4 + ((x + dx) & 3)
            for t in range(times):
                at = pl.ds((column * 4 + k) * width, width)
                lhs[pl.ds(t * i_rows, i_rows), at] = part_ref[source, t]
            for ref, start in columns[column]:
                parts.append(ref[pl.ds(start + k * HALF, HALF), :])
        d = lax.dot_general(
            lhs[:, pl.ds(column * 4 * width, 4 * width)],
            jnp.concatenate(parts, axis=0),
            NN,
            preferred_element_type=F32,
        )
        total = d if total is None else total + d
    total_ref[...] = total
    half = i_rows // 2
    for t in range(times):
        keep = pl.multiple_of(t * i_rows + core * half, half)
        send = pl.multiple_of(t * i_rows + (1 - core) * half, half)
        keep_ref[t] = total_ref[pl.ds(keep, half), :]
        send_ref[t] = total_ref[pl.ds(send, half), :]


def add_kernel(keep_ref, got_ref, out_ref):
    for t in range(keep_ref.shape[0]):
        out_ref[:, t, :] = keep_ref[t] + got_ref[t]


def local(green, factors, pattern, coulomb):
    times, orb, _ = green.shape
    own = factors.shape[0]
    barrier = lax.optimization_barrier
    masked, whole, coulomb = prologue(factors, pattern, coulomb)

    beyond = two_along_z(whole)
    below = along_z(whole, 1)
    above = along_z(whole, -1)
    left = jnp.einsum("qo,tok->tqk", masked, green, preferred_element_type=F32).astype(BF16)
    below, left = barrier((below, left))
    left = along_z(left, 4)

    blocks = [whole, below, above, beyond]
    weights = [block[HALF : HALF + 1] for block in blocks] + [jnp.zeros((4, orb), BF16)]
    here = barrier(jnp.concatenate([block[:HALF] for block in blocks] + weights, axis=0))

    n = 4 * HALF
    west = along_x(here, 1)
    east = along_x(here, -1)
    rest = other_parity(here[HALF:])
    here_q = jnp.concatenate([masked[HALF:], rest], axis=0)
    right = jnp.einsum("qo,tko->tqk", masked, green, preferred_element_type=F32).astype(BF16)
    west, east, right, here_q = barrier((west, east, right, here_q))
    right_other = other_core(right)
    onward, both = mix(west, east)
    far = split_x(onward)
    sides_q = other_parity(both)
    far_q = other_parity(far)
    left = after(left, onward)
    left_other = other_core(left)

    rights, lefts = (right, right_other), (left, left_other)
    two = [(0, 0, n), (1, 0, n)]
    here_z = squares(*rights, (here, here_q), two)
    sides_z = squares(*rights, (west, east), two)
    acc = chunk(lefts, (here, here_q), two, given=(here_z,))
    acc = chunk(lefts, (west, east), two, given=(sides_z,), acc=acc)
    sides = rights + lefts
    acc = chunk(sides, (sides_q, far), [(0, 0, n), (0, n + 8, n), (1, 0, n)], acc=acc)
    keep, theirs = chunk(sides, (far_q,), [(0, 0, n)], acc=acc, last=True)

    got = other_core(theirs)
    chips, i_rows = 16, orb // 16
    part = pl.pallas_call(
        finish_kernel,
        out_shape=jax.ShapeDtypeStruct((chips, times, i_rows, own), BF16),
        in_specs=[VMEM] * 3,
        out_specs=VMEM,
        compiler_params=params(12),
    )(keep, got, coulomb)
    groups = [[2 * chip + core for chip in range(chips)] for core in range(2)]
    part = lax.all_to_all(part, "aux", 0, 0, axis_index_groups=groups, tiled=True)

    shape = jax.ShapeDtypeStruct((times, i_rows // 2, orb), F32)
    keep, theirs = pl.pallas_call(
        sigma_kernel,
        out_shape=(shape, shape),
        in_specs=[VMEM] * 8,
        out_specs=(VMEM, VMEM),
        scratch_shapes=[
            pltpu.VMEM((times * i_rows, chips * own), BF16),
            pltpu.VMEM((times * i_rows, orb), F32),
        ],
        compiler_params=params(12),
    )(part, here, here_q, west, east, sides_q, far, far_q)
    got = other_core(theirs)
    return pl.pallas_call(
        add_kernel,
        out_shape=jax.ShapeDtypeStruct((i_rows // 2, times, orb), F32),
        in_specs=[VMEM] * 2,
        out_specs=VMEM,
        compiler_params=params(8),
    )(keep, got)


def solution(mesh):
    in_specs = (P("tm", None, None), P("aux", None), P("aux", None), P("aux"))
    out_specs = P("aux", "tm", None)
    return jax.shard_map(local, mesh=mesh, in_specs=in_specs, out_specs=out_specs, check_vma=False)
```

```python
import functools

import jax
import jax.numpy as jnp
from jax import lax
from jax.experimental import pallas as pl
from jax.experimental.pallas import tpu as pltpu
from jax.sharding import PartitionSpec as P

BLOCK = 128
HALF = 64
F32, BF16 = jnp.float32, jnp.bfloat16
BOTH = ("tm", "aux")
NT = (((1,), (1,)), ((), ()))
NN = (((1,), (0,)), ((), ()))
VMEM = pl.BlockSpec(memory_space=pltpu.VMEM)


def device_at(x, y, z, core):
    return (z // 4 * 4 + y) * 32 + (z % 4 * 4 + x) * 2 + core


def send(value, to):
    pairs = []
    for x in range(4):
        for y in range(4):
            for z in range(8):
                for core in range(2):
                    tx, ty, tz, tcore = to(x, y, z, core)
                    pairs.append((device_at(x, y, z, core), device_at(tx % 4, ty % 4, tz % 8, tcore)))
    return lax.ppermute(value, BOTH, sorted(pairs))


def along_x(value, step):
    return send(value, lambda x, y, z, core: (x + step, y, z, core))


def along_z(value, step):
    return send(value, lambda x, y, z, core: (x, y, z + step, core))


def other_core(value):
    return send(value, lambda x, y, z, core: (x, y, z, 1 - core))


def two_along_z(value):
    return send(value, lambda x, y, z, core: (x, y, z + (2 if core == 0 else -2), core))


def split_x(value):
    return send(value, lambda x, y, z, core: (x + (1 if core == 0 else -1), y, z, core))


def other_parity(value):
    return send(value, lambda x, y, z, core: (x, y + (1 if y % 2 == core else -1), z, core))


def params(mib):
    return pltpu.CompilerParams(vmem_limit_bytes=mib << 20)


def prologue_kernel(
    factors_in, pattern_in, coulomb_in, green_in, masked_ref, whole_ref, own_ref, left_ref,
    factors, pattern, coulomb, green, sems,
):
    copies = [
        pltpu.make_async_copy(factors_in, factors, sems.at[0]),
        pltpu.make_async_copy(pattern_in, pattern, sems.at[1]),
        pltpu.make_async_copy(coulomb_in, coulomb, sems.at[2]),
    ]
    greens = [
        pltpu.make_async_copy(green_in.at[t], green.at[t], sems.at[3 + t])
        for t in range(green_in.shape[0])
    ]
    for copy in copies + greens:
        copy.start()
    for copy in copies:
        copy.wait()
    parity = lax.axis_index("tm") & 1
    orb = factors.shape[1]
    for block in range(orb // BLOCK):
        lanes = pl.ds(block * BLOCK, BLOCK)
        keep = pattern[:, block : block + 1].astype(F32)
        for half in range(2):
            at = parity if half == 0 else 1 - parity
            part = factors[pl.ds(pl.multiple_of(at * HALF, HALF), HALF), lanes]
            part = (part.astype(F32) * keep).astype(BF16)
            masked_ref[pl.ds(half * HALF, HALF), lanes] = part
            if half == 0:
                whole_ref[pl.ds(0, HALF), lanes] = part
    c = coulomb[...]
    turned = pltpu.roll(c, HALF, 1)
    own = jnp.where(parity == 0, c, turned)
    own_ref[...] = own
    lane = lax.broadcasted_iota(jnp.int32, own.shape, 1)
    twice = jnp.where(lane < HALF, own, pltpu.roll(own, HALF, 1))
    high = twice.astype(BF16)
    rest = twice - high.astype(F32)
    middle = rest.astype(BF16)
    low = (rest - middle.astype(F32)).astype(BF16)
    zero = jnp.zeros((1, orb - 3 * BLOCK), BF16)
    row = jnp.concatenate([high, middle, low, zero], axis=1)
    rows = jnp.broadcast_to(row.astype(F32), (8, orb)).astype(BF16)
    whole_ref[pl.ds(HALF, 8), :] = rows
    for t, copy in enumerate(greens):
        copy.wait()
        left_ref[t] = lax.dot_general(
            masked_ref[...], green[t], NN, preferred_element_type=F32
        ).astype(BF16)


def prologue(factors, pattern, coulomb, green):
    own, orb = factors.shape
    return pl.pallas_call(
        prologue_kernel,
        out_shape=[
            jax.ShapeDtypeStruct((own, orb), BF16),
            jax.ShapeDtypeStruct((HALF + 8, orb), BF16),
            jax.ShapeDtypeStruct((1, own), F32),
            jax.ShapeDtypeStruct((green.shape[0], own, orb), BF16),
        ],
        in_specs=[pl.BlockSpec(memory_space=pltpu.HBM)] * 4,
        out_specs=[VMEM] * 4,
        scratch_shapes=[
            pltpu.VMEM((own, orb), BF16),
            pltpu.VMEM(pattern.shape, jnp.int32),
            pltpu.VMEM((1, own), F32),
            pltpu.VMEM(green.shape, BF16),
            pltpu.SemaphoreType.DMA((3 + green.shape[0],)),
        ],
        compiler_params=params(16),
    )(*[pltpu.with_memory_space_constraint(v, pltpu.HBM) for v in (factors, pattern, coulomb[None, :], green)])


def mix_kernel(west_ref, east_ref, onward_ref, both_ref):
    core = lax.axis_index("aux") & 1
    n = west_ref.shape[0]
    west, east = west_ref[...], east_ref[...]
    onward_ref[...] = jnp.where(core == 0, west, east)
    both_ref[pl.ds(0, n), :] = west
    both_ref[pl.ds(n, n), :] = east


def mix(west, east):
    n, orb = west.shape
    return pl.pallas_call(
        mix_kernel,
        out_shape=(jax.ShapeDtypeStruct((n, orb), BF16), jax.ShapeDtypeStruct((2 * n, orb), BF16)),
        in_specs=[VMEM] * 2,
        out_specs=[VMEM] * 2,
        compiler_params=params(8),
    )(west, east)


def after_kernel(value_ref, first_ref, out_ref):
    del first_ref
    pltpu.touch(value_ref)
    pltpu.touch(out_ref)


def after(value, first):
    return pl.pallas_call(
        after_kernel,
        out_shape=jax.ShapeDtypeStruct(value.shape, value.dtype),
        in_specs=[VMEM] * 2,
        out_specs=VMEM,
        input_output_aliases={0: 0},
        compiler_params=params(8),
    )(value, first)


def weight_of(ref, row):
    parts = [ref[pl.ds(row, 1), pl.ds(k * BLOCK, BLOCK)].astype(F32) for k in range(3)]
    return parts[0] + (parts[1] + parts[2])


def weights_of(ref, row, blocks):
    lane = lax.broadcasted_iota(jnp.int32, (1, BLOCK), 1)
    pairs = []
    for k in range(0, blocks, 2):
        pairs.append(jnp.where(lane < HALF, weight_of(ref, row + k), weight_of(ref, row + k + 1)))
    return jnp.concatenate(pairs, axis=1) if len(pairs) > 1 else pairs[0]


def rows_of(refs, piece):
    at, start, size = piece
    return refs[at][pl.ds(start, size), :], weights_of(refs[at], start + size, size // HALF)


def square_kernel(pieces, right_own, right_other, *refs):
    rows, out = refs[:-1], refs[-1]
    for t in range(right_own.shape[0]):
        right = jnp.concatenate([right_own[t], right_other[t]], axis=0)
        offset = 0
        for piece in pieces:
            part, weight = rows_of(rows, piece)
            a = lax.dot_general(right, part, NT, preferred_element_type=F32)
            out[t, :, pl.ds(offset, piece[2])] = a * a * weight
            offset += piece[2]


def squares(right, right_other, rows, pieces):
    times, own, orb = right.shape
    n = sum(piece[2] for piece in pieces)
    return pl.pallas_call(
        functools.partial(square_kernel, tuple(pieces)),
        out_shape=jax.ShapeDtypeStruct((times, 2 * own, n), F32),
        in_specs=[VMEM] * (2 + len(rows)),
        out_specs=VMEM,
        compiler_params=params(12),
        cost_estimate=pl.CostEstimate(
            flops=times * 2 * (2 * own) * n * orb, bytes_accessed=2 << 20, transcendentals=0
        ),
    )(right, right_other, *rows)


def chunk_kernel(pieces, sides, count, given, first, *refs):
    left_own, left_other = refs[sides - 2 : sides]
    rows = refs[sides : sides + count]
    rest = refs[sides + count :]
    if given:
        squared = rest[0]
        rest = rest[1:]
    if not first:
        acc_own, acc_other = rest[:2]
        rest = rest[2:]
    out_own, out_other = rest
    own = out_own.shape[1]
    for t in range(out_own.shape[0]):
        left = jnp.concatenate([left_own[t], left_other[t]], axis=0)
        total = None
        offset = 0
        for piece in pieces:
            part, weight = rows_of(rows, piece)
            if given:
                square = squared[t, :, pl.ds(offset, piece[2])]
            else:
                right = jnp.concatenate([refs[0][t], refs[1][t]], axis=0)
                a = lax.dot_general(right, part, NT, preferred_element_type=F32)
                square = a * a * weight
            offset += piece[2]
            m = lax.dot_general(left, part, NT, preferred_element_type=F32)
            k = (square * m).astype(BF16)
            d = lax.dot_general(k, part, NN, preferred_element_type=F32)
            total = d if total is None else total + d
        mine, theirs = total[:own], total[own:]
        if not first:
            mine, theirs = acc_own[t] + mine, acc_other[t] + theirs
        out_own[t] = mine
        out_other[t] = theirs.astype(out_other.dtype)


def chunk(sides, rows, pieces, given=(), acc=(), last=False):
    times, own, orb = sides[0].shape
    shape = jax.ShapeDtypeStruct((times, own, orb), F32)
    theirs = jax.ShapeDtypeStruct((times, own, orb), BF16 if last else F32)
    at = len(sides) + len(rows) + len(given)
    aliases = {}
    if acc:
        aliases[at] = 0
        if not last:
            aliases[at + 1] = 1
    n = sum(piece[2] for piece in pieces)
    flops = times * 2 * 2 * (2 * own) * n * orb
    return pl.pallas_call(
        functools.partial(
            chunk_kernel, tuple(pieces), len(sides), len(rows), bool(given), not acc
        ),
        out_shape=(shape, theirs),
        in_specs=[VMEM] * (at + len(acc)),
        out_specs=(VMEM, VMEM),
        input_output_aliases=aliases,
        compiler_params=params(16),
        cost_estimate=pl.CostEstimate(flops=flops, bytes_accessed=2 << 20, transcendentals=0),
    )(*sides, *rows, *given, *acc)


def finish_kernel(own_ref, got_ref, coulomb_ref, out_ref):
    chips, times, rows, _ = out_ref.shape
    for t in range(times):
        d = jnp.transpose(own_ref[t] + got_ref[t].astype(F32)) * coulomb_ref[...]
        d = d.astype(BF16)
        for chip in range(chips):
            out_ref[chip, t] = d[chip * rows : (chip + 1) * rows]


def sigma_kernel(part_ref, *refs):
    here, here_q, west, east, sides_q, far, far_q = refs[:7]
    keep_ref, send_ref, lhs, total_ref = refs[7:]
    skip = west.shape[0]
    columns = [((here, 0), (here_q, 0)), ((west, 0), (sides_q, 0)), ((east, 0), (sides_q, skip)), ((far, 0), (far_q, 0))]
    chips, times, i_rows, width = part_ref.shape
    me = lax.axis_index("aux")
    core, x, z = me & 1, (me >> 1) & 3, me >> 3
    total = None
    for column, dx in enumerate((0, 3, 1, 2)):
        parts = []
        for k, dz in enumerate((0, 3, 1, 2)):
            source = ((z + dz) & 3) * 4 + ((x + dx) & 3)
            for t in range(times):
                at = pl.ds((column * 4 + k) * width, width)
                lhs[pl.ds(t * i_rows, i_rows), at] = part_ref[source, t]
            for ref, start in columns[column]:
                parts.append(ref[pl.ds(start + k * HALF, HALF), :])
        d = lax.dot_general(
            lhs[:, pl.ds(column * 4 * width, 4 * width)],
            jnp.concatenate(parts, axis=0),
            NN,
            preferred_element_type=F32,
        )
        total = d if total is None else total + d
    total_ref[...] = total
    half = i_rows // 2
    for t in range(times):
        keep = pl.multiple_of(t * i_rows + core * half, half)
        send = pl.multiple_of(t * i_rows + (1 - core) * half, half)
        keep_ref[t] = total_ref[pl.ds(keep, half), :]
        send_ref[t] = total_ref[pl.ds(send, half), :]


def add_kernel(keep_ref, got_ref, out_ref):
    for t in range(keep_ref.shape[0]):
        out_ref[:, t, :] = keep_ref[t] + got_ref[t]


def local(green, factors, pattern, coulomb):
    times, orb, _ = green.shape
    own = factors.shape[0]
    barrier = lax.optimization_barrier
    masked, whole, coulomb, left = prologue(factors, pattern, coulomb, green)

    beyond = two_along_z(whole)
    below = along_z(whole, 1)
    above = along_z(whole, -1)
    left = two_along_z(left)

    blocks = [whole, below, above, beyond]
    weights = [block[HALF : HALF + 1] for block in blocks] + [jnp.zeros((4, orb), BF16)]
    here = barrier(jnp.concatenate([block[:HALF] for block in blocks] + weights, axis=0))

    n = 4 * HALF
    west = along_x(here, 1)
    east = along_x(here, -1)
    rest = other_parity(here[HALF:])
    here_q = jnp.concatenate([masked[HALF:], rest], axis=0)
    right = jnp.einsum("qo,tko->tqk", masked, green, preferred_element_type=F32).astype(BF16)
    west, east, right, here_q = barrier((west, east, right, here_q))
    right_other = other_core(right)
    onward, both = mix(west, east)
    far = split_x(onward)
    sides_q = other_parity(both)
    far_q = other_parity(far)
    left = two_along_z(left)
    left_other = other_core(left)

    rights, lefts = (right, right_other), (left, left_other)
    two = [(0, 0, n), (1, 0, n)]
    here_z = squares(*rights, (here, here_q), two)
    sides_z = squares(*rights, (west, east), two)
    acc = chunk(lefts, (here, here_q), two, given=(here_z,))
    acc = chunk(lefts, (west, east), two, given=(sides_z,), acc=acc)
    sides = rights + lefts
    acc = chunk(sides, (sides_q, far), [(0, 0, n), (0, n + 8, n), (1, 0, n)], acc=acc)
    keep, theirs = chunk(sides, (far_q,), [(0, 0, n)], acc=acc, last=True)

    got = other_core(theirs)
    chips, i_rows = 16, orb // 16
    part = pl.pallas_call(
        finish_kernel,
        out_shape=jax.ShapeDtypeStruct((chips, times, i_rows, own), BF16),
        in_specs=[VMEM] * 3,
        out_specs=VMEM,
        compiler_params=params(12),
    )(keep, got, coulomb)
    groups = [[2 * chip + core for chip in range(chips)] for core in range(2)]
    part = lax.all_to_all(part, "aux", 0, 0, axis_index_groups=groups, tiled=True)

    shape = jax.ShapeDtypeStruct((times, i_rows // 2, orb), F32)
    keep, theirs = pl.pallas_call(
        sigma_kernel,
        out_shape=(shape, shape),
        in_specs=[VMEM] * 8,
        out_specs=(VMEM, VMEM),
        scratch_shapes=[
            pltpu.VMEM((times * i_rows, chips * own), BF16),
            pltpu.VMEM((times * i_rows, orb), F32),
        ],
        compiler_params=params(12),
    )(part, here, here_q, west, east, sides_q, far, far_q)
    got = other_core(theirs)
    return pl.pallas_call(
        add_kernel,
        out_shape=jax.ShapeDtypeStruct((i_rows // 2, times, orb), F32),
        in_specs=[VMEM] * 2,
        out_specs=VMEM,
        compiler_params=params(8),
    )(keep, got)


def solution(mesh):
    in_specs = (P("tm", None, None), P("aux", None), P("aux", None), P("aux"))
    out_specs = P("aux", "tm", None)
    return jax.shard_map(local, mesh=mesh, in_specs=in_specs, out_specs=out_specs, check_vma=False)
```

```python
import functools

import jax
import jax.numpy as jnp
from jax import lax
from jax.experimental import pallas as pl
from jax.experimental.pallas import tpu as pltpu
from jax.sharding import PartitionSpec as P

BLOCK = 128
HALF = 64
F32, BF16 = jnp.float32, jnp.bfloat16
BOTH = ("tm", "aux")
NT = (((1,), (1,)), ((), ()))
NN = (((1,), (0,)), ((), ()))
VMEM = pl.BlockSpec(memory_space=pltpu.VMEM)


def device_at(x, y, z, core):
    return (z // 4 * 4 + y) * 32 + (z % 4 * 4 + x) * 2 + core


def send(value, to):
    pairs = []
    for x in range(4):
        for y in range(4):
            for z in range(8):
                for core in range(2):
                    tx, ty, tz, tcore = to(x, y, z, core)
                    pairs.append((device_at(x, y, z, core), device_at(tx % 4, ty % 4, tz % 8, tcore)))
    return lax.ppermute(value, BOTH, sorted(pairs))


def along_x(value, step):
    return send(value, lambda x, y, z, core: (x + step, y, z, core))


def along_z(value, step):
    return send(value, lambda x, y, z, core: (x, y, z + step, core))


def other_core(value):
    return send(value, lambda x, y, z, core: (x, y, z, 1 - core))


def two_along_z(value):
    return send(value, lambda x, y, z, core: (x, y, z + (2 if core == 0 else -2), core))


def split_x(value):
    return send(value, lambda x, y, z, core: (x + (1 if core == 0 else -1), y, z, core))


def other_parity(value):
    return send(value, lambda x, y, z, core: (x, y + (1 if y % 2 == core else -1), z, core))


def params(mib):
    return pltpu.CompilerParams(vmem_limit_bytes=mib << 20)


def prologue_kernel(factors_in, pattern_in, coulomb_in, masked_ref, whole_ref, own_ref, factors, pattern, coulomb, sems):
    copies = [
        pltpu.make_async_copy(factors_in, factors, sems.at[0]),
        pltpu.make_async_copy(pattern_in, pattern, sems.at[1]),
        pltpu.make_async_copy(coulomb_in, coulomb, sems.at[2]),
    ]
    for copy in copies:
        copy.start()
    for copy in copies:
        copy.wait()
    parity = lax.axis_index("tm") & 1
    orb = factors.shape[1]
    for block in range(orb // BLOCK):
        lanes = pl.ds(block * BLOCK, BLOCK)
        keep = pattern[:, block : block + 1].astype(F32)
        for half in range(2):
            at = parity if half == 0 else 1 - parity
            part = factors[pl.ds(pl.multiple_of(at * HALF, HALF), HALF), lanes]
            part = (part.astype(F32) * keep).astype(BF16)
            masked_ref[pl.ds(half * HALF, HALF), lanes] = part
            if half == 0:
                whole_ref[pl.ds(0, HALF), lanes] = part
    c = coulomb[...]
    turned = pltpu.roll(c, HALF, 1)
    own = jnp.where(parity == 0, c, turned)
    own_ref[...] = own
    lane = lax.broadcasted_iota(jnp.int32, own.shape, 1)
    twice = jnp.where(lane < HALF, own, pltpu.roll(own, HALF, 1))
    high = twice.astype(BF16)
    rest = twice - high.astype(F32)
    middle = rest.astype(BF16)
    low = (rest - middle.astype(F32)).astype(BF16)
    zero = jnp.zeros((1, orb - 3 * BLOCK), BF16)
    row = jnp.concatenate([high, middle, low, zero], axis=1)
    rows = jnp.broadcast_to(row.astype(F32), (8, orb)).astype(BF16)
    whole_ref[pl.ds(HALF, 8), :] = rows


def prologue(factors, pattern, coulomb):
    own, orb = factors.shape
    return pl.pallas_call(
        prologue_kernel,
        out_shape=[
            jax.ShapeDtypeStruct((own, orb), BF16),
            jax.ShapeDtypeStruct((HALF + 8, orb), BF16),
            jax.ShapeDtypeStruct((1, own), F32),
        ],
        in_specs=[pl.BlockSpec(memory_space=pltpu.HBM)] * 3,
        out_specs=[VMEM] * 3,
        scratch_shapes=[
            pltpu.VMEM((own, orb), BF16),
            pltpu.VMEM(pattern.shape, jnp.int32),
            pltpu.VMEM((1, own), F32),
            pltpu.SemaphoreType.DMA((3,)),
        ],
        compiler_params=params(16),
    )(*[pltpu.with_memory_space_constraint(v, pltpu.HBM) for v in (factors, pattern, coulomb[None, :])])


def mix_kernel(west_ref, east_ref, onward_ref, both_ref):
    core = lax.axis_index("aux") & 1
    n = west_ref.shape[0]
    west, east = west_ref[...], east_ref[...]
    onward_ref[...] = jnp.where(core == 0, west, east)
    both_ref[pl.ds(0, n), :] = west
    both_ref[pl.ds(n, n), :] = east


def mix(west, east):
    n, orb = west.shape
    return pl.pallas_call(
        mix_kernel,
        out_shape=(jax.ShapeDtypeStruct((n, orb), BF16), jax.ShapeDtypeStruct((2 * n, orb), BF16)),
        in_specs=[VMEM] * 2,
        out_specs=[VMEM] * 2,
        compiler_params=params(8),
    )(west, east)


def after_kernel(value_ref, first_ref, out_ref):
    del first_ref
    pltpu.touch(value_ref)
    pltpu.touch(out_ref)


def after(value, first):
    return pl.pallas_call(
        after_kernel,
        out_shape=jax.ShapeDtypeStruct(value.shape, value.dtype),
        in_specs=[VMEM] * 2,
        out_specs=VMEM,
        input_output_aliases={0: 0},
        compiler_params=params(8),
    )(value, first)


def weight_of(ref, row):
    parts = [ref[pl.ds(row, 1), pl.ds(k * BLOCK, BLOCK)].astype(F32) for k in range(3)]
    return parts[0] + (parts[1] + parts[2])


def weights_of(ref, row, blocks):
    lane = lax.broadcasted_iota(jnp.int32, (1, BLOCK), 1)
    pairs = []
    for k in range(0, blocks, 2):
        pairs.append(jnp.where(lane < HALF, weight_of(ref, row + k), weight_of(ref, row + k + 1)))
    return jnp.concatenate(pairs, axis=1) if len(pairs) > 1 else pairs[0]


def rows_of(refs, piece):
    at, start, size = piece
    return refs[at][pl.ds(start, size), :], weights_of(refs[at], start + size, size // HALF)


def square_kernel(pieces, right_own, right_other, *refs):
    rows, out = refs[:-1], refs[-1]
    for t in range(right_own.shape[0]):
        right = jnp.concatenate([right_own[t], right_other[t]], axis=0)
        offset = 0
        for piece in pieces:
            part, weight = rows_of(rows, piece)
            a = lax.dot_general(right, part, NT, preferred_element_type=F32)
            out[t, :, pl.ds(offset, piece[2])] = a * a * weight
            offset += piece[2]


def squares(right, right_other, rows, pieces):
    times, own, orb = right.shape
    n = sum(piece[2] for piece in pieces)
    return pl.pallas_call(
        functools.partial(square_kernel, tuple(pieces)),
        out_shape=jax.ShapeDtypeStruct((times, 2 * own, n), F32),
        in_specs=[VMEM] * (2 + len(rows)),
        out_specs=VMEM,
        compiler_params=params(12),
        cost_estimate=pl.CostEstimate(
            flops=times * 2 * (2 * own) * n * orb, bytes_accessed=2 << 20, transcendentals=0
        ),
    )(right, right_other, *rows)


def chunk_kernel(pieces, sides, count, given, first, *refs):
    left_own, left_other = refs[sides - 2 : sides]
    rows = refs[sides : sides + count]
    rest = refs[sides + count :]
    if given:
        squared = rest[0]
        rest = rest[1:]
    if not first:
        acc_own, acc_other = rest[:2]
        rest = rest[2:]
    out_own, out_other = rest
    own = out_own.shape[1]
    for t in range(out_own.shape[0]):
        left = jnp.concatenate([left_own[t], left_other[t]], axis=0)
        total = None
        offset = 0
        for piece in pieces:
            part, weight = rows_of(rows, piece)
            if given:
                square = squared[t, :, pl.ds(offset, piece[2])]
            else:
                right = jnp.concatenate([refs[0][t], refs[1][t]], axis=0)
                a = lax.dot_general(right, part, NT, preferred_element_type=F32)
                square = a * a * weight
            offset += piece[2]
            m = lax.dot_general(left, part, NT, preferred_element_type=F32)
            k = (square * m).astype(BF16)
            d = lax.dot_general(k, part, NN, preferred_element_type=F32)
            total = d if total is None else total + d
        mine, theirs = total[:own], total[own:]
        if not first:
            mine, theirs = acc_own[t] + mine, acc_other[t] + theirs
        out_own[t] = mine
        out_other[t] = theirs.astype(out_other.dtype)


def chunk(sides, rows, pieces, given=(), acc=(), last=False):
    times, own, orb = sides[0].shape
    shape = jax.ShapeDtypeStruct((times, own, orb), F32)
    theirs = jax.ShapeDtypeStruct((times, own, orb), BF16 if last else F32)
    at = len(sides) + len(rows) + len(given)
    aliases = {}
    if acc:
        aliases[at] = 0
        if not last:
            aliases[at + 1] = 1
    n = sum(piece[2] for piece in pieces)
    flops = times * 2 * 2 * (2 * own) * n * orb // 2
    return pl.pallas_call(
        functools.partial(
            chunk_kernel, tuple(pieces), len(sides), len(rows), bool(given), not acc
        ),
        out_shape=(shape, theirs),
        in_specs=[VMEM] * (at + len(acc)),
        out_specs=(VMEM, VMEM),
        input_output_aliases=aliases,
        compiler_params=params(16),
        cost_estimate=pl.CostEstimate(flops=flops, bytes_accessed=2 << 20, transcendentals=0),
    )(*sides, *rows, *given, *acc)


def finish_kernel(own_ref, got_ref, coulomb_ref, out_ref):
    chips, times, rows, _ = out_ref.shape
    for t in range(times):
        d = jnp.transpose(own_ref[t] + got_ref[t].astype(F32)) * coulomb_ref[...]
        d = d.astype(BF16)
        for chip in range(chips):
            out_ref[chip, t] = d[chip * rows : (chip + 1) * rows]


def sigma_kernel(part_ref, *refs):
    here, here_q, west, east, sides_q, far, far_q = refs[:7]
    keep_ref, send_ref, lhs, total_ref = refs[7:]
    skip = west.shape[0]
    columns = [((here, 0), (here_q, 0)), ((west, 0), (sides_q, 0)), ((east, 0), (sides_q, skip)), ((far, 0), (far_q, 0))]
    chips, times, i_rows, width = part_ref.shape
    me = lax.axis_index("aux")
    core, x, z = me & 1, (me >> 1) & 3, me >> 3
    total = None
    for column, dx in enumerate((0, 3, 1, 2)):
        parts = []
        for k, dz in enumerate((0, 3, 1, 2)):
            source = ((z + dz) & 3) * 4 + ((x + dx) & 3)
            for t in range(times):
                at = pl.ds((column * 4 + k) * width, width)
                lhs[pl.ds(t * i_rows, i_rows), at] = part_ref[source, t]
            for ref, start in columns[column]:
                parts.append(ref[pl.ds(start + k * HALF, HALF), :])
        d = lax.dot_general(
            lhs[:, pl.ds(column * 4 * width, 4 * width)],
            jnp.concatenate(parts, axis=0),
            NN,
            preferred_element_type=F32,
        )
        total = d if total is None else total + d
    total_ref[...] = total
    half = i_rows // 2
    for t in range(times):
        keep = pl.multiple_of(t * i_rows + core * half, half)
        send = pl.multiple_of(t * i_rows + (1 - core) * half, half)
        keep_ref[t] = total_ref[pl.ds(keep, half), :]
        send_ref[t] = total_ref[pl.ds(send, half), :]


def add_kernel(keep_ref, got_ref, out_ref):
    for t in range(keep_ref.shape[0]):
        out_ref[:, t, :] = keep_ref[t] + got_ref[t]


def local(green, factors, pattern, coulomb):
    times, orb, _ = green.shape
    own = factors.shape[0]
    barrier = lax.optimization_barrier
    masked, whole, coulomb = prologue(factors, pattern, coulomb)

    beyond = two_along_z(whole)
    below = along_z(whole, 1)
    above = along_z(whole, -1)
    left = jnp.einsum("qo,tok->tqk", masked, green, preferred_element_type=F32).astype(BF16)
    left = two_along_z(left)

    blocks = [whole, below, above, beyond]
    weights = [block[HALF : HALF + 1] for block in blocks] + [jnp.zeros((4, orb), BF16)]
    here = barrier(jnp.concatenate([block[:HALF] for block in blocks] + weights, axis=0))

    n = 4 * HALF
    west = along_x(here, 1)
    east = along_x(here, -1)
    rest = other_parity(here[HALF:])
    here_q = jnp.concatenate([masked[HALF:], rest], axis=0)
    right = jnp.einsum("qo,tko->tqk", masked, green, preferred_element_type=F32).astype(BF16)
    west, east, right, here_q = barrier((west, east, right, here_q))
    right_other = other_core(right)
    onward, both = mix(west, east)
    far = split_x(onward)
    sides_q = other_parity(both)
    far_q = other_parity(far)
    left = two_along_z(left)
    left_other = other_core(left)

    rights, lefts = (right, right_other), (left, left_other)
    two = [(0, 0, n), (1, 0, n)]
    here_z = squares(*rights, (here, here_q), two)
    sides_z = squares(*rights, (west, east), two)
    acc = chunk(lefts, (here, here_q), two, given=(here_z,))
    acc = chunk(lefts, (west, east), two, given=(sides_z,), acc=acc)
    sides = rights + lefts
    acc = chunk(sides, (sides_q, far), [(0, 0, n), (0, n + 8, n), (1, 0, n)], acc=acc)
    keep, theirs = chunk(sides, (far_q,), [(0, 0, n)], acc=acc, last=True)

    got = other_core(theirs)
    chips, i_rows = 16, orb // 16
    part = pl.pallas_call(
        finish_kernel,
        out_shape=jax.ShapeDtypeStruct((chips, times, i_rows, own), BF16),
        in_specs=[VMEM] * 3,
        out_specs=VMEM,
        compiler_params=params(12),
    )(keep, got, coulomb)
    groups = [[2 * chip + core for chip in range(chips)] for core in range(2)]
    part = lax.all_to_all(part, "aux", 0, 0, axis_index_groups=groups, tiled=True)

    shape = jax.ShapeDtypeStruct((times, i_rows // 2, orb), F32)
    keep, theirs = pl.pallas_call(
        sigma_kernel,
        out_shape=(shape, shape),
        in_specs=[VMEM] * 8,
        out_specs=(VMEM, VMEM),
        scratch_shapes=[
            pltpu.VMEM((times * i_rows, chips * own), BF16),
            pltpu.VMEM((times * i_rows, orb), F32),
        ],
        compiler_params=params(12),
    )(part, here, here_q, west, east, sides_q, far, far_q)
    got = other_core(theirs)
    return pl.pallas_call(
        add_kernel,
        out_shape=jax.ShapeDtypeStruct((i_rows // 2, times, orb), F32),
        in_specs=[VMEM] * 2,
        out_specs=VMEM,
        compiler_params=params(8),
    )(keep, got)


def solution(mesh):
    in_specs = (P("tm", None, None), P("aux", None), P("aux", None), P("aux"))
    out_specs = P("aux", "tm", None)
    return jax.shard_map(local, mesh=mesh, in_specs=in_specs, out_specs=out_specs, check_vma=False)
```

```python
import functools

import jax
import jax.numpy as jnp
from jax import lax
from jax.experimental import pallas as pl
from jax.experimental.pallas import tpu as pltpu
from jax.sharding import PartitionSpec as P

BLOCK = 128
HALF = 64
F32, BF16 = jnp.float32, jnp.bfloat16
BOTH = ("tm", "aux")
NT = (((1,), (1,)), ((), ()))
NN = (((1,), (0,)), ((), ()))
VMEM = pl.BlockSpec(memory_space=pltpu.VMEM)


def device_at(x, y, z, core):
    return (z // 4 * 4 + y) * 32 + (z % 4 * 4 + x) * 2 + core


def send(value, to):
    pairs = []
    for x in range(4):
        for y in range(4):
            for z in range(8):
                for core in range(2):
                    tx, ty, tz, tcore = to(x, y, z, core)
                    pairs.append((device_at(x, y, z, core), device_at(tx % 4, ty % 4, tz % 8, tcore)))
    return lax.ppermute(value, BOTH, sorted(pairs))


def along_x(value, step):
    return send(value, lambda x, y, z, core: (x + step, y, z, core))


def along_z(value, step):
    return send(value, lambda x, y, z, core: (x, y, z + step, core))


def other_core(value):
    return send(value, lambda x, y, z, core: (x, y, z, 1 - core))


def two_along_z(value):
    return send(value, lambda x, y, z, core: (x, y, z + (2 if core == 0 else -2), core))


def split_x(value):
    return send(value, lambda x, y, z, core: (x + (1 if core == 0 else -1), y, z, core))


def other_parity(value):
    return send(value, lambda x, y, z, core: (x, y + (1 if y % 2 == core else -1), z, core))


def params(mib):
    return pltpu.CompilerParams(vmem_limit_bytes=mib << 20)


def prologue_kernel(factors_in, pattern_in, coulomb_in, masked_ref, whole_ref, own_ref, factors, pattern, coulomb, sems):
    copies = [
        pltpu.make_async_copy(factors_in, factors, sems.at[0]),
        pltpu.make_async_copy(pattern_in, pattern, sems.at[1]),
        pltpu.make_async_copy(coulomb_in, coulomb, sems.at[2]),
    ]
    for copy in copies:
        copy.start()
    for copy in copies:
        copy.wait()
    parity = lax.axis_index("tm") & 1
    orb = factors.shape[1]
    for block in range(orb // BLOCK):
        lanes = pl.ds(block * BLOCK, BLOCK)
        keep = pattern[:, block : block + 1].astype(F32)
        for half in range(2):
            at = parity if half == 0 else 1 - parity
            part = factors[pl.ds(pl.multiple_of(at * HALF, HALF), HALF), lanes]
            part = (part.astype(F32) * keep).astype(BF16)
            masked_ref[pl.ds(half * HALF, HALF), lanes] = part
            if half == 0:
                whole_ref[pl.ds(0, HALF), lanes] = part
    c = coulomb[...]
    turned = pltpu.roll(c, HALF, 1)
    own = jnp.where(parity == 0, c, turned)
    own_ref[...] = own
    lane = lax.broadcasted_iota(jnp.int32, own.shape, 1)
    twice = jnp.where(lane < HALF, own, pltpu.roll(own, HALF, 1))
    high = twice.astype(BF16)
    rest = twice - high.astype(F32)
    middle = rest.astype(BF16)
    low = (rest - middle.astype(F32)).astype(BF16)
    zero = jnp.zeros((1, orb - 3 * BLOCK), BF16)
    row = jnp.concatenate([high, middle, low, zero], axis=1)
    rows = jnp.broadcast_to(row.astype(F32), (8, orb)).astype(BF16)
    whole_ref[pl.ds(HALF, 8), :] = rows


def prologue(factors, pattern, coulomb):
    own, orb = factors.shape
    return pl.pallas_call(
        prologue_kernel,
        out_shape=[
            jax.ShapeDtypeStruct((own, orb), BF16),
            jax.ShapeDtypeStruct((HALF + 8, orb), BF16),
            jax.ShapeDtypeStruct((1, own), F32),
        ],
        in_specs=[pl.BlockSpec(memory_space=pltpu.HBM)] * 3,
        out_specs=[VMEM] * 3,
        scratch_shapes=[
            pltpu.VMEM((own, orb), BF16),
            pltpu.VMEM(pattern.shape, jnp.int32),
            pltpu.VMEM((1, own), F32),
            pltpu.SemaphoreType.DMA((3,)),
        ],
        compiler_params=params(16),
    )(*[pltpu.with_memory_space_constraint(v, pltpu.HBM) for v in (factors, pattern, coulomb[None, :])])


def mix_kernel(west_ref, east_ref, onward_ref, both_ref):
    core = lax.axis_index("aux") & 1
    n = west_ref.shape[0]
    west, east = west_ref[...], east_ref[...]
    onward_ref[...] = jnp.where(core == 0, west, east)
    both_ref[pl.ds(0, n), :] = west
    both_ref[pl.ds(n, n), :] = east


def mix(west, east):
    n, orb = west.shape
    return pl.pallas_call(
        mix_kernel,
        out_shape=(jax.ShapeDtypeStruct((n, orb), BF16), jax.ShapeDtypeStruct((2 * n, orb), BF16)),
        in_specs=[VMEM] * 2,
        out_specs=[VMEM] * 2,
        compiler_params=params(8),
    )(west, east)


def after_kernel(value_ref, *refs):
    pltpu.touch(value_ref)
    pltpu.touch(refs[-1])


def after(value, *first):
    return pl.pallas_call(
        after_kernel,
        out_shape=jax.ShapeDtypeStruct(value.shape, value.dtype),
        in_specs=[VMEM] * (1 + len(first)),
        out_specs=VMEM,
        input_output_aliases={0: 0},
        compiler_params=params(8),
    )(value, *first)


def weight_of(ref, row):
    parts = [ref[pl.ds(row, 1), pl.ds(k * BLOCK, BLOCK)].astype(F32) for k in range(3)]
    return parts[0] + (parts[1] + parts[2])


def weights_of(ref, row, blocks):
    lane = lax.broadcasted_iota(jnp.int32, (1, BLOCK), 1)
    pairs = []
    for k in range(0, blocks, 2):
        pairs.append(jnp.where(lane < HALF, weight_of(ref, row + k), weight_of(ref, row + k + 1)))
    return jnp.concatenate(pairs, axis=1) if len(pairs) > 1 else pairs[0]


def rows_of(refs, piece):
    at, start, size = piece
    return refs[at][pl.ds(start, size), :], weights_of(refs[at], start + size, size // HALF)


def square_kernel(pieces, right_own, right_other, *refs):
    rows, out = refs[:-1], refs[-1]
    for t in range(right_own.shape[0]):
        right = jnp.concatenate([right_own[t], right_other[t]], axis=0)
        offset = 0
        for piece in pieces:
            part, weight = rows_of(rows, piece)
            a = lax.dot_general(right, part, NT, preferred_element_type=F32)
            out[t, :, pl.ds(offset, piece[2])] = a * a * weight
            offset += piece[2]


def squares(right, right_other, rows, pieces):
    times, own, orb = right.shape
    n = sum(piece[2] for piece in pieces)
    return pl.pallas_call(
        functools.partial(square_kernel, tuple(pieces)),
        out_shape=jax.ShapeDtypeStruct((times, 2 * own, n), F32),
        in_specs=[VMEM] * (2 + len(rows)),
        out_specs=VMEM,
        compiler_params=params(12),
        cost_estimate=pl.CostEstimate(
            flops=times * 2 * (2 * own) * n * orb, bytes_accessed=2 << 20, transcendentals=0
        ),
    )(right, right_other, *rows)


def chunk_kernel(pieces, sides, count, given, first, *refs):
    left_own, left_other = refs[sides - 2 : sides]
    rows = refs[sides : sides + count]
    rest = refs[sides + count :]
    if given:
        squared = rest[0]
        rest = rest[1:]
    if not first:
        acc_own, acc_other = rest[:2]
        rest = rest[2:]
    out_own, out_other = rest
    own = out_own.shape[1]
    for t in range(out_own.shape[0]):
        left = jnp.concatenate([left_own[t], left_other[t]], axis=0)
        total = None
        offset = 0
        for piece in pieces:
            part, weight = rows_of(rows, piece)
            if given:
                square = squared[t, :, pl.ds(offset, piece[2])]
            else:
                right = jnp.concatenate([refs[0][t], refs[1][t]], axis=0)
                a = lax.dot_general(right, part, NT, preferred_element_type=F32)
                square = a * a * weight
            offset += piece[2]
            m = lax.dot_general(left, part, NT, preferred_element_type=F32)
            k = (square * m).astype(BF16)
            d = lax.dot_general(k, part, NN, preferred_element_type=F32)
            total = d if total is None else total + d
        mine, theirs = total[:own], total[own:]
        if not first:
            mine, theirs = acc_own[t] + mine, acc_other[t] + theirs
        out_own[t] = mine
        out_other[t] = theirs.astype(out_other.dtype)


def chunk(sides, rows, pieces, given=(), acc=(), last=False):
    times, own, orb = sides[0].shape
    shape = jax.ShapeDtypeStruct((times, own, orb), F32)
    theirs = jax.ShapeDtypeStruct((times, own, orb), BF16 if last else F32)
    at = len(sides) + len(rows) + len(given)
    aliases = {}
    if acc:
        aliases[at] = 0
        if not last:
            aliases[at + 1] = 1
    n = sum(piece[2] for piece in pieces)
    flops = times * 2 * 2 * (2 * own) * n * orb // 2
    return pl.pallas_call(
        functools.partial(
            chunk_kernel, tuple(pieces), len(sides), len(rows), bool(given), not acc
        ),
        out_shape=(shape, theirs),
        in_specs=[VMEM] * (at + len(acc)),
        out_specs=(VMEM, VMEM),
        input_output_aliases=aliases,
        compiler_params=params(16),
        cost_estimate=pl.CostEstimate(flops=flops, bytes_accessed=2 << 20, transcendentals=0),
    )(*sides, *rows, *given, *acc)


def finish_kernel(own_ref, got_ref, coulomb_ref, out_ref):
    chips, times, rows, _ = out_ref.shape
    for t in range(times):
        d = jnp.transpose(own_ref[t] + got_ref[t].astype(F32)) * coulomb_ref[...]
        d = d.astype(BF16)
        for chip in range(chips):
            out_ref[chip, t] = d[chip * rows : (chip + 1) * rows]


def sigma_kernel(part_ref, *refs):
    here, here_q, west, east, sides_q, far, far_q = refs[:7]
    keep_ref, send_ref, lhs, total_ref = refs[7:]
    skip = west.shape[0]
    columns = [((here, 0), (here_q, 0)), ((west, 0), (sides_q, 0)), ((east, 0), (sides_q, skip)), ((far, 0), (far_q, 0))]
    chips, times, i_rows, width = part_ref.shape
    me = lax.axis_index("aux")
    core, x, z = me & 1, (me >> 1) & 3, me >> 3
    total = None
    for column, dx in enumerate((0, 3, 1, 2)):
        parts = []
        for k, dz in enumerate((0, 3, 1, 2)):
            source = ((z + dz) & 3) * 4 + ((x + dx) & 3)
            for t in range(times):
                at = pl.ds((column * 4 + k) * width, width)
                lhs[pl.ds(t * i_rows, i_rows), at] = part_ref[source, t]
            for ref, start in columns[column]:
                parts.append(ref[pl.ds(start + k * HALF, HALF), :])
        d = lax.dot_general(
            lhs[:, pl.ds(column * 4 * width, 4 * width)],
            jnp.concatenate(parts, axis=0),
            NN,
            preferred_element_type=F32,
        )
        total = d if total is None else total + d
    total_ref[...] = total
    half = i_rows // 2
    for t in range(times):
        keep = pl.multiple_of(t * i_rows + core * half, half)
        send = pl.multiple_of(t * i_rows + (1 - core) * half, half)
        keep_ref[t] = total_ref[pl.ds(keep, half), :]
        send_ref[t] = total_ref[pl.ds(send, half), :].astype(BF16)


def add_kernel(keep_ref, got_ref, out_ref):
    for t in range(keep_ref.shape[0]):
        out_ref[:, t, :] = keep_ref[t] + got_ref[t].astype(F32)


def local(green, factors, pattern, coulomb):
    times, orb, _ = green.shape
    own = factors.shape[0]
    barrier = lax.optimization_barrier
    masked, whole, coulomb = prologue(factors, pattern, coulomb)

    beyond = two_along_z(whole)
    below = along_z(whole, 1)
    above = along_z(whole, -1)
    left = jnp.einsum("qo,tok->tqk", masked, green, preferred_element_type=F32).astype(BF16)
    left = two_along_z(left)

    blocks = [whole, below, above, beyond]
    weights = [block[HALF : HALF + 1] for block in blocks] + [jnp.zeros((4, orb), BF16)]
    here = barrier(jnp.concatenate([block[:HALF] for block in blocks] + weights, axis=0))

    n = 4 * HALF
    west = along_x(here, 1)
    east = along_x(here, -1)
    rest = other_parity(here[HALF:])
    here_q = jnp.concatenate([masked[HALF:], rest], axis=0)
    right = jnp.einsum("qo,tko->tqk", masked, green, preferred_element_type=F32).astype(BF16)
    west, east, right, here_q = barrier((west, east, right, here_q))
    right_other = other_core(right)
    onward, both = mix(west, east)
    far = split_x(onward)
    sides_q = other_parity(both)
    far_q = other_parity(far)
    left = two_along_z(left)
    rights = (right, right_other)
    squared = squares(*rights, (here, here_q, west, east), [(k, 0, n) for k in range(4)])
    left_other = other_core(left)

    lefts = (left, left_other)
    four = [(k, 0, n) for k in range(4)]
    acc = chunk(lefts, (here, here_q, west, east), four, given=(squared,))
    sides = rights + lefts
    acc = chunk(sides, (sides_q, far), [(0, 0, n), (0, n + 8, n), (1, 0, n)], acc=acc)
    keep, theirs = chunk(sides, (far_q,), [(0, 0, n)], acc=acc, last=True)

    got = other_core(theirs)
    chips, i_rows = 16, orb // 16
    part = pl.pallas_call(
        finish_kernel,
        out_shape=jax.ShapeDtypeStruct((chips, times, i_rows, own), BF16),
        in_specs=[VMEM] * 3,
        out_specs=VMEM,
        compiler_params=params(12),
    )(keep, got, coulomb)
    groups = [[2 * chip + core for chip in range(chips)] for core in range(2)]
    part = lax.all_to_all(part, "aux", 0, 0, axis_index_groups=groups, tiled=True)

    shape = jax.ShapeDtypeStruct((times, i_rows // 2, orb), F32)
    keep, theirs = pl.pallas_call(
        sigma_kernel,
        out_shape=(shape, jax.ShapeDtypeStruct(shape.shape, BF16)),
        in_specs=[VMEM] * 8,
        out_specs=(VMEM, VMEM),
        scratch_shapes=[
            pltpu.VMEM((times * i_rows, chips * own), BF16),
            pltpu.VMEM((times * i_rows, orb), F32),
        ],
        compiler_params=params(12),
    )(part, here, here_q, west, east, sides_q, far, far_q)
    got = other_core(theirs)
    return pl.pallas_call(
        add_kernel,
        out_shape=jax.ShapeDtypeStruct((i_rows // 2, times, orb), F32),
        in_specs=[VMEM] * 2,
        out_specs=VMEM,
        compiler_params=params(8),
    )(keep, got)


def solution(mesh):
    in_specs = (P("tm", None, None), P("aux", None), P("aux", None), P("aux"))
    out_specs = P("aux", "tm", None)
    return jax.shard_map(local, mesh=mesh, in_specs=in_specs, out_specs=out_specs, check_vma=False)
```

```python
import functools

import jax
import jax.numpy as jnp
from jax import lax
from jax.experimental import pallas as pl
from jax.experimental.pallas import tpu as pltpu
from jax.sharding import PartitionSpec as P

BLOCK = 128
HALF = 64
F32, BF16 = jnp.float32, jnp.bfloat16
BOTH = ("tm", "aux")
NT = (((1,), (1,)), ((), ()))
NN = (((1,), (0,)), ((), ()))
VMEM = pl.BlockSpec(memory_space=pltpu.VMEM)


def device_at(x, y, z, core):
    return (z // 4 * 4 + y) * 32 + (z % 4 * 4 + x) * 2 + core


def send(value, to):
    pairs = []
    for x in range(4):
        for y in range(4):
            for z in range(8):
                for core in range(2):
                    tx, ty, tz, tcore = to(x, y, z, core)
                    pairs.append((device_at(x, y, z, core), device_at(tx % 4, ty % 4, tz % 8, tcore)))
    return lax.ppermute(value, BOTH, sorted(pairs))


def along_x(value, step):
    return send(value, lambda x, y, z, core: (x + step, y, z, core))


def along_z(value, step):
    return send(value, lambda x, y, z, core: (x, y, z + step, core))


def other_core(value):
    return send(value, lambda x, y, z, core: (x, y, z, 1 - core))


def two_along_z(value):
    return send(value, lambda x, y, z, core: (x, y, z + (2 if core == 0 else -2), core))


def split_x(value):
    return send(value, lambda x, y, z, core: (x + (1 if core == 0 else -1), y, z, core))


def other_parity(value):
    return send(value, lambda x, y, z, core: (x, y + (1 if y % 2 == core else -1), z, core))


def params(mib):
    return pltpu.CompilerParams(vmem_limit_bytes=mib << 20)


def prologue_kernel(factors_in, pattern_in, coulomb_in, masked_ref, whole_ref, own_ref, factors, pattern, coulomb, sems):
    copies = [
        pltpu.make_async_copy(factors_in, factors, sems.at[0]),
        pltpu.make_async_copy(pattern_in, pattern, sems.at[1]),
        pltpu.make_async_copy(coulomb_in, coulomb, sems.at[2]),
    ]
    for copy in copies:
        copy.start()
    for copy in copies:
        copy.wait()
    parity = lax.axis_index("tm") & 1
    orb = factors.shape[1]
    for block in range(orb // BLOCK):
        lanes = pl.ds(block * BLOCK, BLOCK)
        keep = pattern[:, block : block + 1].astype(F32)
        for half in range(2):
            at = parity if half == 0 else 1 - parity
            part = factors[pl.ds(pl.multiple_of(at * HALF, HALF), HALF), lanes]
            part = (part.astype(F32) * keep).astype(BF16)
            masked_ref[pl.ds(half * HALF, HALF), lanes] = part
            if half == 0:
                whole_ref[pl.ds(0, HALF), lanes] = part
    c = coulomb[...]
    turned = pltpu.roll(c, HALF, 1)
    own = jnp.where(parity == 0, c, turned)
    own_ref[...] = own
    lane = lax.broadcasted_iota(jnp.int32, own.shape, 1)
    twice = jnp.where(lane < HALF, own, pltpu.roll(own, HALF, 1))
    high = twice.astype(BF16)
    rest = twice - high.astype(F32)
    middle = rest.astype(BF16)
    low = (rest - middle.astype(F32)).astype(BF16)
    zero = jnp.zeros((1, orb - 3 * BLOCK), BF16)
    row = jnp.concatenate([high, middle, low, zero], axis=1)
    rows = jnp.broadcast_to(row.astype(F32), (8, orb)).astype(BF16)
    whole_ref[pl.ds(HALF, 8), :] = rows


def prologue(factors, pattern, coulomb):
    own, orb = factors.shape
    return pl.pallas_call(
        prologue_kernel,
        out_shape=[
            jax.ShapeDtypeStruct((own, orb), BF16),
            jax.ShapeDtypeStruct((HALF + 8, orb), BF16),
            jax.ShapeDtypeStruct((1, own), F32),
        ],
        in_specs=[pl.BlockSpec(memory_space=pltpu.HBM)] * 3,
        out_specs=[VMEM] * 3,
        scratch_shapes=[
            pltpu.VMEM((own, orb), BF16),
            pltpu.VMEM(pattern.shape, jnp.int32),
            pltpu.VMEM((1, own), F32),
            pltpu.SemaphoreType.DMA((3,)),
        ],
        compiler_params=params(16),
    )(*[pltpu.with_memory_space_constraint(v, pltpu.HBM) for v in (factors, pattern, coulomb[None, :])])


def mix_kernel(west_ref, east_ref, onward_ref, both_ref):
    core = lax.axis_index("aux") & 1
    n = west_ref.shape[0]
    west, east = west_ref[...], east_ref[...]
    onward_ref[...] = jnp.where(core == 0, west, east)
    both_ref[pl.ds(0, n), :] = west
    both_ref[pl.ds(n, n), :] = east


def mix(west, east):
    n, orb = west.shape
    return pl.pallas_call(
        mix_kernel,
        out_shape=(jax.ShapeDtypeStruct((n, orb), BF16), jax.ShapeDtypeStruct((2 * n, orb), BF16)),
        in_specs=[VMEM] * 2,
        out_specs=[VMEM] * 2,
        compiler_params=params(8),
    )(west, east)


def weight_of(ref, row):
    parts = [ref[pl.ds(row, 1), pl.ds(k * BLOCK, BLOCK)].astype(F32) for k in range(3)]
    return parts[0] + (parts[1] + parts[2])


def weights_of(ref, row, blocks):
    lane = lax.broadcasted_iota(jnp.int32, (1, BLOCK), 1)
    pairs = []
    for k in range(0, blocks, 2):
        pairs.append(jnp.where(lane < HALF, weight_of(ref, row + k), weight_of(ref, row + k + 1)))
    return jnp.concatenate(pairs, axis=1) if len(pairs) > 1 else pairs[0]


def rows_of(refs, piece):
    at, start, size = piece
    return refs[at][pl.ds(start, size), :], weights_of(refs[at], start + size, size // HALF)


def chunk_kernel(pieces, sides, count, first, *refs):
    left_own, left_other = refs[sides - 2 : sides]
    rows = refs[sides : sides + count]
    rest = refs[sides + count :]
    if not first:
        acc_own, acc_other = rest[:2]
        rest = rest[2:]
    out_own, out_other = rest
    own = out_own.shape[1]
    for t in range(out_own.shape[0]):
        left = jnp.concatenate([left_own[t], left_other[t]], axis=0)
        right = jnp.concatenate([refs[0][t], refs[1][t]], axis=0)
        pairs = [rows_of(rows, piece) for piece in pieces]
        part = jnp.concatenate([pair[0] for pair in pairs], axis=0)
        weight = jnp.concatenate([pair[1] for pair in pairs], axis=1)
        a = lax.dot_general(right, part, NT, preferred_element_type=F32)
        m = lax.dot_general(left, part, NT, preferred_element_type=F32)
        k = (a * a * weight * m).astype(BF16)
        total = lax.dot_general(k, part, NN, preferred_element_type=F32)
        mine, theirs = total[:own], total[own:]
        if not first:
            mine, theirs = acc_own[t] + mine, acc_other[t] + theirs
        out_own[t] = mine
        out_other[t] = theirs.astype(out_other.dtype)


def chunk(sides, rows, pieces, acc=(), last=False):
    times, own, orb = sides[0].shape
    shape = jax.ShapeDtypeStruct((times, own, orb), F32)
    theirs = jax.ShapeDtypeStruct((times, own, orb), BF16 if last else F32)
    at = len(sides) + len(rows)
    aliases = {}
    if acc:
        aliases[at] = 0
        if not last:
            aliases[at + 1] = 1
    n = sum(piece[2] for piece in pieces)
    flops = times * 2 * 2 * (2 * own) * n * orb // 2
    return pl.pallas_call(
        functools.partial(
            chunk_kernel, tuple(pieces), len(sides), len(rows), not acc
        ),
        out_shape=(shape, theirs),
        in_specs=[VMEM] * (at + len(acc)),
        out_specs=(VMEM, VMEM),
        input_output_aliases=aliases,
        compiler_params=params(16),
        cost_estimate=pl.CostEstimate(flops=flops, bytes_accessed=2 << 20, transcendentals=0),
    )(*sides, *rows, *acc)


def finish_kernel(own_ref, got_ref, coulomb_ref, out_ref):
    chips, times, rows, _ = out_ref.shape
    for t in range(times):
        d = jnp.transpose(own_ref[t] + got_ref[t].astype(F32)) * coulomb_ref[...]
        d = d.astype(BF16)
        for chip in range(chips):
            out_ref[chip, t] = d[chip * rows : (chip + 1) * rows]


def sigma_kernel(part_ref, *refs):
    here, here_q, west, east, sides_q, far, far_q = refs[:7]
    keep_ref, send_ref, lhs, total_ref = refs[7:]
    skip = west.shape[0]
    columns = [((here, 0), (here_q, 0)), ((west, 0), (sides_q, 0)), ((east, 0), (sides_q, skip)), ((far, 0), (far_q, 0))]
    chips, times, i_rows, width = part_ref.shape
    me = lax.axis_index("aux")
    core, x, z = me & 1, (me >> 1) & 3, me >> 3
    total = None
    for column, dx in enumerate((0, 3, 1, 2)):
        parts = []
        for k, dz in enumerate((0, 3, 1, 2)):
            source = ((z + dz) & 3) * 4 + ((x + dx) & 3)
            for t in range(times):
                at = pl.ds((column * 4 + k) * width, width)
                lhs[pl.ds(t * i_rows, i_rows), at] = part_ref[source, t]
            for ref, start in columns[column]:
                parts.append(ref[pl.ds(start + k * HALF, HALF), :])
        d = lax.dot_general(
            lhs[:, pl.ds(column * 4 * width, 4 * width)],
            jnp.concatenate(parts, axis=0),
            NN,
            preferred_element_type=F32,
        )
        total = d if total is None else total + d
    total_ref[...] = total
    half = i_rows // 2
    for t in range(times):
        keep = pl.multiple_of(t * i_rows + core * half, half)
        send = pl.multiple_of(t * i_rows + (1 - core) * half, half)
        keep_ref[t] = total_ref[pl.ds(keep, half), :]
        send_ref[t] = total_ref[pl.ds(send, half), :].astype(BF16)


def add_kernel(keep_ref, got_ref, out_ref):
    for t in range(keep_ref.shape[0]):
        out_ref[:, t, :] = keep_ref[t] + got_ref[t].astype(F32)


def local(green, factors, pattern, coulomb):
    times, orb, _ = green.shape
    own = factors.shape[0]
    barrier = lax.optimization_barrier
    masked, whole, coulomb = prologue(factors, pattern, coulomb)

    beyond = two_along_z(whole)
    below = along_z(whole, 1)
    above = along_z(whole, -1)
    left = jnp.einsum("qo,tok->tqk", masked, green, preferred_element_type=F32).astype(BF16)
    left = two_along_z(left)

    blocks = [whole, below, above, beyond]
    weights = [block[HALF : HALF + 1] for block in blocks] + [jnp.zeros((4, orb), BF16)]
    here = barrier(jnp.concatenate([block[:HALF] for block in blocks] + weights, axis=0))

    n = 4 * HALF
    west = along_x(here, 1)
    east = along_x(here, -1)
    rest = other_parity(here[HALF:])
    here_q = jnp.concatenate([masked[HALF:], rest], axis=0)
    right = jnp.einsum("qo,tko->tqk", masked, green, preferred_element_type=F32).astype(BF16)
    west, east, right, here_q = barrier((west, east, right, here_q))
    right_other = other_core(right)
    onward, both = mix(west, east)
    far = split_x(onward)
    sides_q = other_parity(both)
    far_q = other_parity(far)
    left = two_along_z(left)
    rights = (right, right_other)
    left_other = other_core(left)

    lefts = (left, left_other)
    two = [(0, 0, n), (1, 0, n)]
    sides = rights + lefts
    acc = chunk(sides, (here, here_q), two)
    acc = chunk(sides, (west, east), two, acc=acc)
    acc = chunk(sides, (sides_q, far), [(0, 0, n), (0, n + 8, n), (1, 0, n)], acc=acc)
    keep, theirs = chunk(sides, (far_q,), [(0, 0, n)], acc=acc, last=True)

    got = other_core(theirs)
    chips, i_rows = 16, orb // 16
    part = pl.pallas_call(
        finish_kernel,
        out_shape=jax.ShapeDtypeStruct((chips, times, i_rows, own), BF16),
        in_specs=[VMEM] * 3,
        out_specs=VMEM,
        compiler_params=params(12),
    )(keep, got, coulomb)
    groups = [[2 * chip + core for chip in range(chips)] for core in range(2)]
    part = lax.all_to_all(part, "aux", 0, 0, axis_index_groups=groups, tiled=True)

    shape = jax.ShapeDtypeStruct((times, i_rows // 2, orb), F32)
    keep, theirs = pl.pallas_call(
        sigma_kernel,
        out_shape=(shape, jax.ShapeDtypeStruct(shape.shape, BF16)),
        in_specs=[VMEM] * 8,
        out_specs=(VMEM, VMEM),
        scratch_shapes=[
            pltpu.VMEM((times * i_rows, chips * own), BF16),
            pltpu.VMEM((times * i_rows, orb), F32),
        ],
        compiler_params=params(12),
    )(part, here, here_q, west, east, sides_q, far, far_q)
    got = other_core(theirs)
    return pl.pallas_call(
        add_kernel,
        out_shape=jax.ShapeDtypeStruct((i_rows // 2, times, orb), F32),
        in_specs=[VMEM] * 2,
        out_specs=VMEM,
        compiler_params=params(8),
    )(keep, got)


def solution(mesh):
    in_specs = (P("tm", None, None), P("aux", None), P("aux", None), P("aux"))
    out_specs = P("aux", "tm", None)
    return jax.shard_map(local, mesh=mesh, in_specs=in_specs, out_specs=out_specs, check_vma=False)
```

```python
import functools

import jax
import jax.numpy as jnp
from jax import lax
from jax.experimental import pallas as pl
from jax.experimental.pallas import tpu as pltpu
from jax.sharding import PartitionSpec as P

BLOCK = 128
HALF = 64
F32, BF16 = jnp.float32, jnp.bfloat16
BOTH = ("tm", "aux")
NT = (((1,), (1,)), ((), ()))
NN = (((1,), (0,)), ((), ()))
VMEM = pl.BlockSpec(memory_space=pltpu.VMEM)


def device_at(x, y, z, core):
    return (z // 4 * 4 + y) * 32 + (z % 4 * 4 + x) * 2 + core


def send(value, to):
    pairs = []
    for x in range(4):
        for y in range(4):
            for z in range(8):
                for core in range(2):
                    tx, ty, tz, tcore = to(x, y, z, core)
                    pairs.append((device_at(x, y, z, core), device_at(tx % 4, ty % 4, tz % 8, tcore)))
    return lax.ppermute(value, BOTH, sorted(pairs))


def along_x(value, step):
    return send(value, lambda x, y, z, core: (x + step, y, z, core))


def along_z(value, step):
    return send(value, lambda x, y, z, core: (x, y, z + step, core))


def other_core(value):
    return send(value, lambda x, y, z, core: (x, y, z, 1 - core))


def two_along_z(value):
    return send(value, lambda x, y, z, core: (x, y, z + (2 if core == 0 else -2), core))


def split_x(value):
    return send(value, lambda x, y, z, core: (x + (1 if core == 0 else -1), y, z, core))


def other_parity(value):
    return send(value, lambda x, y, z, core: (x, y + (1 if y % 2 == core else -1), z, core))


def params(mib):
    return pltpu.CompilerParams(vmem_limit_bytes=mib << 20)


def prologue_kernel(factors_in, pattern_in, coulomb_in, masked_ref, whole_ref, own_ref, factors, pattern, coulomb, sems):
    copies = [
        pltpu.make_async_copy(factors_in, factors, sems.at[0]),
        pltpu.make_async_copy(pattern_in, pattern, sems.at[1]),
        pltpu.make_async_copy(coulomb_in, coulomb, sems.at[2]),
    ]
    for copy in copies:
        copy.start()
    for copy in copies:
        copy.wait()
    parity = lax.axis_index("tm") & 1
    orb = factors.shape[1]
    for block in range(orb // BLOCK):
        lanes = pl.ds(block * BLOCK, BLOCK)
        keep = pattern[:, block : block + 1].astype(F32)
        for half in range(2):
            at = parity if half == 0 else 1 - parity
            part = factors[pl.ds(pl.multiple_of(at * HALF, HALF), HALF), lanes]
            part = (part.astype(F32) * keep).astype(BF16)
            masked_ref[pl.ds(half * HALF, HALF), lanes] = part
            if half == 0:
                whole_ref[pl.ds(0, HALF), lanes] = part
    c = coulomb[...]
    turned = pltpu.roll(c, HALF, 1)
    own = jnp.where(parity == 0, c, turned)
    own_ref[...] = own
    lane = lax.broadcasted_iota(jnp.int32, own.shape, 1)
    twice = jnp.where(lane < HALF, own, pltpu.roll(own, HALF, 1))
    high = twice.astype(BF16)
    rest = twice - high.astype(F32)
    middle = rest.astype(BF16)
    low = (rest - middle.astype(F32)).astype(BF16)
    zero = jnp.zeros((1, orb - 3 * BLOCK), BF16)
    row = jnp.concatenate([high, middle, low, zero], axis=1)
    rows = jnp.broadcast_to(row.astype(F32), (8, orb)).astype(BF16)
    whole_ref[pl.ds(HALF, 8), :] = rows


def prologue(factors, pattern, coulomb):
    own, orb = factors.shape
    return pl.pallas_call(
        prologue_kernel,
        out_shape=[
            jax.ShapeDtypeStruct((own, orb), BF16),
            jax.ShapeDtypeStruct((HALF + 8, orb), BF16),
            jax.ShapeDtypeStruct((1, own), F32),
        ],
        in_specs=[pl.BlockSpec(memory_space=pltpu.HBM)] * 3,
        out_specs=[VMEM] * 3,
        scratch_shapes=[
            pltpu.VMEM((own, orb), BF16),
            pltpu.VMEM(pattern.shape, jnp.int32),
            pltpu.VMEM((1, own), F32),
            pltpu.SemaphoreType.DMA((3,)),
        ],
        compiler_params=params(16),
    )(*[pltpu.with_memory_space_constraint(v, pltpu.HBM) for v in (factors, pattern, coulomb[None, :])])


def project_kernel(dims, masked_ref, green_ref, out_ref):
    for t in range(green_ref.shape[0]):
        out_ref[t] = lax.dot_general(
            masked_ref[...], green_ref[t], dims, preferred_element_type=F32
        ).astype(BF16)


def project(masked, green, dims):
    own, orb = masked.shape
    return pl.pallas_call(
        functools.partial(project_kernel, dims),
        out_shape=jax.ShapeDtypeStruct((green.shape[0], own, orb), BF16),
        in_specs=[VMEM] * 2,
        out_specs=VMEM,
        compiler_params=params(12),
        cost_estimate=pl.CostEstimate(
            flops=2 * green.shape[0] * own * orb * orb, bytes_accessed=4 << 20, transcendentals=0
        ),
    )(masked, green)


def mix_kernel(west_ref, east_ref, onward_ref, both_ref):
    core = lax.axis_index("aux") & 1
    n = west_ref.shape[0]
    west, east = west_ref[...], east_ref[...]
    onward_ref[...] = jnp.where(core == 0, west, east)
    both_ref[pl.ds(0, n), :] = west
    both_ref[pl.ds(n, n), :] = east


def mix(west, east):
    n, orb = west.shape
    return pl.pallas_call(
        mix_kernel,
        out_shape=(jax.ShapeDtypeStruct((n, orb), BF16), jax.ShapeDtypeStruct((2 * n, orb), BF16)),
        in_specs=[VMEM] * 2,
        out_specs=[VMEM] * 2,
        compiler_params=params(8),
    )(west, east)


def weight_of(ref, row):
    parts = [ref[pl.ds(row, 1), pl.ds(k * BLOCK, BLOCK)].astype(F32) for k in range(3)]
    return parts[0] + (parts[1] + parts[2])


def weights_of(ref, row, blocks):
    lane = lax.broadcasted_iota(jnp.int32, (1, BLOCK), 1)
    pairs = []
    for k in range(0, blocks, 2):
        pairs.append(jnp.where(lane < HALF, weight_of(ref, row + k), weight_of(ref, row + k + 1)))
    return jnp.concatenate(pairs, axis=1) if len(pairs) > 1 else pairs[0]


def rows_of(refs, piece):
    at, start, size = piece
    return refs[at][pl.ds(start, size), :], weights_of(refs[at], start + size, size // HALF)


def chunk_kernel(pieces, sides, count, first, *refs):
    left_own, left_other = refs[sides - 2 : sides]
    rows = refs[sides : sides + count]
    rest = refs[sides + count :]
    if not first:
        acc_own, acc_other = rest[:2]
        rest = rest[2:]
    out_own, out_other = rest
    own = out_own.shape[1]
    for t in range(out_own.shape[0]):
        left = jnp.concatenate([left_own[t], left_other[t]], axis=0)
        right = jnp.concatenate([refs[0][t], refs[1][t]], axis=0)
        pairs = [rows_of(rows, piece) for piece in pieces]
        part = jnp.concatenate([pair[0] for pair in pairs], axis=0)
        weight = jnp.concatenate([pair[1] for pair in pairs], axis=1)
        a = lax.dot_general(right, part, NT, preferred_element_type=F32)
        m = lax.dot_general(left, part, NT, preferred_element_type=F32)
        k = (a * a * weight * m).astype(BF16)
        total = lax.dot_general(k, part, NN, preferred_element_type=F32)
        mine, theirs = total[:own], total[own:]
        if not first:
            mine, theirs = acc_own[t] + mine, acc_other[t] + theirs
        out_own[t] = mine
        out_other[t] = theirs.astype(out_other.dtype)


def chunk(sides, rows, pieces, acc=(), last=False):
    times, own, orb = sides[0].shape
    shape = jax.ShapeDtypeStruct((times, own, orb), F32)
    theirs = jax.ShapeDtypeStruct((times, own, orb), BF16 if last else F32)
    at = len(sides) + len(rows)
    aliases = {}
    if acc:
        aliases[at] = 0
        if not last:
            aliases[at + 1] = 1
    n = sum(piece[2] for piece in pieces)
    flops = times * 2 * 2 * (2 * own) * n * orb // 2
    return pl.pallas_call(
        functools.partial(
            chunk_kernel, tuple(pieces), len(sides), len(rows), not acc
        ),
        out_shape=(shape, theirs),
        in_specs=[VMEM] * (at + len(acc)),
        out_specs=(VMEM, VMEM),
        input_output_aliases=aliases,
        compiler_params=params(16),
        cost_estimate=pl.CostEstimate(flops=flops, bytes_accessed=2 << 20, transcendentals=0),
    )(*sides, *rows, *acc)


def finish_kernel(own_ref, got_ref, coulomb_ref, out_ref):
    chips, times, rows, _ = out_ref.shape
    for t in range(times):
        d = jnp.transpose(own_ref[t] + got_ref[t].astype(F32)) * coulomb_ref[...]
        d = d.astype(BF16)
        for chip in range(chips):
            out_ref[chip, t] = d[chip * rows : (chip + 1) * rows]


def sigma_kernel(part_ref, *refs):
    here, here_q, west, east, sides_q, far, far_q = refs[:7]
    keep_ref, send_ref, lhs, total_ref = refs[7:]
    skip = west.shape[0]
    columns = [((here, 0), (here_q, 0)), ((west, 0), (sides_q, 0)), ((east, 0), (sides_q, skip)), ((far, 0), (far_q, 0))]
    chips, times, i_rows, width = part_ref.shape
    me = lax.axis_index("aux")
    core, x, z = me & 1, (me >> 1) & 3, me >> 3
    total = None
    for column, dx in enumerate((0, 3, 1, 2)):
        parts = []
        for k, dz in enumerate((0, 3, 1, 2)):
            source = ((z + dz) & 3) * 4 + ((x + dx) & 3)
            for t in range(times):
                at = pl.ds((column * 4 + k) * width, width)
                lhs[pl.ds(t * i_rows, i_rows), at] = part_ref[source, t]
            for ref, start in columns[column]:
                parts.append(ref[pl.ds(start + k * HALF, HALF), :])
        d = lax.dot_general(
            lhs[:, pl.ds(column * 4 * width, 4 * width)],
            jnp.concatenate(parts, axis=0),
            NN,
            preferred_element_type=F32,
        )
        total = d if total is None else total + d
    total_ref[...] = total
    half = i_rows // 2
    for t in range(times):
        keep = pl.multiple_of(t * i_rows + core * half, half)
        send = pl.multiple_of(t * i_rows + (1 - core) * half, half)
        keep_ref[t] = total_ref[pl.ds(keep, half), :]
        send_ref[t] = total_ref[pl.ds(send, half), :].astype(BF16)


def add_kernel(keep_ref, got_ref, out_ref):
    for t in range(keep_ref.shape[0]):
        out_ref[:, t, :] = keep_ref[t] + got_ref[t].astype(F32)


def local(green, factors, pattern, coulomb):
    times, orb, _ = green.shape
    own = factors.shape[0]
    barrier = lax.optimization_barrier
    masked, whole, coulomb = prologue(factors, pattern, coulomb)

    beyond = two_along_z(whole)
    below = along_z(whole, 1)
    above = along_z(whole, -1)
    left = project(masked, green, NN)
    left = two_along_z(left)

    blocks = [whole, below, above, beyond]
    weights = [block[HALF : HALF + 1] for block in blocks] + [jnp.zeros((4, orb), BF16)]
    here = barrier(jnp.concatenate([block[:HALF] for block in blocks] + weights, axis=0))

    n = 4 * HALF
    west = along_x(here, 1)
    east = along_x(here, -1)
    rest = other_parity(here[HALF:])
    here_q = jnp.concatenate([masked[HALF:], rest], axis=0)
    right = project(masked, green, NT)
    west, east, right, here_q = barrier((west, east, right, here_q))
    right_other = other_core(right)
    onward, both = mix(west, east)
    far = split_x(onward)
    sides_q = other_parity(both)
    far_q = other_parity(far)
    left = two_along_z(left)
    rights = (right, right_other)
    left_other = other_core(left)

    lefts = (left, left_other)
    four = [(k, 0, n) for k in range(4)]
    sides = rights + lefts
    acc = chunk(sides, (here, here_q, west, east), four)
    acc = chunk(sides, (sides_q, far), [(0, 0, n), (0, n + 8, n), (1, 0, n)], acc=acc)
    keep, theirs = chunk(sides, (far_q,), [(0, 0, n)], acc=acc, last=True)

    got = other_core(theirs)
    chips, i_rows = 16, orb // 16
    part = pl.pallas_call(
        finish_kernel,
        out_shape=jax.ShapeDtypeStruct((chips, times, i_rows, own), BF16),
        in_specs=[VMEM] * 3,
        out_specs=VMEM,
        compiler_params=params(12),
    )(keep, got, coulomb)
    groups = [[2 * chip + core for chip in range(chips)] for core in range(2)]
    part = lax.all_to_all(part, "aux", 0, 0, axis_index_groups=groups, tiled=True)

    shape = jax.ShapeDtypeStruct((times, i_rows // 2, orb), F32)
    keep, theirs = pl.pallas_call(
        sigma_kernel,
        out_shape=(shape, jax.ShapeDtypeStruct(shape.shape, BF16)),
        in_specs=[VMEM] * 8,
        out_specs=(VMEM, VMEM),
        scratch_shapes=[
            pltpu.VMEM((times * i_rows, chips * own), BF16),
            pltpu.VMEM((times * i_rows, orb), F32),
        ],
        compiler_params=params(12),
    )(part, here, here_q, west, east, sides_q, far, far_q)
    got = other_core(theirs)
    return pl.pallas_call(
        add_kernel,
        out_shape=jax.ShapeDtypeStruct((i_rows // 2, times, orb), F32),
        in_specs=[VMEM] * 2,
        out_specs=VMEM,
        compiler_params=params(8),
    )(keep, got)


def solution(mesh):
    in_specs = (P("tm", None, None), P("aux", None), P("aux", None), P("aux"))
    out_specs = P("aux", "tm", None)
    return jax.shard_map(local, mesh=mesh, in_specs=in_specs, out_specs=out_specs, check_vma=False)
```

```python
import functools

import jax
import jax.numpy as jnp
from jax import lax
from jax.experimental import pallas as pl
from jax.experimental.pallas import tpu as pltpu
from jax.sharding import PartitionSpec as P

BLOCK = 128
HALF = 64
F32, BF16 = jnp.float32, jnp.bfloat16
BOTH = ("tm", "aux")
NT = (((1,), (1,)), ((), ()))
NN = (((1,), (0,)), ((), ()))
VMEM = pl.BlockSpec(memory_space=pltpu.VMEM)


def device_at(x, y, z, core):
    return (z // 4 * 4 + y) * 32 + (z % 4 * 4 + x) * 2 + core


def send(value, to):
    pairs = []
    for x in range(4):
        for y in range(4):
            for z in range(8):
                for core in range(2):
                    tx, ty, tz, tcore = to(x, y, z, core)
                    pairs.append((device_at(x, y, z, core), device_at(tx % 4, ty % 4, tz % 8, tcore)))
    return lax.ppermute(value, BOTH, sorted(pairs))


def along_x(value, step):
    return send(value, lambda x, y, z, core: (x + step, y, z, core))


def along_z(value, step):
    return send(value, lambda x, y, z, core: (x, y, z + step, core))


def other_core(value):
    return send(value, lambda x, y, z, core: (x, y, z, 1 - core))


def two_along_z(value):
    return send(value, lambda x, y, z, core: (x, y, z + (2 if core == 0 else -2), core))


def split_x(value):
    return send(value, lambda x, y, z, core: (x + (1 if core == 0 else -1), y, z, core))


def other_parity(value):
    return send(value, lambda x, y, z, core: (x, y + (1 if y % 2 == core else -1), z, core))


def params(mib):
    return pltpu.CompilerParams(vmem_limit_bytes=mib << 20)


def prologue_kernel(factors_in, pattern_in, coulomb_in, masked_ref, whole_ref, own_ref, factors, pattern, coulomb, sems):
    copies = [
        pltpu.make_async_copy(factors_in, factors, sems.at[0]),
        pltpu.make_async_copy(pattern_in, pattern, sems.at[1]),
        pltpu.make_async_copy(coulomb_in, coulomb, sems.at[2]),
    ]
    for copy in copies:
        copy.start()
    for copy in copies:
        copy.wait()
    parity = lax.axis_index("tm") & 1
    orb = factors.shape[1]
    for block in range(orb // BLOCK):
        lanes = pl.ds(block * BLOCK, BLOCK)
        keep = pattern[:, block : block + 1].astype(F32)
        for half in range(2):
            at = parity if half == 0 else 1 - parity
            part = factors[pl.ds(pl.multiple_of(at * HALF, HALF), HALF), lanes]
            part = (part.astype(F32) * keep).astype(BF16)
            masked_ref[pl.ds(half * HALF, HALF), lanes] = part
            if half == 0:
                whole_ref[pl.ds(0, HALF), lanes] = part
    c = coulomb[...]
    turned = pltpu.roll(c, HALF, 1)
    own = jnp.where(parity == 0, c, turned)
    own_ref[...] = own
    lane = lax.broadcasted_iota(jnp.int32, own.shape, 1)
    twice = jnp.where(lane < HALF, own, pltpu.roll(own, HALF, 1))
    high = twice.astype(BF16)
    rest = twice - high.astype(F32)
    middle = rest.astype(BF16)
    low = (rest - middle.astype(F32)).astype(BF16)
    zero = jnp.zeros((1, orb - 3 * BLOCK), BF16)
    row = jnp.concatenate([high, middle, low, zero], axis=1)
    rows = jnp.broadcast_to(row.astype(F32), (8, orb)).astype(BF16)
    whole_ref[pl.ds(HALF, 8), :] = rows


def prologue(factors, pattern, coulomb):
    own, orb = factors.shape
    return pl.pallas_call(
        prologue_kernel,
        out_shape=[
            jax.ShapeDtypeStruct((own, orb), BF16),
            jax.ShapeDtypeStruct((HALF + 8, orb), BF16),
            jax.ShapeDtypeStruct((1, own), F32),
        ],
        in_specs=[pl.BlockSpec(memory_space=pltpu.HBM)] * 3,
        out_specs=[VMEM] * 3,
        scratch_shapes=[
            pltpu.VMEM((own, orb), BF16),
            pltpu.VMEM(pattern.shape, jnp.int32),
            pltpu.VMEM((1, own), F32),
            pltpu.SemaphoreType.DMA((3,)),
        ],
        compiler_params=params(16),
    )(*[pltpu.with_memory_space_constraint(v, pltpu.HBM) for v in (factors, pattern, coulomb[None, :])])


def project_kernel(dims, masked_ref, green_ref, out_ref):
    for t in range(green_ref.shape[0]):
        out_ref[t] = lax.dot_general(
            masked_ref[...], green_ref[t], dims, preferred_element_type=F32
        ).astype(BF16)


def project(masked, green, dims):
    own, orb = masked.shape
    return pl.pallas_call(
        functools.partial(project_kernel, dims),
        out_shape=jax.ShapeDtypeStruct((green.shape[0], own, orb), BF16),
        in_specs=[VMEM] * 2,
        out_specs=VMEM,
        compiler_params=params(12),
        cost_estimate=pl.CostEstimate(
            flops=2 * green.shape[0] * own * orb * orb, bytes_accessed=4 << 20, transcendentals=0
        ),
    )(masked, green)


def pick_kernel(west_ref, east_ref, out_ref):
    core = lax.axis_index("aux") & 1
    out_ref[...] = jnp.where(core == 0, west_ref[...], east_ref[...])


def pair_kernel(west_ref, east_ref, first_ref, out_ref):
    del first_ref
    n = west_ref.shape[0]
    out_ref[pl.ds(0, n), :] = west_ref[...]
    out_ref[pl.ds(n, n), :] = east_ref[...]


def small(kernel, rows, *values):
    return pl.pallas_call(
        kernel,
        out_shape=jax.ShapeDtypeStruct((rows, values[0].shape[1]), BF16),
        in_specs=[VMEM] * len(values),
        out_specs=VMEM,
        compiler_params=params(8),
    )(*values)


def weight_of(ref, row):
    parts = [ref[pl.ds(row, 1), pl.ds(k * BLOCK, BLOCK)].astype(F32) for k in range(3)]
    return parts[0] + (parts[1] + parts[2])


def weights_of(ref, row, blocks):
    lane = lax.broadcasted_iota(jnp.int32, (1, BLOCK), 1)
    pairs = []
    for k in range(0, blocks, 2):
        pairs.append(jnp.where(lane < HALF, weight_of(ref, row + k), weight_of(ref, row + k + 1)))
    return jnp.concatenate(pairs, axis=1) if len(pairs) > 1 else pairs[0]


def rows_of(refs, piece):
    at, start, size = piece
    return refs[at][pl.ds(start, size), :], weights_of(refs[at], start + size, size // HALF)


def chunk_kernel(pieces, sides, count, first, *refs):
    left_own, left_other = refs[sides - 2 : sides]
    rows = refs[sides : sides + count]
    rest = refs[sides + count :]
    if not first:
        acc_own, acc_other = rest[:2]
        rest = rest[2:]
    out_own, out_other = rest
    own = out_own.shape[1]
    for t in range(out_own.shape[0]):
        left = jnp.concatenate([left_own[t], left_other[t]], axis=0)
        right = jnp.concatenate([refs[0][t], refs[1][t]], axis=0)
        pairs = [rows_of(rows, piece) for piece in pieces]
        part = jnp.concatenate([pair[0] for pair in pairs], axis=0)
        weight = jnp.concatenate([pair[1] for pair in pairs], axis=1)
        a = lax.dot_general(right, part, NT, preferred_element_type=F32)
        m = lax.dot_general(left, part, NT, preferred_element_type=F32)
        k = (a * a * weight * m).astype(BF16)
        total = lax.dot_general(k, part, NN, preferred_element_type=F32)
        mine, theirs = total[:own], total[own:]
        if not first:
            mine, theirs = acc_own[t] + mine, acc_other[t] + theirs
        out_own[t] = mine
        out_other[t] = theirs.astype(out_other.dtype)


def chunk(sides, rows, pieces, acc=(), last=False):
    times, own, orb = sides[0].shape
    shape = jax.ShapeDtypeStruct((times, own, orb), F32)
    theirs = jax.ShapeDtypeStruct((times, own, orb), BF16 if last else F32)
    at = len(sides) + len(rows)
    aliases = {}
    if acc:
        aliases[at] = 0
        if not last:
            aliases[at + 1] = 1
    n = sum(piece[2] for piece in pieces)
    flops = times * 2 * 2 * (2 * own) * n * orb // 2
    return pl.pallas_call(
        functools.partial(
            chunk_kernel, tuple(pieces), len(sides), len(rows), not acc
        ),
        out_shape=(shape, theirs),
        in_specs=[VMEM] * (at + len(acc)),
        out_specs=(VMEM, VMEM),
        input_output_aliases=aliases,
        compiler_params=params(16),
        cost_estimate=pl.CostEstimate(flops=flops, bytes_accessed=2 << 20, transcendentals=0),
    )(*sides, *rows, *acc)


def finish_kernel(own_ref, got_ref, coulomb_ref, out_ref):
    chips, times, rows, _ = out_ref.shape
    for t in range(times):
        d = jnp.transpose(own_ref[t] + got_ref[t].astype(F32)) * coulomb_ref[...]
        d = d.astype(BF16)
        for chip in range(chips):
            out_ref[chip, t] = d[chip * rows : (chip + 1) * rows]


def sigma_kernel(part_ref, *refs):
    here, here_q, west, east, sides_q, far, far_q = refs[:7]
    keep_ref, send_ref, lhs, total_ref = refs[7:]
    skip = west.shape[0]
    columns = [((here, 0), (here_q, 0)), ((west, 0), (sides_q, 0)), ((east, 0), (sides_q, skip)), ((far, 0), (far_q, 0))]
    chips, times, i_rows, width = part_ref.shape
    me = lax.axis_index("aux")
    core, x, z = me & 1, (me >> 1) & 3, me >> 3
    total = None
    for column, dx in enumerate((0, 3, 1, 2)):
        parts = []
        for k, dz in enumerate((0, 3, 1, 2)):
            source = ((z + dz) & 3) * 4 + ((x + dx) & 3)
            for t in range(times):
                at = pl.ds((column * 4 + k) * width, width)
                lhs[pl.ds(t * i_rows, i_rows), at] = part_ref[source, t]
            for ref, start in columns[column]:
                parts.append(ref[pl.ds(start + k * HALF, HALF), :])
        d = lax.dot_general(
            lhs[:, pl.ds(column * 4 * width, 4 * width)],
            jnp.concatenate(parts, axis=0),
            NN,
            preferred_element_type=F32,
        )
        total = d if total is None else total + d
    total_ref[...] = total
    half = i_rows // 2
    for t in range(times):
        keep = pl.multiple_of(t * i_rows + core * half, half)
        send = pl.multiple_of(t * i_rows + (1 - core) * half, half)
        keep_ref[t] = total_ref[pl.ds(keep, half), :]
        send_ref[t] = total_ref[pl.ds(send, half), :].astype(BF16)


def add_kernel(keep_ref, got_ref, out_ref):
    for t in range(keep_ref.shape[0]):
        out_ref[:, t, :] = keep_ref[t] + got_ref[t].astype(F32)


def local(green, factors, pattern, coulomb):
    times, orb, _ = green.shape
    own = factors.shape[0]
    barrier = lax.optimization_barrier
    masked, whole, coulomb = prologue(factors, pattern, coulomb)

    beyond = two_along_z(whole)
    below = along_z(whole, 1)
    above = along_z(whole, -1)
    left = project(masked, green, NN)
    left = two_along_z(left)

    blocks = [whole, below, above, beyond]
    weights = [block[HALF : HALF + 1] for block in blocks] + [jnp.zeros((4, orb), BF16)]
    here = barrier(jnp.concatenate([block[:HALF] for block in blocks] + weights, axis=0))

    n = 4 * HALF
    west = along_x(here, 1)
    east = along_x(here, -1)
    rest = other_parity(here[HALF:])
    here_q = jnp.concatenate([masked[HALF:], rest], axis=0)
    right = project(masked, green, NT)
    right_other = other_core(right)
    west, east, right, here_q = barrier((west, east, right, here_q))
    onward = small(pick_kernel, n + 8, west, east)
    both = small(pair_kernel, 2 * (n + 8), west, east, right_other)
    far = split_x(onward)
    sides_q = other_parity(both)
    far_q = other_parity(far)
    left = two_along_z(left)
    rights = (right, right_other)
    left_other = other_core(left)

    lefts = (left, left_other)
    four = [(k, 0, n) for k in range(4)]
    sides = rights + lefts
    acc = chunk(sides, (here, here_q, west, east), four)
    acc = chunk(sides, (sides_q, far), [(0, 0, n), (0, n + 8, n), (1, 0, n)], acc=acc)
    keep, theirs = chunk(sides, (far_q,), [(0, 0, n)], acc=acc, last=True)

    got = other_core(theirs)
    chips, i_rows = 16, orb // 16
    part = pl.pallas_call(
        finish_kernel,
        out_shape=jax.ShapeDtypeStruct((chips, times, i_rows, own), BF16),
        in_specs=[VMEM] * 3,
        out_specs=VMEM,
        compiler_params=params(12),
    )(keep, got, coulomb)
    groups = [[2 * chip + core for chip in range(chips)] for core in range(2)]
    part = lax.all_to_all(part, "aux", 0, 0, axis_index_groups=groups, tiled=True)

    shape = jax.ShapeDtypeStruct((times, i_rows // 2, orb), F32)
    keep, theirs = pl.pallas_call(
        sigma_kernel,
        out_shape=(shape, jax.ShapeDtypeStruct(shape.shape, BF16)),
        in_specs=[VMEM] * 8,
        out_specs=(VMEM, VMEM),
        scratch_shapes=[
            pltpu.VMEM((times * i_rows, chips * own), BF16),
            pltpu.VMEM((times * i_rows, orb), F32),
        ],
        compiler_params=params(12),
    )(part, here, here_q, west, east, sides_q, far, far_q)
    got = other_core(theirs)
    return pl.pallas_call(
        add_kernel,
        out_shape=jax.ShapeDtypeStruct((i_rows // 2, times, orb), F32),
        in_specs=[VMEM] * 2,
        out_specs=VMEM,
        compiler_params=params(8),
    )(keep, got)


def solution(mesh):
    in_specs = (P("tm", None, None), P("aux", None), P("aux", None), P("aux"))
    out_specs = P("aux", "tm", None)
    return jax.shard_map(local, mesh=mesh, in_specs=in_specs, out_specs=out_specs, check_vma=False)
```

```python
import functools

import jax
import jax.numpy as jnp
from jax import lax
from jax.experimental import pallas as pl
from jax.experimental.pallas import tpu as pltpu
from jax.sharding import PartitionSpec as P

BLOCK = 128
HALF = 64
F32, BF16 = jnp.float32, jnp.bfloat16
BOTH = ("tm", "aux")
NT = (((1,), (1,)), ((), ()))
NN = (((1,), (0,)), ((), ()))
VMEM = pl.BlockSpec(memory_space=pltpu.VMEM)


def device_at(x, y, z, core):
    return (z // 4 * 4 + y) * 32 + (z % 4 * 4 + x) * 2 + core


def send(value, to):
    pairs = []
    for x in range(4):
        for y in range(4):
            for z in range(8):
                for core in range(2):
                    tx, ty, tz, tcore = to(x, y, z, core)
                    pairs.append((device_at(x, y, z, core), device_at(tx % 4, ty % 4, tz % 8, tcore)))
    return lax.ppermute(value, BOTH, sorted(pairs))


def along_x(value, step):
    return send(value, lambda x, y, z, core: (x + step, y, z, core))


def along_z(value, step):
    return send(value, lambda x, y, z, core: (x, y, z + step, core))


def other_core(value):
    return send(value, lambda x, y, z, core: (x, y, z, 1 - core))


def two_along_z(value):
    return send(value, lambda x, y, z, core: (x, y, z + (2 if core == 0 else -2), core))


def split_x(value):
    return send(value, lambda x, y, z, core: (x + (1 if core == 0 else -1), y, z, core))


def other_parity(value):
    return send(value, lambda x, y, z, core: (x, y + (1 if y % 2 == core else -1), z, core))


def params(mib):
    return pltpu.CompilerParams(vmem_limit_bytes=mib << 20)


def prologue_kernel(factors_in, pattern_in, coulomb_in, masked_ref, whole_ref, own_ref, factors, pattern, coulomb, sems):
    copies = [
        pltpu.make_async_copy(factors_in, factors, sems.at[0]),
        pltpu.make_async_copy(pattern_in, pattern, sems.at[1]),
        pltpu.make_async_copy(coulomb_in, coulomb, sems.at[2]),
    ]
    for copy in copies:
        copy.start()
    for copy in copies:
        copy.wait()
    parity = lax.axis_index("tm") & 1
    orb = factors.shape[1]
    for block in range(orb // BLOCK):
        lanes = pl.ds(block * BLOCK, BLOCK)
        keep = pattern[:, block : block + 1].astype(F32)
        for half in range(2):
            at = parity if half == 0 else 1 - parity
            part = factors[pl.ds(pl.multiple_of(at * HALF, HALF), HALF), lanes]
            part = (part.astype(F32) * keep).astype(BF16)
            masked_ref[pl.ds(half * HALF, HALF), lanes] = part
            if half == 0:
                whole_ref[pl.ds(0, HALF), lanes] = part
    c = coulomb[...]
    turned = pltpu.roll(c, HALF, 1)
    own = jnp.where(parity == 0, c, turned)
    own_ref[...] = own
    lane = lax.broadcasted_iota(jnp.int32, own.shape, 1)
    twice = jnp.where(lane < HALF, own, pltpu.roll(own, HALF, 1))
    high = twice.astype(BF16)
    rest = twice - high.astype(F32)
    middle = rest.astype(BF16)
    low = (rest - middle.astype(F32)).astype(BF16)
    zero = jnp.zeros((1, orb - 3 * BLOCK), BF16)
    row = jnp.concatenate([high, middle, low, zero], axis=1)
    rows = jnp.broadcast_to(row.astype(F32), (8, orb)).astype(BF16)
    whole_ref[pl.ds(HALF, 8), :] = rows


def prologue(factors, pattern, coulomb):
    own, orb = factors.shape
    return pl.pallas_call(
        prologue_kernel,
        out_shape=[
            jax.ShapeDtypeStruct((own, orb), BF16),
            jax.ShapeDtypeStruct((HALF + 8, orb), BF16),
            jax.ShapeDtypeStruct((1, own), F32),
        ],
        in_specs=[pl.BlockSpec(memory_space=pltpu.HBM)] * 3,
        out_specs=[VMEM] * 3,
        scratch_shapes=[
            pltpu.VMEM((own, orb), BF16),
            pltpu.VMEM(pattern.shape, jnp.int32),
            pltpu.VMEM((1, own), F32),
            pltpu.SemaphoreType.DMA((3,)),
        ],
        compiler_params=params(16),
    )(*[pltpu.with_memory_space_constraint(v, pltpu.HBM) for v in (factors, pattern, coulomb[None, :])])


def mix_kernel(west_ref, east_ref, onward_ref, both_ref):
    core = lax.axis_index("aux") & 1
    n = west_ref.shape[0]
    west, east = west_ref[...], east_ref[...]
    onward_ref[...] = jnp.where(core == 0, west, east)
    both_ref[pl.ds(0, n), :] = west
    both_ref[pl.ds(n, n), :] = east


def mix(west, east):
    n, orb = west.shape
    return pl.pallas_call(
        mix_kernel,
        out_shape=(jax.ShapeDtypeStruct((n, orb), BF16), jax.ShapeDtypeStruct((2 * n, orb), BF16)),
        in_specs=[VMEM] * 2,
        out_specs=[VMEM] * 2,
        compiler_params=params(8),
    )(west, east)


def weight_of(ref, row):
    parts = [ref[pl.ds(row, 1), pl.ds(k * BLOCK, BLOCK)].astype(F32) for k in range(3)]
    return parts[0] + (parts[1] + parts[2])


def weights_of(ref, row, blocks):
    lane = lax.broadcasted_iota(jnp.int32, (1, BLOCK), 1)
    pairs = []
    for k in range(0, blocks, 2):
        pairs.append(jnp.where(lane < HALF, weight_of(ref, row + k), weight_of(ref, row + k + 1)))
    return jnp.concatenate(pairs, axis=1) if len(pairs) > 1 else pairs[0]


def rows_of(refs, piece):
    at, start, size = piece
    return refs[at][pl.ds(start, size), :], weights_of(refs[at], start + size, size // HALF)


def chunk_kernel(pieces, sides, count, first, *refs):
    left_own, left_other = refs[sides - 2 : sides]
    rows = refs[sides : sides + count]
    rest = refs[sides + count :]
    if not first:
        acc_own, acc_other = rest[:2]
        rest = rest[2:]
    out_own, out_other = rest
    own = out_own.shape[1]
    for t in range(out_own.shape[0]):
        left = jnp.concatenate([left_own[t], left_other[t]], axis=0)
        right = jnp.concatenate([refs[0][t], refs[1][t]], axis=0)
        pairs = [rows_of(rows, piece) for piece in pieces]
        part = jnp.concatenate([pair[0] for pair in pairs], axis=0)
        weight = jnp.concatenate([pair[1] for pair in pairs], axis=1)
        a = lax.dot_general(right, part, NT, preferred_element_type=F32)
        m = lax.dot_general(left, part, NT, preferred_element_type=F32)
        k = (a * a * weight * m).astype(BF16)
        total = lax.dot_general(k, part, NN, preferred_element_type=F32)
        mine, theirs = total[:own], total[own:]
        if not first:
            mine, theirs = acc_own[t] + mine, acc_other[t] + theirs
        out_own[t] = mine
        out_other[t] = theirs.astype(out_other.dtype)


def chunk(sides, rows, pieces, acc=(), last=False):
    times, own, orb = sides[0].shape
    shape = jax.ShapeDtypeStruct((times, own, orb), F32)
    theirs = jax.ShapeDtypeStruct((times, own, orb), BF16 if last else F32)
    at = len(sides) + len(rows)
    aliases = {}
    if acc:
        aliases[at] = 0
        if not last:
            aliases[at + 1] = 1
    n = sum(piece[2] for piece in pieces)
    flops = times * 2 * 2 * (2 * own) * n * orb // 2
    return pl.pallas_call(
        functools.partial(
            chunk_kernel, tuple(pieces), len(sides), len(rows), not acc
        ),
        out_shape=(shape, theirs),
        in_specs=[VMEM] * (at + len(acc)),
        out_specs=(VMEM, VMEM),
        input_output_aliases=aliases,
        compiler_params=params(16),
        cost_estimate=pl.CostEstimate(flops=flops, bytes_accessed=2 << 20, transcendentals=0),
    )(*sides, *rows, *acc)


def finish_kernel(own_ref, got_ref, coulomb_ref, out_ref):
    chips, times, rows, _ = out_ref.shape
    for t in range(times):
        d = jnp.transpose(own_ref[t] + got_ref[t].astype(F32)) * coulomb_ref[...]
        d = d.astype(BF16)
        for chip in range(chips):
            out_ref[chip, t] = d[chip * rows : (chip + 1) * rows]


def sigma_kernel(part_ref, *refs):
    here, here_q, west, east, sides_q, far, far_q = refs[:7]
    keep_ref, send_ref, lhs, total_ref = refs[7:]
    skip = west.shape[0]
    columns = [((here, 0), (here_q, 0)), ((west, 0), (sides_q, 0)), ((east, 0), (sides_q, skip)), ((far, 0), (far_q, 0))]
    chips, times, i_rows, width = part_ref.shape
    me = lax.axis_index("aux")
    core, x, z = me & 1, (me >> 1) & 3, me >> 3
    total = None
    for column, dx in enumerate((0, 3, 1, 2)):
        parts = []
        for k, dz in enumerate((0, 3, 1, 2)):
            source = ((z + dz) & 3) * 4 + ((x + dx) & 3)
            for t in range(times):
                at = pl.ds((column * 4 + k) * width, width)
                lhs[pl.ds(t * i_rows, i_rows), at] = part_ref[source, t]
            for ref, start in columns[column]:
                parts.append(ref[pl.ds(start + k * HALF, HALF), :])
        d = lax.dot_general(
            lhs[:, pl.ds(column * 4 * width, 4 * width)],
            jnp.concatenate(parts, axis=0),
            NN,
            preferred_element_type=F32,
        )
        total = d if total is None else total + d
    total_ref[...] = total
    half = i_rows // 2
    for t in range(times):
        keep = pl.multiple_of(t * i_rows + core * half, half)
        send = pl.multiple_of(t * i_rows + (1 - core) * half, half)
        keep_ref[t] = total_ref[pl.ds(keep, half), :]
        send_ref[t] = total_ref[pl.ds(send, half), :].astype(BF16)


def add_kernel(keep_ref, got_ref, out_ref):
    for t in range(keep_ref.shape[0]):
        out_ref[:, t, :] = keep_ref[t] + got_ref[t].astype(F32)


def local(green, factors, pattern, coulomb):
    times, orb, _ = green.shape
    own = factors.shape[0]
    barrier = lax.optimization_barrier
    masked, whole, coulomb = prologue(factors, pattern, coulomb)

    beyond = two_along_z(whole)
    below = along_z(whole, 1)
    above = along_z(whole, -1)
    left = jnp.einsum("qo,tok->tqk", masked, green, preferred_element_type=F32).astype(BF16)
    left = two_along_z(left)

    blocks = [whole, below, above, beyond]
    weights = [block[HALF : HALF + 1] for block in blocks] + [jnp.zeros((4, orb), BF16)]
    here = barrier(jnp.concatenate([block[:HALF] for block in blocks] + weights, axis=0))

    n = 4 * HALF
    west = along_x(here, 1)
    east = along_x(here, -1)
    rest = other_parity(here[HALF:])
    here_q = jnp.concatenate([masked[HALF:], rest], axis=0)
    right = jnp.einsum("qo,tko->tqk", masked, green, preferred_element_type=F32).astype(BF16)
    west, east, right, here_q = barrier((west, east, right, here_q))
    right_other = other_core(right)
    onward, both = mix(west, east)
    far = split_x(onward)
    sides_q = other_parity(both)
    far_q = other_parity(far)
    left = two_along_z(left)
    rights = (right, right_other)
    left_other = other_core(left)

    lefts = (left, left_other)
    four = [(k, 0, n) for k in range(4)]
    sides = rights + lefts
    acc = chunk(sides, (here, here_q, west, east), four)
    acc = chunk(sides, (sides_q, far), [(0, 0, n), (0, n + 8, n), (1, 0, n)], acc=acc)
    keep, theirs = chunk(sides, (far_q,), [(0, 0, n)], acc=acc, last=True)

    got = other_core(theirs)
    chips, i_rows = 16, orb // 16
    part = pl.pallas_call(
        finish_kernel,
        out_shape=jax.ShapeDtypeStruct((chips, times, i_rows, own), BF16),
        in_specs=[VMEM] * 3,
        out_specs=VMEM,
        compiler_params=params(12),
    )(keep, got, coulomb)
    groups = [[2 * chip + core for chip in range(chips)] for core in range(2)]
    part = lax.all_to_all(part, "aux", 0, 0, axis_index_groups=groups, tiled=True)

    shape = jax.ShapeDtypeStruct((times, i_rows // 2, orb), F32)
    keep, theirs = pl.pallas_call(
        sigma_kernel,
        out_shape=(shape, jax.ShapeDtypeStruct(shape.shape, BF16)),
        in_specs=[VMEM] * 8,
        out_specs=(VMEM, VMEM),
        scratch_shapes=[
            pltpu.VMEM((times * i_rows, chips * own), BF16),
            pltpu.VMEM((times * i_rows, orb), F32),
        ],
        compiler_params=params(12),
    )(part, here, here_q, west, east, sides_q, far, far_q)
    got = other_core(theirs)
    return pl.pallas_call(
        add_kernel,
        out_shape=jax.ShapeDtypeStruct((i_rows // 2, times, orb), F32),
        in_specs=[VMEM] * 2,
        out_specs=VMEM,
        compiler_params=params(8),
    )(keep, got)


def solution(mesh):
    in_specs = (P("tm", None, None), P("aux", None), P("aux", None), P("aux"))
    out_specs = P("aux", "tm", None)
    return jax.shard_map(local, mesh=mesh, in_specs=in_specs, out_specs=out_specs, check_vma=False)
```
